32 devices in a mesh: dp: 4 (over x, core), fsdp: 8 (over z, y).
Axes of the slice: x: 2, y: 2, z: 4, core: 2. Of those that a mesh axis runs over, the one named last changes fastest.
Arguments:
- resid_pre: bfloat16 [64, 64, 768], P(('dp', 'fsdp')), may hold values from -6 to 6
- token_ids: int32 [64, 64], P('dp'), may hold values from 0 to 50303
- valid_mask: int32 [64, 64], P('dp'), may hold values from 0 to 1, as said below
- picked: int32 [64, 32], P('dp'), may hold values from 1 to 62, as said below
- norm_gains: float32 [3, 768], replicated, may hold values from 0.5 to 1.5
- norm_biases: float32 [3, 768], replicated, may hold values from -1.75 to 1.75
- qkv_w: bfloat16 [768, 2304], replicated, may hold values from -0.21875 to 0.21875
- out_w: bfloat16 [768, 768], replicated, may hold values from -0.875 to 0.875
- fc_w: bfloat16 [768, 3072], replicated, may hold values from -0.21875 to 0.21875
- proj_w: bfloat16 [3072, 768], replicated, may hold values from -0.109375 to 0.109375
- layer_bias: float32 [6912], replicated, may hold values from -1.75 to 1.75
- wte: bfloat16 [50304, 768], P('fsdp'), may hold values from -0.3125 to 0.3125
- w_enc: float32 [24576, 768], P('fsdp'), may hold values from -0.21875 to 0.21875
- enc_first: float32 [24576, 768], P('fsdp'), may hold values from -5.9604645e-07 to 5.9604645e-07
- enc_second: float32 [24576, 768], P('fsdp'), may hold values from 1.0839308e-15 to 4.3357232e-15
- b_enc: float32 [24576], P('fsdp'), may hold values from -1.75 to 1.75
- w_dec: float32 [24576, 768], P('fsdp'), may hold values from -0.0390625 to 0.0390625
- dec_first: float32 [24576, 768], P('fsdp'), may hold values from -2.861023e-06 to 2.861023e-06
- dec_second: float32 [24576, 768], P('fsdp'), may hold values from 2.3412905e-14 to 9.365162e-14
- b_dec: float32 [768], replicated, may hold values from -1.75 to 1.75
Outputs:
- weights: float32 [2, 24576, 768], P(None, 'fsdp')
- first_moments: float32 [2, 24576, 768], P(None, 'fsdp')
- second_moments: float32 [2, 24576, 768], P(None, 'fsdp')
- loss: float32 [], replicated
- clip_norm: float32 [], replicated
- weight_norms: float32 [2], replicated
- step_norms: float32 [2], replicated
The draws below stay inside these ranges and needn't reach their ends.
Inputs may be any that keep to these rules, and one draw needn't show every extreme that they name: `valid_mask`: 0 at each sequence's first position, 1 at its second. `picked`: each row holds 32 distinct positions in increasing order, among them 1 and 62.
All inputs are finite; a program needn't handle non-finite values.
Results may differ from the reference program's by a relative error of at most 0.0029.
Values may be sent and summed in bfloat16 or wider, within the bound.
No kernel may reach another device: no remote copies, remote signals or barrier semaphores. Data moves between devices by JAX's collectives and lax.ppermute only.
A program may use at most 448 MiB of HBM per device.

```python
import math
import jax
import jax.numpy as jnp
import numpy as np
from jax import lax

D = 768
HEADS = 12
HEAD_DIM = 64
FF = 3072
VOCAB = 50304
F = 24576
SEQ_LEN = 64
STEP = 10
PICK = 32
SEQS = 64
TOKENS = 4096


def draw_valid_mask(key, part):
    dice_rolls = jax.random.randint(key, (SEQS, SEQ_LEN), 0, 100)
    seq_index = jax.lax.broadcasted_iota(jnp.int32, (SEQS, SEQ_LEN), 0)
    threshold = 20 + 75 * seq_index // (SEQS - 1)
    valid_marks = (dice_rolls < threshold).astype(jnp.int32)
    position = jax.lax.broadcasted_iota(jnp.int32, (SEQS, SEQ_LEN), 1)
    valid_marks = jnp.where(position == 0, 0, valid_marks)
    return jnp.where(position == 1, 1, valid_marks).astype(jnp.int32)


def draw_picked(key, part):
    subkeys = jax.random.split(key, SEQS)
    orders = jax.vmap(lambda subkey: jax.random.permutation(subkey, SEQ_LEN - 4))(subkeys)
    chosen = (orders[:, :PICK - 2] + 2).astype(jnp.int32)
    bounds = jnp.broadcast_to(jnp.array([1, SEQ_LEN - 2], jnp.int32), (SEQS, 2))
    return jnp.sort(jnp.concatenate([bounds, chosen], 1), axis=1).astype(jnp.int32)


def touch_ends(drawn, stream_key, smallest, largest):
    longest = drawn.shape.index(max(drawn.shape))
    spots = []
    for shift in (0, 1):
        where = [jax.random.randint(jax.random.fold_in(stream_key, axis), (), 0, length) for axis, length in enumerate(drawn.shape)]
        where[longest] = (where[longest] + shift) % drawn.shape[longest]
        spots.append(tuple(where))
    return drawn.at[spots[0]].set(smallest).at[spots[1]].set(largest)


def level_of(own_key, shape, cuts, smallest, top_value):
    def one(dim, parts):
        draws = jax.random.uniform(jax.random.fold_in(jax.random.fold_in(own_key, 6), dim), (parts,), jnp.float32, smallest / len(cuts), top_value / len(cuts))
        return jnp.repeat(jnp.exp(draws), shape[dim] // parts).reshape((-1,) + (1,) * (len(shape) - dim - 1))

    factor_of = one(*cuts[0])
    for cut in cuts[1:]:
        factor_of = factor_of * one(*cut)
    return factor_of


def cumulative_ranks(amount, lean):
    weights = [(1 << 20) // math.isqrt(standing ** lean) + 1 for standing in range(1, amount + 1)]
    width = 1 + sum(weights) // (1 << 30)
    return np.cumsum(np.array([max(1, weight // width) for weight in weights]))


def ranked_ids(own_key, shape, amount, skew):
    listing = cumulative_ranks(amount, skew)
    lot = jax.random.randint(jax.random.fold_in(own_key, 1), shape, 0, int(listing[amount - 1]))
    grade = jnp.searchsorted(jnp.asarray(listing, jnp.int32), lot, side="right")
    return jax.random.permutation(jax.random.fold_in(own_key, 2), amount)[grade].astype(jnp.int32)


def noise(key, shape, scale, bound, shards=(), kind=jnp.bfloat16):
    drawn = jax.random.normal(key, shape, jnp.float32) * scale
    if len(shards) > 0:
        drawn = level_of(key, shape, shards, -0.22, 0.18) * drawn
    return jnp.clip(drawn, min=-bound, max=bound).astype(kind)


def setup_inputs(seed: int = 0) -> dict:
    key_list = jax.random.split(jax.random.key(seed), 21)
    return {
        "resid_pre": noise(key_list[0], (SEQS, SEQ_LEN, D), 1.0, 6.0, ((0, 32),)),
        "token_ids": touch_ends(ranked_ids(key_list[1], (SEQS, SEQ_LEN), VOCAB, 2), jax.random.fold_in(key_list[1], 3), 0, VOCAB - 1).astype(jnp.int32),
        "valid_mask": draw_valid_mask(jax.random.fold_in(key_list[20], 71), 0),
        "picked": draw_picked(jax.random.fold_in(key_list[20], 71), 0),
        "norm_gains": jnp.clip(1.0 + 0.1 * jax.random.normal(key_list[4], (3, D), jnp.float32), 0.5, 1.5),
        "norm_biases": noise(key_list[5], (3, D), 0.3, 1.75, (), jnp.float32),
        "qkv_w": noise(key_list[6], (D, 3 * D), D ** -0.5, 0.21875),
        "out_w": noise(key_list[7], (D, D), (D * 4 // SEQ_LEN) ** -0.5, 0.875),
        "fc_w": noise(key_list[8], (D, FF), D ** -0.5, 0.21875),
        "proj_w": noise(key_list[9], (FF, D), FF ** -0.5, 0.109375),
        "layer_bias": noise(key_list[10], (5 * D + FF,), 0.3, 1.75, (), jnp.float32),
        "wte": noise(key_list[11], (VOCAB, D), (D // 2) ** -0.5, 0.3125, ((0, 8),)),
        "w_enc": noise(key_list[12], (F, D), D ** -0.5, 0.21875, ((0, 8),), jnp.float32),
        "enc_first": noise(key_list[13], (F, D), (0.0022 / (TOKENS * F) ** 0.5 / (F / (1.5 * TOKENS) + 800 / F) ** 0.5), 5.960464477539062e-07, ((0, 8),), jnp.float32),
        "enc_second": jnp.clip(jnp.exp(math.log(4.335723217220111e-15) - 1.3862944 * jax.random.uniform(key_list[14], (F, D), jnp.float32) ** level_of(key_list[14], (F, D), ((0, 8),), -0.2, 0.2)), 1.0839308043050278e-15, 4.335723217220111e-15),
        "b_enc": noise(key_list[15], (F,), 0.3, 1.75, ((0, 8),), jnp.float32),
        "w_dec": noise(key_list[16], (F, D), F ** -0.5, 0.0390625, ((0, 8),), jnp.float32),
        "dec_first": noise(key_list[17], (F, D), (0.0018 / (TOKENS * D) ** 0.5 / (F / (1.5 * TOKENS) + 800 / F) ** 0.5), 2.86102294921875e-06, ((0, 8),), jnp.float32),
        "dec_second": jnp.clip(jnp.exp(math.log(9.365162183076758e-14) - 1.3862944 * jax.random.uniform(key_list[18], (F, D), jnp.float32) ** level_of(key_list[18], (F, D), ((0, 8),), -0.2, 0.2)), 2.3412905457691896e-14, 9.365162183076758e-14),
        "b_dec": noise(key_list[19], (D,), 0.3, 1.75, (), jnp.float32),
    }


@jax.custom_vjp
def low(v):
    return lax.optimization_barrier(v.astype(jnp.bfloat16)).astype(jnp.float32)

@jax.custom_vjp
def low_back(v):
    return v

def low_keep(v):
    return (low(v), None)

def low_pass(kept, grad):
    return (grad,)

def back_keep(v):
    return (v, None)

def back_low(kept, grad):
    return (low(grad),)
low.defvjp(low_keep, low_pass)
low_back.defvjp(back_keep, back_low)
highest = lax.Precision.HIGHEST
norm_eps = 1e-05
l1_scale = 40.0
clip_limit = 0.02
learn_rate = 0.3
beta_one = 0.9
beta_two = 0.999
adam_eps = 1e-08
weight_decay = 0.01

def matmul(left, right):
    return jnp.matmul(left, right, precision=highest)

def layer_norm(values, gain, shift):
    center = values - lax.optimization_barrier(jnp.mean(values, -1, keepdims=True))
    spread = lax.optimization_barrier(jnp.mean(center * center, -1, keepdims=True))
    return center * lax.rsqrt(spread + norm_eps) * gain + shift

def attend(inputs, frozen):
    gains, shifts, qkv_w, qkv_b, out_w, out_b = frozen
    count_seq, length = (inputs.shape[0], inputs.shape[1])
    normed = low(layer_norm(inputs, gains[0], shifts[0]))
    packed = low(matmul(normed, qkv_w) + qkv_b).reshape(count_seq, length, 3, HEADS, HEAD_DIM)
    scores = jnp.einsum('sqhd,skhd->shqk', packed[:, :, 0], packed[:, :, 1], precision=highest) * HEAD_DIM ** (-0.5)
    row_ids = lax.broadcasted_iota(jnp.int32, (length, length), 0)
    col_ids = lax.broadcasted_iota(jnp.int32, (length, length), 1)
    scores = jnp.where(row_ids >= col_ids, scores, -1e+30)
    probs = low(jax.nn.softmax(scores, axis=-1))
    context = jnp.einsum('shqk,skhd->sqhd', probs, packed[:, :, 2], precision=highest)
    context = low(context.reshape(count_seq, length, D))
    return matmul(context, out_w) + out_b

def block_loss(params, tables, inputs, attn, targets, masks, picks):
    w_enc, w_dec = params
    gains, shifts, fc_w, fc_b, proj_w, proj_b, table, valid_total, b_enc, b_dec = tables
    centered = low(attn - b_dec)
    pre = low_back(matmul(centered, low(w_enc).T) + b_enc)
    features = jnp.maximum(pre, 0.0)
    recon = low_back(matmul(low(features), low(w_dec)) + b_dec)
    mid = inputs + recon
    normed = low(layer_norm(mid, gains[1], shifts[1]))
    up_val = low_back(matmul(normed, fc_w) + fc_b)
    act = low(jax.nn.gelu(up_val, approximate=True))
    out_val = low_back(matmul(act, proj_w) + proj_b)
    hidden = mid + out_val
    rows_at = jnp.take_along_axis(hidden, picks[:, :, None], axis=1)
    final = low(layer_norm(rows_at, gains[2], shifts[2]))
    logits = low_back(matmul(final, table.T))
    lse = jax.nn.logsumexp(logits, axis=-1)
    target_logit = jnp.take_along_axis(logits, targets[:, :, None], axis=2)[:, :, 0]
    cross = jnp.sum(lse - target_logit) / (SEQS * PICK)
    sparse = l1_scale / F * jnp.sum(masks[:, :, None] * features) / valid_total
    return cross + sparse

def optimize(weight, grad, first, second, factor):
    clipped = grad * factor
    first_new = beta_one * first + (1.0 - beta_one) * clipped
    second_new = beta_two * second + (1.0 - beta_two) * clipped * clipped
    direction = first_new / (1.0 - beta_one ** STEP) / (jnp.sqrt(second_new / (1.0 - beta_two ** STEP)) + adam_eps) + weight_decay * weight
    return (first_new, second_new, direction)

def reference(resid_pre, token_ids, valid_mask, picked, norm_gains, norm_biases, qkv_w, out_w, fc_w, proj_w, layer_bias, wte, w_enc, enc_first, enc_second, b_enc, w_dec, dec_first, dec_second, b_dec):
    block = 8
    blocks = SEQS // block
    inputs = resid_pre.astype(jnp.float32).reshape(blocks, block, SEQ_LEN, D)
    targets = jnp.take_along_axis(token_ids, picked + 1, axis=1).astype(jnp.int32).reshape(blocks, block, PICK)
    picks = picked.reshape(blocks, block, PICK)
    masks = valid_mask.astype(jnp.float32).reshape(blocks, block, SEQ_LEN)
    valid_total = jnp.sum(masks)
    qkv_b = layer_bias[:3 * D]
    out_b = layer_bias[3 * D:4 * D]
    fc_b = layer_bias[4 * D:4 * D + FF]
    proj_b = layer_bias[4 * D + FF:]
    frozen = (norm_gains, norm_biases, qkv_w.astype(jnp.float32), qkv_b, out_w.astype(jnp.float32), out_b)
    attn_all = lax.map(lambda piece: attend(piece, frozen), inputs)
    tables = (norm_gains, norm_biases, fc_w.astype(jnp.float32), fc_b, proj_w.astype(jnp.float32), proj_b, wte.astype(jnp.float32), valid_total, b_enc, b_dec)
    checked = jax.checkpoint(block_loss)

    def total_loss(params):

        def step(carry, pieces):
            return (carry + checked(params, tables, *pieces), None)
        result, _ = lax.scan(step, jnp.zeros((), jnp.float32), (inputs, attn_all, targets, masks, picks))
        return result
    loss, pullback = jax.vjp(total_loss, (w_enc, w_dec))
    grad_enc, grad_dec = pullback(jnp.ones((), jnp.float32))[0]
    squares = jnp.sum(grad_enc * grad_enc) + jnp.sum(grad_dec * grad_dec)
    clip_norm = jnp.sqrt(squares)
    factor = clip_limit / jnp.maximum(clip_norm, clip_limit)
    enc_m, enc_v, enc_dir = optimize(w_enc, grad_enc, enc_first, enc_second, factor)
    dec_m, dec_v, dec_dir = optimize(w_dec, grad_dec, dec_first, dec_second, factor)
    enc_norm = jnp.sqrt(jnp.sum(w_enc * w_enc))
    enc_step = jnp.sqrt(jnp.sum(enc_dir * enc_dir))
    dec_norm = jnp.sqrt(jnp.sum(w_dec * w_dec))
    dec_step = jnp.sqrt(jnp.sum(dec_dir * dec_dir))
    new_enc = w_enc - learn_rate * (enc_norm / enc_step) * enc_dir
    dec_raw = w_dec - learn_rate * (dec_norm / dec_step) * dec_dir
    new_dec = dec_raw * lax.rsqrt(lax.optimization_barrier(jnp.sum(dec_raw * dec_raw, 1, keepdims=True)) + 1e-06)
    return (jnp.stack([new_enc, new_dec]), jnp.stack([enc_m, dec_m]), jnp.stack([enc_v, dec_v]), loss, clip_norm, jnp.stack([enc_norm, dec_norm]), jnp.stack([enc_step, dec_step]))
```

```python
import jax
import jax.numpy as jnp
from jax import lax
from jax.sharding import PartitionSpec as P

HEADS = 12
HEAD_DIM = 64
F = 24576
STEP = 10


norm_eps = 1e-05
l1_scale = 40.0
clip_limit = 0.02
learn_rate = 0.3
beta_one = 0.9
beta_two = 0.999
adam_eps = 1e-08
weight_decay = 0.01


def layer_norm(values, gain, shift):
    center = values - jnp.mean(values, -1, keepdims=True)
    spread = jnp.mean(center * center, -1, keepdims=True)
    return center * lax.rsqrt(spread + norm_eps) * gain + shift


def times(left, right):
    return jnp.dot(left, right, preferred_element_type=jnp.float32)


def times_trans(left, right):
    return lax.dot_general(
        left, right, (((1,), (1,)), ((), ())), preferred_element_type=jnp.float32
    )


def trans_times(left, right):
    return lax.dot_general(
        left, right, (((0,), (0,)), ((), ())), preferred_element_type=jnp.float32
    )


def swap(block, axis, bit):
    size = lax.axis_size(axis)
    return lax.ppermute(block, axis, [(i, i ^ bit) for i in range(size)])


def gather_group(block):
    size = lax.axis_size("fsdp")
    half = size // 2
    far = swap(block, "fsdp", half)
    near = [block] + [swap(block, "fsdp", k) for k in range(1, half)]
    return near + [far] + [swap(far, "fsdp", k) for k in range(1, half)]


def sum_to_owners(blocks):
    total = blocks[0].astype(jnp.float32)
    for k in range(1, len(blocks)):
        total = total + swap(blocks[k], "fsdp", k).astype(jnp.float32)
    return total


def gather_copies(block):
    blocks = [block]
    bit = lax.axis_size("dp") // 2
    while bit:
        blocks = blocks + [swap(held, "dp", bit) for held in blocks]
        bit //= 2
    return blocks


def gather_small(row):
    size = lax.axis_size("fsdp")
    spread = jnp.broadcast_to(row[None], (size, *row.shape))
    return lax.all_to_all(spread, "fsdp", 0, 0, tiled=True)


def sum_small(values):
    row = jnp.zeros((8, 128), jnp.float32)
    columns = lax.broadcasted_iota(jnp.int32, row.shape, 1)
    for i, value in enumerate(values):
        row = jnp.where(columns == i, value, row)
    total = jnp.sum(gather_small(row), 0)
    return [total[0, i] for i in range(len(values))]


def attention(inputs, gain, shift, qkv_w, qkv_b, out_w, out_b):
    count, length, model_width = inputs.shape
    normed = layer_norm(inputs, gain, shift).astype(jnp.bfloat16).reshape(-1, model_width)
    packed = (times(normed, qkv_w) + qkv_b).astype(jnp.bfloat16)
    packed = packed.reshape(count, length, 3, HEADS, HEAD_DIM)
    scores = jnp.einsum(
        "sqhd,skhd->shqk", packed[:, :, 0], packed[:, :, 1], preferred_element_type=jnp.float32
    ) * HEAD_DIM ** (-0.5)
    row_ids = lax.broadcasted_iota(jnp.int32, (length, length), 0)
    col_ids = lax.broadcasted_iota(jnp.int32, (length, length), 1)
    scores = jnp.where(row_ids >= col_ids, scores, -1e30)
    probs = jax.nn.softmax(scores, axis=-1).astype(jnp.bfloat16)
    context = jnp.einsum("shqk,skhd->sqhd", probs, packed[:, :, 2], preferred_element_type=jnp.float32)
    context = context.reshape(-1, model_width).astype(jnp.bfloat16)
    return (times(context, out_w) + out_b).reshape(count, length, model_width)


def optimize(weight, grad, first, second, factor):
    clipped = grad * factor
    first_new = beta_one * first + (1.0 - beta_one) * clipped
    second_new = beta_two * second + (1.0 - beta_two) * clipped * clipped
    direction = (
        first_new
        / (1.0 - beta_one**STEP)
        / (jnp.sqrt(second_new / (1.0 - beta_two**STEP)) + adam_eps)
        + weight_decay * weight
    )
    return (first_new, second_new, direction)


def shards(
    resid_pre,
    token_ids,
    valid_mask,
    picked,
    norm_gains,
    norm_biases,
    qkv_w,
    out_w,
    fc_w,
    proj_w,
    layer_bias,
    wte,
    w_enc,
    enc_first,
    enc_second,
    b_enc,
    w_dec,
    dec_first,
    dec_second,
    b_dec,
):
    low = jnp.bfloat16
    count, seq_len, model_width = resid_pre.shape
    size = lax.axis_size("fsdp")
    mine = lax.axis_index("fsdp")
    pick_count = picked.shape[1]
    rest_count = seq_len - pick_count
    hidden_units = fc_w.shape[1]
    vocab_rows = wte.shape[0]
    total_picks = lax.axis_size("dp") * size * count * pick_count
    qkv_b = layer_bias[: 3 * model_width]
    out_b = layer_bias[3 * model_width : 4 * model_width]
    fc_b = layer_bias[4 * model_width : 4 * model_width + hidden_units]
    proj_b = layer_bias[4 * model_width + hidden_units :]

    order = jnp.arange(size) ^ mine
    ids = token_ids.reshape(size, count, seq_len)[order]
    mask = valid_mask.reshape(size, count, seq_len)[order].astype(jnp.float32)
    picks = picked.reshape(size, count, pick_count)[order]
    place = lax.broadcasted_iota(jnp.int32, (1, 1, 1, seq_len), 3)
    chosen = picks[..., None] == place
    targets = jnp.sum(jnp.where(picks[..., None] + 1 == place, ids[:, :, None, :], 0), -1)
    free = jnp.logical_not(jnp.any(chosen, 2))
    before = lax.broadcasted_iota(jnp.int32, (seq_len, seq_len), 0) > lax.broadcasted_iota(
        jnp.int32, (seq_len, seq_len), 1
    )
    rank = jnp.sum(jnp.where(before & free[:, :, None, :], 1, 0), -1)
    slot = lax.broadcasted_iota(jnp.int32, (1, 1, rest_count, 1), 2)
    others = (rank[:, :, None, :] == slot) & free[:, :, None, :]
    pick_mask = jnp.sum(jnp.where(chosen, mask[:, :, None, :], 0.0), -1).reshape(1, -1)
    rest_mask = jnp.sum(jnp.where(others, mask[:, :, None, :], 0.0), -1).reshape(1, -1)
    masks = gather_copies(jnp.concatenate([pick_mask, rest_mask], 1))
    half = pick_mask.shape[1]
    pick_mask = jnp.concatenate([held[0, :half] for held in masks])
    rest_mask = jnp.concatenate([held[0, half:] for held in masks])
    sparse_coef = l1_scale / F / (jnp.sum(pick_mask) + jnp.sum(rest_mask))

    inputs = resid_pre.astype(jnp.float32)
    attn = attention(inputs, norm_gains[0], norm_biases[0], qkv_w, qkv_b, out_w, out_b)
    centered = (attn - b_dec).astype(low)

    def rows_of(selector, values):
        return jnp.einsum("skl,sld->skd", selector.astype(low), values).reshape(-1, model_width)

    own_pick = rows_of(chosen[0], centered)
    own_rest = rows_of(others[0], centered)
    own_inputs = rows_of(chosen[0], resid_pre).astype(jnp.float32)

    enc_low = w_enc.astype(low)
    dec_low = w_dec.astype(low)
    group_pick = jnp.concatenate(gather_group(own_pick), 0)
    features = jnp.maximum(times_trans(group_pick, enc_low) + b_enc, 0.0)
    feat_low = features.astype(low)
    shares = times(feat_low, dec_low).astype(low).reshape(size, -1, model_width)
    recon = sum_to_owners([shares[k] for k in range(size)]) + b_dec

    mid = own_inputs + recon
    normed, second_norm_back = jax.vjp(
        lambda values: layer_norm(values, norm_gains[1], norm_biases[1]), mid
    )
    up_val = times(normed.astype(low), fc_w) + fc_b
    act, gelu_back = jax.vjp(lambda values: jax.nn.gelu(values, approximate=True), up_val)
    hidden = mid + times(act.astype(low), proj_w) + proj_b
    final, final_norm_back = jax.vjp(
        lambda values: layer_norm(values, norm_gains[2], norm_biases[2]), hidden
    )
    finals = jnp.concatenate(gather_group(final.astype(low)), 0)

    all_pick = jnp.concatenate(gather_copies(group_pick), 0)
    all_rest = jnp.concatenate(
        gather_copies(jnp.concatenate(gather_group(own_rest), 0)), 0
    )
    group_rows = group_pick.shape[0]
    more = jnp.maximum(times_trans(all_pick[group_rows:], enc_low) + b_enc, 0.0)
    all_feat = jnp.concatenate([feat_low, more.astype(low)], 0)
    idle = jnp.maximum(times_trans(all_rest, enc_low) + b_enc, 0.0)
    sparse = (
        jnp.sum(pick_mask[:group_rows, None] * features)
        + jnp.sum(pick_mask[group_rows:, None] * more)
        + jnp.sum(rest_mask[:, None] * idle)
    )
    idle_pre = jnp.where(idle > 0, sparse_coef * rest_mask[:, None], 0.0).astype(low)
    idle_grad = trans_times(idle_pre, all_rest)

    logits = times_trans(finals, wte)
    columns = lax.broadcasted_iota(jnp.int32, logits.shape, 1)
    at_target = columns == (targets.reshape(-1) - mine * vocab_rows)[:, None]
    top = jnp.max(logits, 1)
    mass = jnp.sum(jnp.exp(logits - top[:, None]), 1)
    at = jnp.sum(jnp.where(at_target, logits, 0.0), 1)
    stats = jnp.stack([top, mass, at]).reshape(3, size, -1)[:, order]
    stats = gather_small(stats)
    best = jnp.max(stats[:, 0], 0)
    log_total = best + jnp.log(jnp.sum(stats[:, 1] * jnp.exp(stats[:, 0] - best), 0))
    cross = jnp.sum(log_total - jnp.sum(stats[:, 2], 0))
    log_total = log_total[order].reshape(-1)
    dlogits = (
        (jnp.exp(logits - log_total[:, None]) - at_target.astype(jnp.float32)) / total_picks
    ).astype(low)
    shares = times(dlogits, wte).astype(low).reshape(size, -1, model_width)
    dfinal = sum_to_owners([shares[k] for k in range(size)])

    dhidden = final_norm_back(dfinal)[0]
    dact = times_trans(dhidden.astype(low), proj_w)
    dup_low = gelu_back(dact)[0].astype(low)
    dnormed = times_trans(dup_low, fc_w)
    drecon = (dhidden + second_norm_back(dnormed)[0]).astype(low)

    group_drecon = jnp.concatenate(gather_group(drecon), 0)
    all_drecon = jnp.concatenate(gather_copies(group_drecon), 0)
    dfeatures = times_trans(all_drecon, dec_low)
    dpre = jnp.where(all_feat > 0, dfeatures + sparse_coef * pick_mask[:, None], 0.0).astype(low)
    grad_dec = trans_times(all_feat, all_drecon)
    grad_enc = idle_grad + trans_times(dpre, all_pick)

    cross = sum(held[0, 0] for held in gather_copies(jnp.broadcast_to(cross, (1, 128))))
    square_total, enc_square, dec_square, sparse = sum_small(
        [
            jnp.sum(grad_enc * grad_enc) + jnp.sum(grad_dec * grad_dec),
            jnp.sum(w_enc * w_enc),
            jnp.sum(w_dec * w_dec),
            sparse,
        ]
    )
    loss = cross / total_picks + sparse_coef * sparse
    clip_norm = jnp.sqrt(square_total)
    factor = clip_limit / jnp.maximum(clip_norm, clip_limit)
    enc_m, enc_v, enc_dir = optimize(w_enc, grad_enc, enc_first, enc_second, factor)
    dec_m, dec_v, dec_dir = optimize(w_dec, grad_dec, dec_first, dec_second, factor)
    enc_dir_sq, dec_dir_sq = sum_small([jnp.sum(enc_dir * enc_dir), jnp.sum(dec_dir * dec_dir)])
    enc_norm = jnp.sqrt(enc_square)
    enc_step = jnp.sqrt(enc_dir_sq)
    dec_norm = jnp.sqrt(dec_square)
    dec_step = jnp.sqrt(dec_dir_sq)
    new_enc = w_enc - learn_rate * (enc_norm / enc_step) * enc_dir
    dec_raw = w_dec - learn_rate * (dec_norm / dec_step) * dec_dir
    new_dec = dec_raw * lax.rsqrt(jnp.sum(dec_raw * dec_raw, 1, keepdims=True) + 1e-06)
    return (
        jnp.stack([new_enc, new_dec]),
        jnp.stack([enc_m, dec_m]),
        jnp.stack([enc_v, dec_v]),
        loss,
        clip_norm,
        jnp.stack([enc_norm, dec_norm]),
        jnp.stack([enc_step, dec_step]),
    )


def solution(mesh):
    in_specs = (
        P(("dp", "fsdp"), None, None),
        P("dp", None),
        P("dp", None),
        P("dp", None),
        P(),
        P(),
        P(),
        P(),
        P(),
        P(),
        P(),
        P("fsdp", None),
        P("fsdp", None),
        P("fsdp", None),
        P("fsdp", None),
        P("fsdp"),
        P("fsdp", None),
        P("fsdp", None),
        P("fsdp", None),
        P(),
    )
    out_specs = (
        P(None, "fsdp", None),
        P(None, "fsdp", None),
        P(None, "fsdp", None),
        P(),
        P(),
        P(),
        P(),
    )
    return jax.shard_map(shards, mesh=mesh, in_specs=in_specs, out_specs=out_specs, check_vma=False)
```

```python
import jax
import jax.numpy as jnp
from jax import lax
from jax.experimental import pallas as pl
from jax.experimental.pallas import tpu as pltpu
from jax.sharding import PartitionSpec as P

HEADS = 12
HEAD_DIM = 64
F = 24576
STEP = 10


norm_eps = 1e-05
l1_scale = 40.0
clip_limit = 0.02
learn_rate = 0.3
beta_one = 0.9
beta_two = 0.999
adam_eps = 1e-08
weight_decay = 0.01


def layer_norm(values, gain, shift):
    center = values - jnp.mean(values, -1, keepdims=True)
    spread = jnp.mean(center * center, -1, keepdims=True)
    return center * lax.rsqrt(spread + norm_eps) * gain + shift


def times(left, right):
    return jnp.dot(left, right, preferred_element_type=jnp.float32)


def times_trans(left, right):
    return lax.dot_general(
        left, right, (((1,), (1,)), ((), ())), preferred_element_type=jnp.float32
    )


def trans_times(left, right):
    return lax.dot_general(
        left, right, (((0,), (0,)), ((), ())), preferred_element_type=jnp.float32
    )


def swap(block, axis, bit):
    size = lax.axis_size(axis)
    return lax.ppermute(block, axis, [(i, i ^ bit) for i in range(size)])


def trade(blocks):
    return lax.all_to_all(blocks, "fsdp", 0, 0, tiled=True)


def gather_group(block):
    size = lax.axis_size("fsdp")
    spread = jnp.broadcast_to(block[None], (size, *block.shape))
    return trade(spread).reshape(-1, *block.shape[1:])


def sum_to_owners(shares):
    size = lax.axis_size("fsdp")
    blocks = shares.reshape(size, -1, shares.shape[1])
    return jnp.sum(trade(blocks).astype(jnp.float32), 0)


def pieces_of(block):
    size = lax.axis_size("fsdp")
    return [block] + [swap(block, "fsdp", k) for k in range(1, size)]


def paired(pieces):
    while len(pieces) > 1:
        pieces = [a + b for a, b in zip(pieces[::2], pieces[1::2])]
    return pieces[0]


def gather_copies(block):
    blocks = [block]
    bit = lax.axis_size("dp") // 2
    while bit:
        blocks = blocks + [swap(held, "dp", bit) for held in blocks]
        bit //= 2
    return blocks


def attention(inputs, gain, shift, qkv_w, qkv_b, out_w, out_b):
    count, length, model_width = inputs.shape
    normed = layer_norm(inputs, gain, shift).astype(jnp.bfloat16).reshape(-1, model_width)
    packed = (times(normed, qkv_w) + qkv_b).astype(jnp.bfloat16)
    packed = packed.reshape(count, length, 3, HEADS, HEAD_DIM)
    scores = jnp.einsum(
        "sqhd,skhd->shqk", packed[:, :, 0], packed[:, :, 1], preferred_element_type=jnp.float32
    ) * HEAD_DIM ** (-0.5)
    row_ids = lax.broadcasted_iota(jnp.int32, (length, length), 0)
    col_ids = lax.broadcasted_iota(jnp.int32, (length, length), 1)
    scores = jnp.where(row_ids >= col_ids, scores, -1e30)
    probs = jax.nn.softmax(scores, axis=-1).astype(jnp.bfloat16)
    context = jnp.einsum("shqk,skhd->sqhd", probs, packed[:, :, 2], preferred_element_type=jnp.float32)
    context = context.reshape(-1, model_width).astype(jnp.bfloat16)
    return (times(context, out_w) + out_b).reshape(count, length, model_width)


VMEM = pl.BlockSpec(memory_space=pltpu.VMEM)
PLACED = pl.BlockSpec(memory_space=pl.ANY)
ONCE = pl.Buffered(1)


def in_vmem(values):
    return pltpu.with_memory_space_constraint(values, pltpu.VMEM)


def in_hbm(values):
    return pltpu.with_memory_space_constraint(values, pltpu.HBM)


def fold(values):
    rows, width = values.shape
    total = jnp.sum(values.reshape(rows // 8, 8, width), 0)
    return sum(total[:, k : k + 128] for k in range(0, width, 128))


def block_rows(count, most):
    return max(rows for rows in range(16, most + 1, 16) if count % rows == 0)


def lower(w_enc, w_dec):
    feats, width = w_enc.shape
    rows = block_rows(feats, 512)

    def kernel(enc_ref, dec_ref, enc_low_ref, dec_low_ref, square_ref):
        @pl.when(pl.program_id(0) == 0)
        def _():
            square_ref[...] = jnp.zeros_like(square_ref)

        for plane, (full, low) in enumerate(((enc_ref, enc_low_ref), (dec_ref, dec_low_ref))):
            values = full[...]
            low[...] = values.astype(jnp.bfloat16)
            square_ref[plane] += fold(values * values)

    block = pl.BlockSpec((rows, width), lambda i: (i, 0))
    return pl.pallas_call(
        kernel,
        grid=(feats // rows,),
        in_specs=[block, block],
        out_specs=[block, block, pl.BlockSpec((2, 8, 128), lambda i: (0, 0, 0))],
        out_shape=[
            jax.ShapeDtypeStruct((feats, width), jnp.bfloat16),
            jax.ShapeDtypeStruct((feats, width), jnp.bfloat16),
            jax.ShapeDtypeStruct((2, 8, 128), jnp.float32),
        ],
        compiler_params=pltpu.CompilerParams(vmem_limit_bytes=20 << 20),
        cost_estimate=pl.CostEstimate(
            flops=4 * feats * width, bytes_accessed=12 * feats * width, transcendentals=0
        ),
        name="lower",
    )(w_enc, w_dec)


def feature_rows(tokens, enc_low, bias, masks):
    count = len(tokens)
    part, width = tokens[0].shape
    feats = enc_low.shape[0]
    rows = block_rows(feats, 512 if part <= 512 else 128)

    def kernel(*refs):
        token_refs = refs[:count]
        enc_ref, bias_ref, mask_ref, out_ref, sum_ref = refs[count:]

        @pl.when(pl.program_id(0) == 0)
        def _():
            sum_ref[...] = jnp.zeros_like(sum_ref)

        for k in range(count):
            at = pl.ds(k * part, part)
            pre = times_trans(enc_ref[...], token_refs[k][...]) + bias_ref[...]
            kept = jnp.maximum(pre, 0.0)
            out_ref[:, at] = kept.astype(jnp.bfloat16)
            sum_ref[...] += fold(kept * mask_ref[:, at])

    whole = pl.BlockSpec((part, width), lambda i: (0, 0), pipeline_mode=ONCE)
    return pl.pallas_call(
        kernel,
        grid=(feats // rows,),
        in_specs=[whole] * count
        + [
            pl.BlockSpec((rows, width), lambda i: (i, 0)),
            pl.BlockSpec((rows, 1), lambda i: (i, 0)),
            pl.BlockSpec((1, count * part), lambda i: (0, 0)),
        ],
        out_specs=[
            pl.BlockSpec((rows, count * part), lambda i: (i, 0)),
            pl.BlockSpec((8, 128), lambda i: (0, 0)),
        ],
        out_shape=[
            jax.ShapeDtypeStruct((feats, count * part), jnp.bfloat16),
            jax.ShapeDtypeStruct((8, 128), jnp.float32),
        ],
        compiler_params=pltpu.CompilerParams(
            vmem_limit_bytes=(24 << 20) + 2 * count * part * width
        ),
        cost_estimate=pl.CostEstimate(
            flops=2 * feats * width * count * part,
            bytes_accessed=2 * (feats + width) * count * part + 2 * feats * width,
            transcendentals=0,
        ),
        name="features",
    )(*tokens, enc_low, bias, masks)


def idle_gradient(tokens, enc_low, bias, masks, marks):
    count = len(tokens)
    part, width = tokens[0].shape
    feats = enc_low.shape[0]
    rows = block_rows(feats, 512 if part <= 512 else 128)

    def kernel(*refs):
        token_refs = refs[:count]
        enc_ref, bias_ref, mask_ref, mark_ref, out_ref, sum_ref = refs[count:]

        @pl.when(pl.program_id(0) == 0)
        def _():
            sum_ref[...] = jnp.zeros_like(sum_ref)

        grad = jnp.zeros(out_ref.shape, jnp.float32)
        for k in range(count):
            at = pl.ds(k * part, part)
            pre = times_trans(enc_ref[...], token_refs[k][...]) + bias_ref[...]
            sum_ref[...] += fold(jnp.maximum(pre, 0.0) * mask_ref[:, at])
            dpre = jnp.where(pre > 0, mark_ref[:, at], 0.0).astype(jnp.bfloat16)
            grad = grad + times(dpre, token_refs[k][...])
        out_ref[...] = grad

    whole = pl.BlockSpec((part, width), lambda i: (0, 0), pipeline_mode=ONCE)
    row = pl.BlockSpec((1, count * part), lambda i: (0, 0))
    return pl.pallas_call(
        kernel,
        grid=(feats // rows,),
        in_specs=[whole] * count
        + [
            pl.BlockSpec((rows, width), lambda i: (i, 0)),
            pl.BlockSpec((rows, 1), lambda i: (i, 0)),
            row,
            row,
        ],
        out_specs=[
            pl.BlockSpec((rows, width), lambda i: (i, 0)),
            pl.BlockSpec((8, 128), lambda i: (0, 0)),
        ],
        out_shape=[
            jax.ShapeDtypeStruct((feats, width), jnp.float32),
            jax.ShapeDtypeStruct((8, 128), jnp.float32),
        ],
        compiler_params=pltpu.CompilerParams(
            vmem_limit_bytes=(24 << 20) + 2 * count * part * width
        ),
        cost_estimate=pl.CostEstimate(
            flops=4 * feats * width * count * part,
            bytes_accessed=2 * width * count * part + 6 * feats * width,
            transcendentals=0,
        ),
        name="idle",
    )(*tokens, enc_low, bias, masks, marks)


def gradients(tokens, errors, features, dec_low, marks, idle):
    count = len(tokens)
    part, width = tokens[0].shape
    feats = dec_low.shape[0]
    rows = block_rows(feats, 256 if part <= 512 else 128)

    def kernel(*refs):
        token_refs, error_refs = refs[:count], refs[count : 2 * count]
        feat_ref, dec_ref, mark_ref, idle_ref, out_ref, square_ref = refs[2 * count :]

        @pl.when(pl.program_id(0) == 0)
        def _():
            square_ref[...] = jnp.zeros_like(square_ref)

        enc, dec = idle_ref[...], jnp.zeros(idle_ref.shape, jnp.float32)
        for k in range(count):
            at = pl.ds(k * part, part)
            feat = feat_ref[:, at]
            dfeat = times_trans(dec_ref[...], error_refs[k][...]) + mark_ref[:, at]
            dpre = jnp.where(feat > 0, dfeat, 0.0).astype(jnp.bfloat16)
            enc = enc + times(dpre, token_refs[k][...])
            dec = dec + times(feat, error_refs[k][...])
        out_ref[0] = enc
        out_ref[1] = dec
        square_ref[...] += fold(enc * enc) + fold(dec * dec)

    whole = pl.BlockSpec((part, width), lambda i: (0, 0), pipeline_mode=ONCE)
    return pl.pallas_call(
        kernel,
        grid=(feats // rows,),
        in_specs=[whole] * (2 * count)
        + [
            pl.BlockSpec((rows, count * part), lambda i: (i, 0)),
            pl.BlockSpec((rows, width), lambda i: (i, 0)),
            pl.BlockSpec((1, count * part), lambda i: (0, 0)),
            pl.BlockSpec((rows, width), lambda i: (i, 0)),
        ],
        out_specs=[
            pl.BlockSpec((2, rows, width), lambda i: (0, i, 0)),
            pl.BlockSpec((8, 128), lambda i: (0, 0)),
        ],
        out_shape=[
            pltpu.HBM((2, feats, width), jnp.float32),
            jax.ShapeDtypeStruct((8, 128), jnp.float32),
        ],
        compiler_params=pltpu.CompilerParams(
            vmem_limit_bytes=(18 << 20) + 4 * count * part * width
        ),
        cost_estimate=pl.CostEstimate(
            flops=6 * feats * width * count * part,
            bytes_accessed=(2 * feats + 4 * width) * count * part + 14 * feats * width,
            transcendentals=0,
        ),
        name="gradients",
    )(*tokens, *errors, features, dec_low, marks, idle)


def room(pieces, feats, width):
    def kernel(*refs):
        total = jnp.sum(paired([ref[...] for ref in refs[:-2]]), keepdims=True).reshape(1, 1)
        refs[-2][...] = jnp.broadcast_to(jnp.sqrt(total), refs[-2].shape)

    return pl.pallas_call(
        kernel,
        in_specs=[VMEM] * len(pieces),
        out_specs=[VMEM, PLACED],
        out_shape=[
            jax.ShapeDtypeStruct((8, 128), jnp.float32),
            pltpu.VMEM((2, feats, width), jnp.float32),
        ],
        compiler_params=pltpu.CompilerParams(vmem_limit_bytes=1 << 20),
        name="room",
    )(*pieces)


def moments(clip_norm, space, grads, w_enc, enc_first, enc_second, w_dec, dec_first, dec_second):
    _, feats, width = grads.shape
    rows = block_rows(feats, 192)


    def kernel(norm_ref, space_ref, grad_ref, *refs):
        del space_ref
        enc, dec, outs = refs[:3], refs[3:6], refs[6:]
        dir_ref, first_out, second_out, square_ref = outs
        factor = clip_limit / jnp.maximum(norm_ref[:1, :1], clip_limit)
        square_ref[...] = jnp.zeros_like(square_ref)

        def body(grad, enc_first, enc_second, dec_first, dec_second, first_ref, second_ref):
            at = pl.ds(pl.multiple_of(pl.program_id(0) * rows, rows), rows)
            sides = ((enc[0], enc_first, enc_second), (dec[0], dec_first, dec_second))
            for plane, (weight, first, second) in enumerate(sides):
                clipped = grad[plane] * factor
                first_new = beta_one * first[...] + (1.0 - beta_one) * clipped
                second_new = beta_two * second[...] + (1.0 - beta_two) * clipped * clipped
                first_ref[plane] = first_new
                second_ref[plane] = second_new
                scaled = second_new * (1.0 / (1.0 - beta_two**STEP))
                spread = scaled * lax.rsqrt(scaled) + adam_eps
                direction = (
                    first_new * (1.0 / (1.0 - beta_one**STEP)) * pltpu.reciprocal(spread)
                    + weight_decay * weight[at, :]
                )
                dir_ref[plane, at, :] = direction
                square_ref[plane] += fold(direction * direction)

        block = pl.BlockSpec((rows, width), lambda i: (i, 0))
        both = pl.BlockSpec((2, rows, width), lambda i: (0, i, 0))
        pltpu.emit_pipeline(
            body, grid=(feats // rows,), in_specs=[both] + [block] * 4, out_specs=[both, both]
        )(grad_ref, enc[1], enc[2], dec[1], dec[2], first_out, second_out)

    full = (2, feats, width)
    return pl.pallas_call(
        kernel,
        in_specs=[VMEM, VMEM, PLACED, VMEM, PLACED, PLACED, VMEM, PLACED, PLACED],
        out_specs=[VMEM, PLACED, PLACED, VMEM],
        out_shape=[
            pltpu.VMEM(full, jnp.float32),
            pltpu.HBM(full, jnp.float32),
            pltpu.HBM(full, jnp.float32),
            jax.ShapeDtypeStruct((2, 8, 128), jnp.float32),
        ],
        input_output_aliases={1: 0},
        compiler_params=pltpu.CompilerParams(vmem_limit_bytes=16 << 20),
        cost_estimate=pl.CostEstimate(
            flops=20 * grads.size, bytes_accessed=20 * grads.size, transcendentals=grads.size
        ),
        name="moments",
    )(
        clip_norm,
        in_vmem(space),
        in_hbm(grads),
        in_vmem(w_enc),
        in_hbm(enc_first),
        in_hbm(enc_second),
        in_vmem(w_dec),
        in_hbm(dec_first),
        in_hbm(dec_second),
    )


def renew(sums, small, terms, clip_norm, direction, w_enc, w_dec, total_picks):
    _, feats, width = direction.shape
    rows = block_rows(feats, 256)

    count = len(sums)

    def kernel(*refs):
        sum_refs = refs[:count]
        small_ref, term_ref, clip_ref, dir_ref, enc_ref, dec_ref, out_ref, row_ref = refs[count:]
        sums = paired([ref[...] for ref in sum_refs])
        def total(values):
            return jnp.sum(values, keepdims=True).reshape(1, 1)

        norms = [jnp.sqrt(total(small_ref[:, plane])) for plane in range(2)]
        steps = [jnp.sqrt(total(sums[plane])) for plane in range(2)]
        rates = [learn_rate * (norms[plane] / steps[plane]) for plane in range(2)]
        loss = term_ref[0, :1, :1] / total_picks + term_ref[1, :1, :1] * total(small_ref[:, 2])
        for i, value in enumerate((*norms, *steps, loss, clip_ref[:1, :1])):
            row_ref[i : i + 1, :] = jnp.broadcast_to(value, (1, 128))
        row_ref[6:, :] = jnp.zeros((2, 128), jnp.float32)

        def body(new_ref):
            at = pl.ds(pl.multiple_of(pl.program_id(0) * rows, rows), rows)
            new_ref[0] = enc_ref[at, :] - rates[0] * dir_ref[0, at, :]
            raw = dec_ref[at, :] - rates[1] * dir_ref[1, at, :]
            new_ref[1] = raw * lax.rsqrt(jnp.sum(raw * raw, 1, keepdims=True) + 1e-06)

        both = pl.BlockSpec((2, rows, width), lambda i: (0, i, 0))
        pltpu.emit_pipeline(body, grid=(feats // rows,), out_specs=[both])(out_ref)

    return pl.pallas_call(
        kernel,
        in_specs=[VMEM] * (count + 6),
        out_specs=[PLACED, VMEM],
        out_shape=[
            pltpu.HBM(direction.shape, jnp.float32),
            jax.ShapeDtypeStruct((8, 128), jnp.float32),
        ],
        compiler_params=pltpu.CompilerParams(vmem_limit_bytes=16 << 20),
        cost_estimate=pl.CostEstimate(
            flops=6 * direction.size, bytes_accessed=4 * direction.size, transcendentals=0
        ),
        name="renew",
    )(*sums, small, terms, clip_norm, in_vmem(direction), in_vmem(w_enc), in_vmem(w_dec))


def shards(
    resid_pre,
    token_ids,
    valid_mask,
    picked,
    norm_gains,
    norm_biases,
    qkv_w,
    out_w,
    fc_w,
    proj_w,
    layer_bias,
    wte,
    w_enc,
    enc_first,
    enc_second,
    b_enc,
    w_dec,
    dec_first,
    dec_second,
    b_dec,
):
    low = jnp.bfloat16
    count, seq_len, model_width = resid_pre.shape
    size = lax.axis_size("fsdp")
    mine = lax.axis_index("fsdp")
    pick_count = picked.shape[1]
    rest_count = seq_len - pick_count
    hidden_units = fc_w.shape[1]
    vocab_rows = wte.shape[0]
    total_picks = lax.axis_size("dp") * size * count * pick_count
    qkv_b = layer_bias[: 3 * model_width]
    out_b = layer_bias[3 * model_width : 4 * model_width]
    fc_b = layer_bias[4 * model_width : 4 * model_width + hidden_units]
    proj_b = layer_bias[4 * model_width + hidden_units :]

    inputs = resid_pre.astype(jnp.float32)
    attn = attention(inputs, norm_gains[0], norm_biases[0], qkv_w, qkv_b, out_w, out_b)
    centered = (attn - b_dec).astype(low)

    place = lax.broadcasted_iota(jnp.int32, (1, 1, 1, seq_len), 3)
    before = lax.broadcasted_iota(jnp.int32, (seq_len, seq_len), 0) > lax.broadcasted_iota(
        jnp.int32, (seq_len, seq_len), 1
    )
    slot = lax.broadcasted_iota(jnp.int32, (1, 1, rest_count, 1), 2)

    def selectors(picks):
        chosen = picks[..., None] == place
        free = jnp.logical_not(jnp.any(chosen, 2))
        rank = jnp.sum(jnp.where(before & free[:, :, None, :], 1, 0), -1)
        return chosen, (rank[:, :, None, :] == slot) & free[:, :, None, :]

    def rows_of(selector, values):
        return jnp.einsum("skl,sld->skd", selector.astype(low), values).reshape(-1, model_width)

    grouped_picks = picked.reshape(size, count, pick_count)
    chosen, others = selectors(lax.dynamic_slice_in_dim(grouped_picks, mine, 1, 0))
    own_pick = rows_of(chosen[0], centered)
    own_rest = rows_of(others[0], centered)
    own_inputs = rows_of(chosen[0], resid_pre).astype(jnp.float32)

    token_ids, valid_mask, grouped_picks, own_pick = lax.optimization_barrier(
        (token_ids, valid_mask, grouped_picks, own_pick)
    )
    enc_low, dec_low, weight_squares = lower(w_enc, w_dec)
    group_pick = gather_group(own_pick)
    ids = token_ids.reshape(size, count, seq_len)
    mask = valid_mask.reshape(size, count, seq_len).astype(jnp.float32)
    chosen, others = selectors(grouped_picks)
    targets = jnp.sum(jnp.where(grouped_picks[..., None] + 1 == place, ids[:, :, None, :], 0), -1)
    pick_mask = jnp.sum(jnp.where(chosen, mask[:, :, None, :], 0.0), -1).reshape(1, -1)
    rest_mask = jnp.sum(jnp.where(others, mask[:, :, None, :], 0.0), -1).reshape(1, -1)
    masks = gather_copies(jnp.concatenate([pick_mask, rest_mask], 1))
    half = pick_mask.shape[1]
    pick_mask = jnp.concatenate([held[:, :half] for held in masks], 1)
    rest_mask = jnp.concatenate([held[:, half:] for held in masks], 1)
    sparse_coef = l1_scale / F / (jnp.sum(pick_mask) + jnp.sum(rest_mask))
    pick_marks, rest_marks = sparse_coef * pick_mask, sparse_coef * rest_mask
    bias = b_enc.reshape(-1, 1)

    features = jnp.maximum(times_trans(group_pick, enc_low) + b_enc, 0.0).astype(low)
    recon = sum_to_owners(times(features, dec_low).astype(low)) + b_dec
    all_pick = gather_copies(group_pick)

    mid = own_inputs + recon
    normed, second_norm_back = jax.vjp(
        lambda values: layer_norm(values, norm_gains[1], norm_biases[1]), mid
    )
    up_val = times(normed.astype(low), fc_w) + fc_b
    act, gelu_back = jax.vjp(lambda values: jax.nn.gelu(values, approximate=True), up_val)
    hidden = mid + times(act.astype(low), proj_w) + proj_b
    final, final_norm_back = jax.vjp(
        lambda values: layer_norm(values, norm_gains[2], norm_biases[2]), hidden
    )
    finals = gather_group(final.astype(low))
    all_feat, pick_sparse = feature_rows(all_pick, enc_low, bias, pick_mask)
    finals, all_feat, own_rest = lax.optimization_barrier((finals, all_feat, own_rest))
    group_rest = gather_group(own_rest)

    logits = times_trans(finals, wte)
    columns = lax.broadcasted_iota(jnp.int32, logits.shape, 1)
    at_target = columns == (targets.reshape(-1) - mine * vocab_rows)[:, None]
    top = jnp.max(logits, 1)
    mass = jnp.sum(jnp.exp(logits - top[:, None]), 1)
    at = jnp.sum(jnp.where(at_target, logits, 0.0), 1)
    stats = trade(jnp.broadcast_to(jnp.stack([top, mass, at])[None], (size, 3, top.shape[0])))
    best = jnp.max(stats[:, 0], 0)
    log_total = best + jnp.log(jnp.sum(stats[:, 1] * jnp.exp(stats[:, 0] - best), 0))
    cross = jnp.sum(log_total - jnp.sum(stats[:, 2], 0))
    dlogits = (
        (jnp.exp(logits - log_total[:, None]) - at_target.astype(jnp.float32)) / total_picks
    ).astype(low)
    dfinal = sum_to_owners(times(dlogits, wte).astype(low))

    dhidden = final_norm_back(dfinal)[0]
    dact = times_trans(dhidden.astype(low), proj_w)
    dup_low = gelu_back(dact)[0].astype(low)
    dnormed = times_trans(dup_low, fc_w)
    drecon = (dhidden + second_norm_back(dnormed)[0]).astype(low)

    drecon, group_rest = lax.optimization_barrier((drecon, group_rest))
    all_rest = gather_copies(group_rest)
    all_error = gather_copies(gather_group(drecon))
    idle, rest_sparse = idle_gradient(all_rest, enc_low, bias, rest_mask, rest_marks)

    cross = sum(gather_copies(jnp.broadcast_to(cross, (1, 128))))
    small = jnp.stack([weight_squares[0], weight_squares[1], pick_sparse + rest_sparse])
    small = trade(jnp.broadcast_to(small[None], (size, 3, 8, 128)))
    terms = jnp.stack([cross, jnp.broadcast_to(sparse_coef, (1, 128))])
    all_error[0], small, terms = lax.optimization_barrier((all_error[0], small, terms))

    grads, squares = gradients(all_pick, all_error, all_feat, dec_low, pick_marks, idle)
    clip_norm, space = room(pieces_of(squares), *w_enc.shape)
    direction, firsts, seconds, squares = moments(
        clip_norm, space, grads, w_enc, enc_first, enc_second, w_dec, dec_first, dec_second
    )
    weights, rows = renew(
        pieces_of(squares), small, terms, clip_norm, direction, w_enc, w_dec, total_picks
    )
    return weights, firsts, seconds, rows[4, 0], rows[5, 0], rows[:2, 0], rows[2:4, 0]


def solution(mesh):
    in_specs = (
        P(("dp", "fsdp"), None, None),
        P("dp", None),
        P("dp", None),
        P("dp", None),
        P(),
        P(),
        P(),
        P(),
        P(),
        P(),
        P(),
        P("fsdp", None),
        P("fsdp", None),
        P("fsdp", None),
        P("fsdp", None),
        P("fsdp"),
        P("fsdp", None),
        P("fsdp", None),
        P("fsdp", None),
        P(),
    )
    out_specs = (
        P(None, "fsdp", None),
        P(None, "fsdp", None),
        P(None, "fsdp", None),
        P(),
        P(),
        P(),
        P(),
    )
    return jax.shard_map(shards, mesh=mesh, in_specs=in_specs, out_specs=out_specs, check_vma=False)
```

```python
import jax
import jax.numpy as jnp
from jax import lax
from jax.experimental import pallas as pl
from jax.experimental.pallas import tpu as pltpu
from jax.sharding import PartitionSpec as P

HEADS = 12
HEAD_DIM = 64
F = 24576
STEP = 10


norm_eps = 1e-05
l1_scale = 40.0
clip_limit = 0.02
learn_rate = 0.3
beta_one = 0.9
beta_two = 0.999
adam_eps = 1e-08
weight_decay = 0.01


def layer_norm(values, gain, shift):
    center = values - jnp.mean(values, -1, keepdims=True)
    spread = jnp.mean(center * center, -1, keepdims=True)
    return center * lax.rsqrt(spread + norm_eps) * gain + shift


def times(left, right):
    return jnp.dot(left, right, preferred_element_type=jnp.float32)


def times_trans(left, right):
    return lax.dot_general(
        left, right, (((1,), (1,)), ((), ())), preferred_element_type=jnp.float32
    )


def trans_times(left, right):
    return lax.dot_general(
        left, right, (((0,), (0,)), ((), ())), preferred_element_type=jnp.float32
    )


def swap(block, axis, bit):
    size = lax.axis_size(axis)
    return lax.ppermute(block, axis, [(i, i ^ bit) for i in range(size)])


def trade(blocks):
    return lax.all_to_all(blocks, "fsdp", 0, 0, tiled=True)


def gather_group(block):
    size = lax.axis_size("fsdp")
    spread = jnp.broadcast_to(block[None], (size, *block.shape))
    return trade(spread).reshape(-1, *block.shape[1:])


def gather_near(block):
    half = lax.axis_size("fsdp") // 2
    far = swap(block, "fsdp", half)
    near = [block] + [swap(block, "fsdp", k) for k in range(1, half)]
    return near + [far] + [swap(far, "fsdp", k) for k in range(1, half)]


def pieces_of(block):
    size = lax.axis_size("fsdp")
    return [block] + [swap(block, "fsdp", k) for k in range(1, size)]


def paired(pieces):
    while len(pieces) > 1:
        pieces = [a + b for a, b in zip(pieces[::2], pieces[1::2])]
    return pieces[0]


def gather_copies(block):
    blocks = [block]
    bit = lax.axis_size("dp") // 2
    while bit:
        blocks = blocks + [swap(held, "dp", bit) for held in blocks]
        bit //= 2
    return blocks


def attention(inputs, gain, shift, qkv_w, qkv_b, out_w, out_b):
    count, length, model_width = inputs.shape
    normed = layer_norm(inputs, gain, shift).astype(jnp.bfloat16).reshape(-1, model_width)
    packed = (times(normed, qkv_w) + qkv_b).astype(jnp.bfloat16)
    packed = packed.reshape(count, length, 3, HEADS, HEAD_DIM)
    scores = jnp.einsum(
        "sqhd,skhd->shqk", packed[:, :, 0], packed[:, :, 1], preferred_element_type=jnp.float32
    ) * HEAD_DIM ** (-0.5)
    row_ids = lax.broadcasted_iota(jnp.int32, (length, length), 0)
    col_ids = lax.broadcasted_iota(jnp.int32, (length, length), 1)
    scores = jnp.where(row_ids >= col_ids, scores, -1e30)
    probs = jax.nn.softmax(scores, axis=-1).astype(jnp.bfloat16)
    context = jnp.einsum("shqk,skhd->sqhd", probs, packed[:, :, 2], preferred_element_type=jnp.float32)
    context = context.reshape(-1, model_width).astype(jnp.bfloat16)
    return (times(context, out_w) + out_b).reshape(count, length, model_width)


VMEM = pl.BlockSpec(memory_space=pltpu.VMEM)
PLACED = pl.BlockSpec(memory_space=pl.ANY)
ONCE = pl.Buffered(1)


def in_vmem(values):
    return pltpu.with_memory_space_constraint(values, pltpu.VMEM)


def in_hbm(values):
    return pltpu.with_memory_space_constraint(values, pltpu.HBM)


def fold(values):
    rows, width = values.shape
    total = jnp.sum(values.reshape(rows // 8, 8, width), 0)
    return sum(total[:, k : k + 128] for k in range(0, width, 128))


def block_rows(count, most):
    return max(rows for rows in range(16, most + 1, 16) if count % rows == 0)


def scalars(grid, in_specs, out_specs, scratch_shapes=()):
    return pltpu.PrefetchScalarGridSpec(
        num_scalar_prefetch=1,
        grid=grid,
        in_specs=in_specs,
        out_specs=out_specs,
        scratch_shapes=scratch_shapes,
    )


def join(blocks, kinds):
    rows, width = blocks[0].shape
    part = rows // kinds
    count = len(blocks)

    def kernel(*refs):
        for kind in range(kinds):
            for k, ref in enumerate(refs[:-1]):
                at = (kind * count + k) * part
                refs[-1][at : at + part, :] = ref[kind * part : (kind + 1) * part, :]

    return pl.pallas_call(
        kernel,
        in_specs=[VMEM] * count,
        out_specs=VMEM,
        out_shape=jax.ShapeDtypeStruct((rows * count, width), blocks[0].dtype),
        name="join",
    )(*blocks)


def encode(mine, tokens, count, part, w_enc, w_dec, b_enc):
    width = tokens.shape[1]
    feats = w_enc.shape[0]
    rows = block_rows(feats, 512)
    steps = feats // rows

    def kernel(mine_ref, token_ref, enc_ref, dec_ref, bias_ref, *refs):
        share_ref, enc_low_ref, dec_low_ref, square_ref, total_ref = refs

        @pl.when(pl.program_id(0) == 0)
        def _():
            square_ref[...] = jnp.zeros_like(square_ref)
            total_ref[...] = jnp.zeros_like(total_ref)

        enc, dec = enc_ref[...], dec_ref[...]
        square_ref[0] += fold(enc * enc)
        square_ref[1] += fold(dec * dec)
        enc_low, dec_low = enc.astype(jnp.bfloat16), dec.astype(jnp.bfloat16)
        enc_low_ref[...] = enc_low
        dec_low_ref[...] = dec_low
        features = jnp.maximum(times_trans(token_ref[...], enc_low) + bias_ref[...], 0.0)
        total_ref[...] += times(features.astype(jnp.bfloat16), dec_low)

        @pl.when(pl.program_id(0) == steps - 1)
        def _():
            for k in range(count):
                share_ref[mine_ref[0] ^ k] = total_ref[k * part : (k + 1) * part, :].astype(
                    jnp.bfloat16
                )

    whole = pl.BlockSpec((count * part, width), lambda i, s: (0, 0), pipeline_mode=ONCE)
    block = pl.BlockSpec((rows, width), lambda i, s: (i, 0))
    return pl.pallas_call(
        kernel,
        grid_spec=scalars(
            (steps,),
            [whole, block, block, pl.BlockSpec((1, rows), lambda i, s: (0, i))],
            [
                pl.BlockSpec((count, part, width), lambda i, s: (0, 0, 0)),
                block,
                block,
                pl.BlockSpec((2, 8, 128), lambda i, s: (0, 0, 0)),
            ],
            [pltpu.VMEM((count * part, width), jnp.float32)],
        ),
        out_shape=[
            jax.ShapeDtypeStruct((count, part, width), jnp.bfloat16),
            pltpu.HBM((feats, width), jnp.bfloat16),
            pltpu.HBM((feats, width), jnp.bfloat16),
            jax.ShapeDtypeStruct((2, 8, 128), jnp.float32),
        ],
        compiler_params=pltpu.CompilerParams(
            vmem_limit_bytes=(24 << 20) + 12 * count * part * width
        ),
        cost_estimate=pl.CostEstimate(
            flops=4 * feats * width * count * part, bytes_accessed=12 * feats * width, transcendentals=0
        ),
        name="encode",
    )(mine, in_hbm(tokens), in_hbm(w_enc), in_hbm(w_dec), b_enc)


def feature_rows(core, tokens, part, enc_low, bias, masks):
    count = len(tokens)
    width = tokens[0].shape[1]
    feats = enc_low.shape[0] // 2
    rows = block_rows(feats, 512 if part <= 512 else 128)
    steps = feats // rows

    def kernel(core_ref, *refs):
        token_refs = refs[:count]
        enc_ref, bias_ref, mask_ref, out_ref, sum_ref = refs[count:]

        @pl.when(pl.program_id(0) == 0)
        def _():
            sum_ref[...] = jnp.zeros_like(sum_ref)

        for k in range(count):
            at = pl.ds(k * part, part)
            pre = times_trans(enc_ref[...], token_refs[k][...]) + bias_ref[...]
            kept = jnp.maximum(pre, 0.0)
            out_ref[:, at] = kept.astype(jnp.bfloat16)
            sum_ref[...] += fold(kept * mask_ref[:, at])

    whole = pl.BlockSpec((part, width), lambda i, s: (0, 0), pipeline_mode=ONCE)
    return pl.pallas_call(
        kernel,
        grid_spec=scalars(
            (steps,),
            [whole] * count
            + [
                pl.BlockSpec((rows, width), lambda i, s: (s[0] * steps + i, 0)),
                pl.BlockSpec((rows, 1), lambda i, s: (s[0] * steps + i, 0)),
                pl.BlockSpec((1, count * part), lambda i, s: (0, 0)),
            ],
            [
                pl.BlockSpec((rows, count * part), lambda i, s: (i, 0)),
                pl.BlockSpec((8, 128), lambda i, s: (0, 0)),
            ],
        ),
        out_shape=[
            pltpu.HBM((feats, count * part), jnp.bfloat16),
            jax.ShapeDtypeStruct((8, 128), jnp.float32),
        ],
        compiler_params=pltpu.CompilerParams(
            vmem_limit_bytes=(24 << 20) + 2 * count * part * width
        ),
        cost_estimate=pl.CostEstimate(
            flops=2 * feats * width * count * part,
            bytes_accessed=2 * (feats + width) * count * part + 2 * feats * width,
            transcendentals=0,
        ),
        name="features",
    )(core, *map(in_hbm, tokens), in_hbm(enc_low), bias, masks)


def idle_gradient(core, tokens, part, enc_low, bias, masks, marks):
    count = len(tokens)
    width = tokens[0].shape[1]
    feats = enc_low.shape[0] // 2
    rows = block_rows(feats, 512 if part <= 512 else 128)
    steps = feats // rows

    def kernel(core_ref, *refs):
        token_refs = refs[:count]
        enc_ref, bias_ref, mask_ref, mark_ref, out_ref, sum_ref = refs[count:]

        @pl.when(pl.program_id(0) == 0)
        def _():
            sum_ref[...] = jnp.zeros_like(sum_ref)

        grad = jnp.zeros(out_ref.shape, jnp.float32)
        for k in range(count):
            at = pl.ds(k * part, part)
            pre = times_trans(enc_ref[...], token_refs[k][...]) + bias_ref[...]
            sum_ref[...] += fold(jnp.maximum(pre, 0.0) * mask_ref[:, at])
            dpre = jnp.where(pre > 0, mark_ref[:, at], 0.0).astype(jnp.bfloat16)
            grad = grad + times(dpre, token_refs[k][...])
        out_ref[...] = grad

    whole = pl.BlockSpec((part, width), lambda i, s: (1, 0), pipeline_mode=ONCE)
    row = pl.BlockSpec((1, count * part), lambda i, s: (0, 0))
    return pl.pallas_call(
        kernel,
        grid_spec=scalars(
            (steps,),
            [whole] * count
            + [
                pl.BlockSpec((rows, width), lambda i, s: (s[0] * steps + i, 0)),
                pl.BlockSpec((rows, 1), lambda i, s: (s[0] * steps + i, 0)),
                row,
                row,
            ],
            [
                pl.BlockSpec((rows, width), lambda i, s: (i, 0)),
                pl.BlockSpec((8, 128), lambda i, s: (0, 0)),
            ],
        ),
        out_shape=[
            pltpu.HBM((feats, width), jnp.float32),
            jax.ShapeDtypeStruct((8, 128), jnp.float32),
        ],
        compiler_params=pltpu.CompilerParams(
            vmem_limit_bytes=(24 << 20) + 2 * count * part * width
        ),
        cost_estimate=pl.CostEstimate(
            flops=4 * feats * width * count * part,
            bytes_accessed=2 * width * count * part + 6 * feats * width,
            transcendentals=0,
        ),
        name="idle",
    )(core, *map(in_hbm, tokens), in_hbm(enc_low), bias, masks, marks)


def gradients(core, tokens, errors, features, dec_low, marks, idle):
    count = len(tokens)
    part, width = errors[0].shape
    feats = dec_low.shape[0] // 2
    rows = block_rows(feats, 256 if part <= 512 else 128)
    steps = feats // rows

    def kernel(core_ref, *refs):
        token_refs, error_refs = refs[:count], refs[count : 2 * count]
        feat_ref, dec_ref, mark_ref, idle_ref, out_ref, square_ref = refs[2 * count :]

        @pl.when(pl.program_id(0) == 0)
        def _():
            square_ref[...] = jnp.zeros_like(square_ref)

        enc, dec = idle_ref[...], jnp.zeros(idle_ref.shape, jnp.float32)
        for k in range(count):
            at = pl.ds(k * part, part)
            feat = feat_ref[:, at]
            dfeat = times_trans(dec_ref[...], error_refs[k][...]) + mark_ref[:, at]
            dpre = jnp.where(feat > 0, dfeat, 0.0).astype(jnp.bfloat16)
            enc = enc + times(dpre, token_refs[k][...])
            dec = dec + times(feat, error_refs[k][...])
        out_ref[0] = enc
        out_ref[1] = dec
        square_ref[...] += fold(enc * enc) + fold(dec * dec)

    whole = pl.BlockSpec((part, width), lambda i, s: (0, 0), pipeline_mode=ONCE)
    return pl.pallas_call(
        kernel,
        grid_spec=scalars(
            (steps,),
            [whole] * (2 * count)
            + [
                pl.BlockSpec((rows, count * part), lambda i, s: (i, 0)),
                pl.BlockSpec((rows, width), lambda i, s: (s[0] * steps + i, 0)),
                pl.BlockSpec((1, count * part), lambda i, s: (0, 0)),
                pl.BlockSpec((rows, width), lambda i, s: (i, 0)),
            ],
            [
                pl.BlockSpec((2, rows, width), lambda i, s: (0, i, 0)),
                pl.BlockSpec((8, 128), lambda i, s: (0, 0)),
            ],
        ),
        out_shape=[
            pltpu.HBM((2, feats, width), jnp.float32),
            jax.ShapeDtypeStruct((8, 128), jnp.float32),
        ],
        compiler_params=pltpu.CompilerParams(
            vmem_limit_bytes=(18 << 20) + 4 * count * part * width
        ),
        cost_estimate=pl.CostEstimate(
            flops=6 * feats * width * count * part,
            bytes_accessed=(2 * feats + 4 * width) * count * part + 14 * feats * width,
            transcendentals=0,
        ),
        name="gradients",
    )(
        core,
        *map(in_hbm, tokens),
        *map(in_hbm, errors),
        in_hbm(features),
        in_hbm(dec_low),
        marks,
        in_hbm(idle),
    )


def norm_of(pieces):
    def kernel(*refs):
        total = jnp.sum(paired([ref[...] for ref in refs[:-1]]), keepdims=True).reshape(1, 1)
        refs[-1][...] = jnp.broadcast_to(jnp.sqrt(total), refs[-1].shape)

    return pl.pallas_call(
        kernel,
        in_specs=[VMEM] * len(pieces),
        out_specs=VMEM,
        out_shape=jax.ShapeDtypeStruct((8, 128), jnp.float32),
        compiler_params=pltpu.CompilerParams(vmem_limit_bytes=1 << 20),
        name="norm",
    )(*pieces)


def moments(
    core, clip_norm, own, other, w_enc, enc_first, enc_second, w_dec, dec_first, dec_second
):
    feats, width = w_enc.shape
    rows = block_rows(feats // 2, 192)
    half = feats // 2 // rows
    steps = 2 * half

    def kernel(core_ref, norm_ref, own_ref, other_ref, *refs):
        enc, dec, outs = refs[:3], refs[3:6], refs[6:]
        dir_refs, (first_out, second_out, square_ref) = outs[:2], outs[2:]
        factor = clip_limit / jnp.maximum(norm_ref[:1, :1], clip_limit)
        square_ref[...] = jnp.zeros_like(square_ref)
        start = core_ref[0] * half

        def place(i):
            return lax.rem(start + i, steps)

        def body(own, other, enc_first, enc_second, dec_first, dec_second, first_ref, second_ref):
            step = pl.program_id(0)
            at = pl.ds(pl.multiple_of(place(step) * rows, rows), rows)
            sides = ((enc[0], enc_first, enc_second), (dec[0], dec_first, dec_second))
            for plane, (weight, first, second) in enumerate(sides):
                clipped = jnp.where(step < half, own[plane], other[plane]) * factor
                first_new = beta_one * first[...] + (1.0 - beta_one) * clipped
                second_new = beta_two * second[...] + (1.0 - beta_two) * clipped * clipped
                first_ref[plane] = first_new
                second_ref[plane] = second_new
                scaled = second_new * (1.0 / (1.0 - beta_two**STEP))
                spread = scaled * lax.rsqrt(scaled) + adam_eps
                direction = (
                    first_new * (1.0 / (1.0 - beta_one**STEP)) * pltpu.reciprocal(spread)
                    + weight_decay * weight[at, :]
                )
                dir_refs[plane][at, :] = direction
                square_ref[plane] += fold(direction * direction)

        block = pl.BlockSpec((rows, width), lambda i: (place(i), 0))
        both = pl.BlockSpec((2, rows, width), lambda i: (0, place(i), 0))
        early = pl.BlockSpec((2, rows, width), lambda i: (0, jnp.minimum(i, half - 1), 0))
        late = pl.BlockSpec((2, rows, width), lambda i: (0, jnp.maximum(i - half, 0), 0))
        pltpu.emit_pipeline(
            body,
            grid=(steps,),
            in_specs=[early, late] + [block] * 4,
            out_specs=[both, both],
        )(own_ref, other_ref, enc[1], enc[2], dec[1], dec[2], first_out, second_out)

    full = (2, feats, width)
    return pl.pallas_call(
        kernel,
        in_specs=[pl.BlockSpec(memory_space=pltpu.SMEM), VMEM, PLACED, PLACED]
        + [VMEM, PLACED, PLACED] * 2,
        out_specs=[VMEM, VMEM, PLACED, PLACED, VMEM],
        out_shape=[
            pltpu.VMEM((feats, width), jnp.float32),
            pltpu.VMEM((feats, width), jnp.float32),
            pltpu.HBM(full, jnp.float32),
            pltpu.HBM(full, jnp.float32),
            jax.ShapeDtypeStruct((2, 8, 128), jnp.float32),
        ],
        compiler_params=pltpu.CompilerParams(vmem_limit_bytes=16 << 20),
        cost_estimate=pl.CostEstimate(
            flops=40 * feats * width,
            bytes_accessed=40 * feats * width,
            transcendentals=4 * feats * width,
        ),
        name="moments",
    )(
        core,
        clip_norm,
        in_hbm(own),
        in_hbm(other),
        in_vmem(w_enc),
        in_hbm(enc_first),
        in_hbm(enc_second),
        in_vmem(w_dec),
        in_hbm(dec_first),
        in_hbm(dec_second),
    )


def renew(sums, small, terms, clip_norm, directions, w_enc, w_dec, total_picks):
    feats, width = w_enc.shape
    rows = block_rows(feats, 256)

    count = len(sums)

    def kernel(*refs):
        sum_refs = refs[:count]
        small_ref, term_ref, clip_ref, enc_dir, dec_dir, enc_ref, dec_ref, out_ref, row_ref = refs[count:]
        sums = paired([ref[...] for ref in sum_refs])
        def total(values):
            return jnp.sum(values, keepdims=True).reshape(1, 1)

        norms = [jnp.sqrt(total(small_ref[:, plane])) for plane in range(2)]
        steps = [jnp.sqrt(total(sums[plane])) for plane in range(2)]
        rates = [learn_rate * (norms[plane] / steps[plane]) for plane in range(2)]
        loss = term_ref[0, :1, :1] / total_picks + term_ref[1, :1, :1] * total(small_ref[:, 2])
        for i, value in enumerate((*norms, *steps, loss, clip_ref[:1, :1])):
            row_ref[i : i + 1, :] = jnp.broadcast_to(value, (1, 128))
        row_ref[6:, :] = jnp.zeros((2, 128), jnp.float32)

        def body(enc_w, dec_w, new_ref):
            at = pl.ds(pl.multiple_of(pl.program_id(0) * rows, rows), rows)
            new_ref[0] = enc_w[...] - rates[0] * enc_dir[at, :]
            raw = dec_w[...] - rates[1] * dec_dir[at, :]
            new_ref[1] = raw * lax.rsqrt(jnp.sum(raw * raw, 1, keepdims=True) + 1e-06)

        both = pl.BlockSpec((2, rows, width), lambda i: (0, i, 0))
        block = pl.BlockSpec((rows, width), lambda i: (i, 0))
        pltpu.emit_pipeline(
            body, grid=(feats // rows,), in_specs=[block, block], out_specs=[both]
        )(enc_ref, dec_ref, out_ref)

    return pl.pallas_call(
        kernel,
        in_specs=[VMEM] * (count + 5) + [PLACED] * 2,
        out_specs=[PLACED, VMEM],
        out_shape=[
            pltpu.HBM((2, feats, width), jnp.float32),
            jax.ShapeDtypeStruct((8, 128), jnp.float32),
        ],
        compiler_params=pltpu.CompilerParams(vmem_limit_bytes=16 << 20),
        cost_estimate=pl.CostEstimate(
            flops=12 * w_enc.size, bytes_accessed=8 * w_enc.size, transcendentals=0
        ),
        name="renew",
    )(*sums, small, terms, clip_norm, *map(in_vmem, directions), in_hbm(w_enc), in_hbm(w_dec))


def shards(
    resid_pre,
    token_ids,
    valid_mask,
    picked,
    norm_gains,
    norm_biases,
    qkv_w,
    out_w,
    fc_w,
    proj_w,
    layer_bias,
    wte,
    w_enc,
    enc_first,
    enc_second,
    b_enc,
    w_dec,
    dec_first,
    dec_second,
    b_dec,
):
    low = jnp.bfloat16
    count, seq_len, model_width = resid_pre.shape
    size = lax.axis_size("fsdp")
    mine = lax.axis_index("fsdp")
    pick_count = picked.shape[1]
    rest_count = seq_len - pick_count
    hidden_units = fc_w.shape[1]
    vocab_rows = wte.shape[0]
    total_picks = lax.axis_size("dp") * size * count * pick_count
    qkv_b = layer_bias[: 3 * model_width]
    out_b = layer_bias[3 * model_width : 4 * model_width]
    fc_b = layer_bias[4 * model_width : 4 * model_width + hidden_units]
    proj_b = layer_bias[4 * model_width + hidden_units :]

    inputs = resid_pre.astype(jnp.float32)
    attn = attention(inputs, norm_gains[0], norm_biases[0], qkv_w, qkv_b, out_w, out_b)
    centered = (attn - b_dec).astype(low)

    place = lax.broadcasted_iota(jnp.int32, (1, 1, 1, seq_len), 3)
    before = lax.broadcasted_iota(jnp.int32, (seq_len, seq_len), 0) > lax.broadcasted_iota(
        jnp.int32, (seq_len, seq_len), 1
    )
    slot = lax.broadcasted_iota(jnp.int32, (1, 1, rest_count, 1), 2)

    def selectors(picks):
        chosen = picks[..., None] == place
        free = jnp.logical_not(jnp.any(chosen, 2))
        rank = jnp.sum(jnp.where(before & free[:, :, None, :], 1, 0), -1)
        return chosen, (rank[:, :, None, :] == slot) & free[:, :, None, :]

    def rows_of(selector, values):
        return jnp.einsum("skl,sld->skd", selector.astype(low), values).reshape(-1, model_width)

    grouped_picks = picked.reshape(size, count, pick_count)
    chosen, others = selectors(lax.dynamic_slice_in_dim(grouped_picks, mine, 1, 0))
    own_pick = rows_of(chosen[0], centered)
    own_rest = rows_of(others[0], centered)
    own_inputs = rows_of(chosen[0], resid_pre).astype(jnp.float32)

    blocks = gather_near(jnp.concatenate([own_pick, own_rest], 0))
    group_rows = size * own_pick.shape[0]
    me = mine.reshape(1).astype(jnp.int32)
    core = (lax.axis_index("dp") & 1).reshape(1).astype(jnp.int32)
    tokens, token_ids, valid_mask, grouped_picks = lax.optimization_barrier(
        (join(blocks, 2), token_ids, valid_mask, grouped_picks)
    )
    shares, enc_low, dec_low, weight_squares = encode(
        me, tokens, size, own_pick.shape[0], w_enc, w_dec, b_enc.reshape(1, -1)
    )
    recon = jnp.sum(trade(shares).astype(jnp.float32), 0) + b_dec

    ids = token_ids.reshape(size, count, seq_len)
    mask = valid_mask.reshape(size, count, seq_len).astype(jnp.float32)
    chosen, others = selectors(grouped_picks)
    targets = jnp.sum(
        jnp.where(grouped_picks[..., None] + 1 == place, ids[:, :, None, :], 0), -1
    ).reshape(-1)
    targets = targets - mine * vocab_rows
    here = (targets >= 0) & (targets < vocab_rows)
    target_rows = jnp.take(wte, jnp.clip(targets, 0, vocab_rows - 1), axis=0)
    target_rows = jnp.where(here[:, None], target_rows, jnp.zeros_like(target_rows))
    order = jnp.arange(size) ^ mine
    pick_mask = jnp.sum(jnp.where(chosen, mask[:, :, None, :], 0.0), -1)[order].reshape(1, -1)
    rest_mask = jnp.sum(jnp.where(others, mask[:, :, None, :], 0.0), -1)[order].reshape(1, -1)
    masks = gather_copies(jnp.concatenate([pick_mask, rest_mask], 1))
    half = pick_mask.shape[1]
    pick_mask = jnp.concatenate([held[:, :half] for held in masks], 1)
    rest_mask = jnp.concatenate([held[:, half:] for held in masks], 1)
    sparse_coef = l1_scale / F / (jnp.sum(pick_mask) + jnp.sum(rest_mask))
    pick_marks, rest_marks = sparse_coef * pick_mask, sparse_coef * rest_mask
    bias = b_enc.reshape(-1, 1)
    all_tokens = gather_copies(tokens)
    recon, target_rows, pick_marks, rest_marks = lax.optimization_barrier(
        (recon, target_rows, pick_marks, rest_marks)
    )

    mid = own_inputs + recon
    normed, second_norm_back = jax.vjp(
        lambda values: layer_norm(values, norm_gains[1], norm_biases[1]), mid
    )
    up_val = times(normed.astype(low), fc_w) + fc_b
    act, gelu_back = jax.vjp(lambda values: jax.nn.gelu(values, approximate=True), up_val)
    hidden = mid + times(act.astype(low), proj_w) + proj_b
    final, final_norm_back = jax.vjp(
        lambda values: layer_norm(values, norm_gains[2], norm_biases[2]), hidden
    )
    finals = gather_group(final.astype(low))
    all_feat, pick_sparse = feature_rows(
        core, all_tokens, group_rows, enc_low, bias, pick_mask
    )
    finals, all_feat = lax.optimization_barrier((finals, all_feat))

    logits = times_trans(finals, wte)
    top = jnp.max(logits, 1)
    parts = jnp.exp(logits - top[:, None])
    mass = jnp.sum(parts, 1)
    at = jnp.sum(finals.astype(jnp.float32) * target_rows.astype(jnp.float32), 1)
    stats = trade(jnp.broadcast_to(jnp.stack([top, mass, at])[None], (size, 3, top.shape[0])))
    mixed = times(parts.astype(low), wte)
    stats, mixed = lax.optimization_barrier((stats, mixed))
    best = jnp.max(stats[:, 0], 0)
    total = jnp.sum(stats[:, 1] * jnp.exp(stats[:, 0] - best), 0)
    cross = jnp.sum(best + jnp.log(total) - jnp.sum(stats[:, 2], 0))
    scale = jnp.exp(top - best) / total
    dshares = (mixed * scale[:, None] - target_rows.astype(jnp.float32)) / total_picks
    dshares = dshares.astype(low).reshape(size, -1, model_width)
    dshares, idle_marks = lax.optimization_barrier((dshares, rest_marks))
    dfinal = jnp.sum(trade(dshares).astype(jnp.float32), 0)
    idle, rest_sparse = idle_gradient(
        core, all_tokens, group_rows, enc_low, bias, rest_mask, idle_marks
    )
    dfinal, idle, pick_sparse, cross = lax.optimization_barrier((dfinal, idle, pick_sparse, cross))

    cross = jnp.broadcast_to(cross, (1, 128))
    bit = lax.axis_size("dp") // 2
    while bit:
        cross = cross + swap(cross, "dp", bit)
        bit //= 2
    sparse = pick_sparse + rest_sparse
    sparse = sparse + swap(sparse, "dp", 1)
    small = jnp.stack([weight_squares[0], weight_squares[1], sparse])
    small = trade(jnp.broadcast_to(small[None], (size, 3, 8, 128)))
    terms = jnp.stack([cross, jnp.broadcast_to(sparse_coef, (1, 128))])

    dhidden = final_norm_back(dfinal)[0]
    dact = times_trans(dhidden.astype(low), proj_w)
    dup_low = gelu_back(dact)[0].astype(low)
    dnormed = times_trans(dup_low, fc_w)
    drecon = (dhidden + second_norm_back(dnormed)[0]).astype(low)

    drecon, small, terms = lax.optimization_barrier((drecon, small, terms))
    all_error = gather_copies(join(gather_near(drecon), 1))
    own, squares = gradients(core, all_tokens, all_error, all_feat, dec_low, pick_marks, idle)
    squares, own = lax.optimization_barrier((squares + swap(squares, "dp", 1), own))
    other = swap(own, "dp", 1)
    clip_norm = norm_of(pieces_of(squares))
    *directions, firsts, seconds, squares = moments(
        core,
        clip_norm,
        own,
        other,
        w_enc,
        enc_first,
        enc_second,
        w_dec,
        dec_first,
        dec_second,
    )
    weights, rows = renew(
        pieces_of(squares), small, terms, clip_norm, directions, w_enc, w_dec, total_picks
    )
    return weights, firsts, seconds, rows[4, 0], rows[5, 0], rows[:2, 0], rows[2:4, 0]


def solution(mesh):
    in_specs = (
        P(("dp", "fsdp"), None, None),
        P("dp", None),
        P("dp", None),
        P("dp", None),
        P(),
        P(),
        P(),
        P(),
        P(),
        P(),
        P(),
        P("fsdp", None),
        P("fsdp", None),
        P("fsdp", None),
        P("fsdp", None),
        P("fsdp"),
        P("fsdp", None),
        P("fsdp", None),
        P("fsdp", None),
        P(),
    )
    out_specs = (
        P(None, "fsdp", None),
        P(None, "fsdp", None),
        P(None, "fsdp", None),
        P(),
        P(),
        P(),
        P(),
    )
    return jax.shard_map(shards, mesh=mesh, in_specs=in_specs, out_specs=out_specs, check_vma=False)
```

```python
import jax
import jax.numpy as jnp
from jax import lax
from jax.experimental import pallas as pl
from jax.experimental.pallas import tpu as pltpu
from jax.sharding import PartitionSpec as P

HEADS = 12
HEAD_DIM = 64
F = 24576
STEP = 10


norm_eps = 1e-05
l1_scale = 40.0
clip_limit = 0.02
learn_rate = 0.3
beta_one = 0.9
beta_two = 0.999
adam_eps = 1e-08
weight_decay = 0.01


def layer_norm(values, gain, shift):
    center = values - jnp.mean(values, -1, keepdims=True)
    spread = jnp.mean(center * center, -1, keepdims=True)
    return center * lax.rsqrt(spread + norm_eps) * gain + shift


def times(left, right):
    return jnp.dot(left, right, preferred_element_type=jnp.float32)


def times_trans(left, right):
    return lax.dot_general(
        left, right, (((1,), (1,)), ((), ())), preferred_element_type=jnp.float32
    )


def trans_times(left, right):
    return lax.dot_general(
        left, right, (((0,), (0,)), ((), ())), preferred_element_type=jnp.float32
    )


def swap(block, axis, bit):
    size = lax.axis_size(axis)
    return lax.ppermute(block, axis, [(i, i ^ bit) for i in range(size)])


def trade(blocks):
    return lax.all_to_all(blocks, "fsdp", 0, 0, tiled=True)


def gather_group(block):
    size = lax.axis_size("fsdp")
    spread = jnp.broadcast_to(block[None], (size, *block.shape))
    return trade(spread).reshape(-1, *block.shape[1:])


def gather_near(block):
    half = lax.axis_size("fsdp") // 2
    far = swap(block, "fsdp", half)
    near = [block] + [swap(block, "fsdp", k) for k in range(1, half)]
    return near + [far] + [swap(far, "fsdp", k) for k in range(1, half)]


def pieces_of(block):
    size = lax.axis_size("fsdp")
    return [block] + [swap(block, "fsdp", k) for k in range(1, size)]


def paired(pieces):
    while len(pieces) > 1:
        pieces = [a + b for a, b in zip(pieces[::2], pieces[1::2])]
    return pieces[0]


def across(block):
    return swap(block, "dp", lax.axis_size("dp") // 2)


def spread(block):
    blocks = [block]
    bit = lax.axis_size("dp") // 4
    while bit:
        blocks = blocks + [swap(held, "dp", bit) for held in blocks]
        bit //= 2
    return blocks


def gather_copies(block):
    return spread(block) + spread(across(block))


VMEM = pl.BlockSpec(memory_space=pltpu.VMEM)
PLACED = pl.BlockSpec(memory_space=pl.ANY)
ONCE = pl.Buffered(1)


def in_vmem(values):
    return pltpu.with_memory_space_constraint(values, pltpu.VMEM)


def in_hbm(values):
    return pltpu.with_memory_space_constraint(values, pltpu.HBM)


def fold(values):
    rows, width = values.shape
    total = jnp.sum(values.reshape(rows // 8, 8, width), 0)
    return sum(total[:, k : k + 128] for k in range(0, width, 128))


def block_rows(count, most):
    return max(rows for rows in range(16, most + 1, 16) if count % rows == 0)


def scalars(grid, in_specs, out_specs, scratch_shapes=()):
    return pltpu.PrefetchScalarGridSpec(
        num_scalar_prefetch=1,
        grid=grid,
        in_specs=in_specs,
        out_specs=out_specs,
        scratch_shapes=scratch_shapes,
    )


def attention(resid, picks, gains, shifts, qkv_w, out_w, layer_bias, b_dec):
    count, length, width = resid.shape
    pick_count = picks.shape[1]
    rest_count = length - pick_count
    pair = 2 * HEAD_DIM

    def kernel(
        resid_ref, pick_ref, gain_ref, shift_ref, qkv_ref, out_ref, bias_ref, dec_ref, rows_ref, inputs_ref
    ):
        values = resid_ref[...].astype(jnp.float32).reshape(count * length, width)
        normed = layer_norm(values, gain_ref[:1, :], shift_ref[:1, :]).astype(jnp.bfloat16)
        packed = (times(normed, qkv_ref[...]) + bias_ref[:, : 3 * width]).astype(jnp.bfloat16)
        first = lax.broadcasted_iota(jnp.int32, (length, pair), 1) < HEAD_DIM
        row_ids = lax.broadcasted_iota(jnp.int32, (length, length), 0)
        col_ids = lax.broadcasted_iota(jnp.int32, (length, length), 1)
        causal = jnp.concatenate([row_ids >= col_ids] * 2, 0)
        contexts = []
        for s in range(count):
            at = slice(s * length, (s + 1) * length)
            pairs = []
            for lane in range(0, width, pair):
                query = packed[at, lane : lane + pair]
                key = packed[at, width + lane : width + lane + pair]
                value = packed[at, 2 * width + lane : 2 * width + lane + pair]
                zero = jnp.zeros_like(query)
                both = jnp.concatenate(
                    [jnp.where(first, query, zero), jnp.where(first, zero, query)], 0
                )
                scores = times_trans(both, key) * HEAD_DIM ** (-0.5)
                scores = jnp.where(causal, scores, -1e30)
                powers = jnp.exp(scores - jnp.max(scores, -1, keepdims=True))
                probs = (powers / jnp.sum(powers, -1, keepdims=True)).astype(jnp.bfloat16)
                mixed = times(probs, value)
                pairs.append(jnp.where(first, mixed[:length], mixed[length:]))
            contexts.append(jnp.concatenate(pairs, 1).astype(jnp.bfloat16))
        context = jnp.concatenate(contexts, 0)
        attn = times(context, out_ref[...]) + bias_ref[:, 3 * width : 4 * width]
        centered = (attn - dec_ref[...]).astype(jnp.bfloat16)
        after = (row_ids < col_ids).astype(jnp.float32)
        lanes = lax.broadcasted_iota(jnp.int32, (pick_count, length), 1)
        slots = lax.broadcasted_iota(jnp.int32, (rest_count, length), 0).astype(jnp.float32)
        for s in range(count):
            at = slice(s * length, (s + 1) * length)
            chosen = (pick_ref[s] == lanes).astype(jnp.float32)
            free = 1.0 - jnp.sum(chosen, 0, keepdims=True)
            rank = times(jnp.broadcast_to(free, (8, length)), after)[:1]
            others = jnp.where((rank == slots) & (free > 0), 1.0, 0.0).astype(jnp.bfloat16)
            chosen = chosen.astype(jnp.bfloat16)
            base = count * pick_count
            rows_ref[s * pick_count : (s + 1) * pick_count, :] = times(
                chosen, centered[at]
            ).astype(jnp.bfloat16)
            rows_ref[base + s * rest_count : base + (s + 1) * rest_count, :] = times(
                others, centered[at]
            ).astype(jnp.bfloat16)
            inputs_ref[s * pick_count : (s + 1) * pick_count, :] = times(chosen, resid_ref[s])

    return pl.pallas_call(
        kernel,
        in_specs=[VMEM] * 8,
        out_specs=[VMEM, VMEM],
        out_shape=[
            jax.ShapeDtypeStruct((count * length, width), jnp.bfloat16),
            jax.ShapeDtypeStruct((count * pick_count, width), jnp.float32),
        ],
        compiler_params=pltpu.CompilerParams(vmem_limit_bytes=32 << 20),
        cost_estimate=pl.CostEstimate(
            flops=8 * count * length * width * width,
            bytes_accessed=8 * width * width,
            transcendentals=count * length * width,
        ),
        name="attention",
    )(resid, picks[..., None], gains, shifts, qkv_w, out_w, layer_bias, b_dec)


def join(blocks, kinds):
    rows, width = blocks[0].shape
    part = rows // kinds
    count = len(blocks)

    def kernel(*refs):
        for kind in range(kinds):
            for k in range(count):
                refs[count + kind][k * part : (k + 1) * part, :] = refs[k][
                    kind * part : (kind + 1) * part, :
                ]

    return pl.pallas_call(
        kernel,
        in_specs=[VMEM] * count,
        out_specs=[VMEM] * kinds,
        out_shape=[jax.ShapeDtypeStruct((part * count, width), blocks[0].dtype)] * kinds,
        name="join",
    )(*blocks)


def encode(mine, tokens, count, part, w_enc, w_dec, b_enc):
    width = tokens.shape[1]
    feats = w_enc.shape[0]
    rows = block_rows(feats, 512)
    steps = feats // rows

    def kernel(mine_ref, token_ref, enc_ref, dec_ref, bias_ref, share_ref, square_ref, total_ref):

        @pl.when(pl.program_id(0) == 0)
        def _():
            square_ref[...] = jnp.zeros_like(square_ref)
            total_ref[...] = jnp.zeros_like(total_ref)

        enc, dec = enc_ref[...], dec_ref[...]
        square_ref[0] += fold(enc * enc)
        square_ref[1] += fold(dec * dec)
        enc_low, dec_low = enc.astype(jnp.bfloat16), dec.astype(jnp.bfloat16)
        features = jnp.maximum(times_trans(token_ref[...], enc_low) + bias_ref[...], 0.0)
        total_ref[...] += times(features.astype(jnp.bfloat16), dec_low)

        @pl.when(pl.program_id(0) == steps - 1)
        def _():
            for k in range(count):
                share_ref[mine_ref[0] ^ k] = total_ref[k * part : (k + 1) * part, :].astype(
                    jnp.bfloat16
                )

    whole = pl.BlockSpec((count * part, width), lambda i, s: (0, 0), pipeline_mode=ONCE)
    block = pl.BlockSpec((rows, width), lambda i, s: (i, 0))
    return pl.pallas_call(
        kernel,
        grid_spec=scalars(
            (steps,),
            [whole, block, block, pl.BlockSpec((1, rows), lambda i, s: (0, i))],
            [
                pl.BlockSpec((count, part, width), lambda i, s: (0, 0, 0)),
                pl.BlockSpec((2, 8, 128), lambda i, s: (0, 0, 0)),
            ],
            [pltpu.VMEM((count * part, width), jnp.float32)],
        ),
        out_shape=[
            jax.ShapeDtypeStruct((count, part, width), jnp.bfloat16),
            jax.ShapeDtypeStruct((2, 8, 128), jnp.float32),
        ],
        compiler_params=pltpu.CompilerParams(
            vmem_limit_bytes=(24 << 20) + 12 * count * part * width
        ),
        cost_estimate=pl.CostEstimate(
            flops=4 * feats * width * count * part, bytes_accessed=8 * feats * width, transcendentals=0
        ),
        name="encode",
    )(mine, in_hbm(tokens), in_hbm(w_enc), in_hbm(w_dec), b_enc)


def feature_rows(core, tokens, part, w_enc, bias, masks):
    count = len(tokens)
    width = tokens[0].shape[1]
    feats = w_enc.shape[0] // 2
    rows = block_rows(feats, 512 if part <= 512 else 128)
    steps = feats // rows

    def kernel(core_ref, *refs):
        token_refs = refs[:count]
        enc_ref, bias_ref, mask_ref, out_ref, sum_ref = refs[count:]

        @pl.when(pl.program_id(0) == 0)
        def _():
            sum_ref[...] = jnp.zeros_like(sum_ref)

        enc = enc_ref[...].astype(jnp.bfloat16)
        for k in range(count):
            at = pl.ds(k * part, part)
            pre = times_trans(enc, token_refs[k][...]) + bias_ref[...]
            kept = jnp.maximum(pre, 0.0)
            out_ref[:, at] = kept.astype(jnp.bfloat16)
            sum_ref[...] += fold(kept * mask_ref[:, at])

    whole = pl.BlockSpec((part, width), lambda i, s: (0, 0), pipeline_mode=ONCE)
    return pl.pallas_call(
        kernel,
        grid_spec=scalars(
            (steps,),
            [whole] * count
            + [
                pl.BlockSpec((rows, width), lambda i, s: (s[0] * steps + i, 0)),
                pl.BlockSpec((rows, 1), lambda i, s: (s[0] * steps + i, 0)),
                pl.BlockSpec((1, count * part), lambda i, s: (0, 0)),
            ],
            [
                pl.BlockSpec((rows, count * part), lambda i, s: (i, 0)),
                pl.BlockSpec((8, 128), lambda i, s: (0, 0)),
            ],
        ),
        out_shape=[
            pltpu.HBM((feats, count * part), jnp.bfloat16),
            jax.ShapeDtypeStruct((8, 128), jnp.float32),
        ],
        compiler_params=pltpu.CompilerParams(
            vmem_limit_bytes=(24 << 20) + 2 * count * part * width
        ),
        cost_estimate=pl.CostEstimate(
            flops=2 * feats * width * count * part,
            bytes_accessed=2 * (feats + width) * count * part + 2 * feats * width,
            transcendentals=0,
        ),
        name="features",
    )(core, *map(in_hbm, tokens), in_hbm(w_enc), bias, masks)


def idle_gradient(core, tokens, part, w_enc, bias, masks, marks):
    count = len(tokens)
    width = tokens[0].shape[1]
    feats = w_enc.shape[0] // 2
    rows = block_rows(feats, 512 if part <= 512 else 128)
    steps = feats // rows

    def kernel(core_ref, *refs):
        token_refs = refs[:count]
        enc_ref, bias_ref, mask_ref, mark_ref, out_ref, sum_ref = refs[count:]

        @pl.when(pl.program_id(0) == 0)
        def _():
            sum_ref[...] = jnp.zeros_like(sum_ref)

        grad = jnp.zeros(out_ref.shape, jnp.float32)
        enc = enc_ref[...].astype(jnp.bfloat16)
        for k in range(count):
            at = pl.ds(k * part, part)
            pre = times_trans(enc, token_refs[k][...]) + bias_ref[...]
            sum_ref[...] += fold(jnp.maximum(pre, 0.0) * mask_ref[:, at])
            dpre = jnp.where(pre > 0, mark_ref[:, at], 0.0).astype(jnp.bfloat16)
            grad = grad + times(dpre, token_refs[k][...])
        out_ref[...] = grad

    whole = pl.BlockSpec((part, width), lambda i, s: (0, 0), pipeline_mode=ONCE)
    row = pl.BlockSpec((1, count * part), lambda i, s: (0, 0))
    return pl.pallas_call(
        kernel,
        grid_spec=scalars(
            (steps,),
            [whole] * count
            + [
                pl.BlockSpec((rows, width), lambda i, s: (s[0] * steps + i, 0)),
                pl.BlockSpec((rows, 1), lambda i, s: (s[0] * steps + i, 0)),
                row,
                row,
            ],
            [
                pl.BlockSpec((rows, width), lambda i, s: (i, 0)),
                pl.BlockSpec((8, 128), lambda i, s: (0, 0)),
            ],
        ),
        out_shape=[
            pltpu.HBM((feats, width), jnp.float32),
            jax.ShapeDtypeStruct((8, 128), jnp.float32),
        ],
        compiler_params=pltpu.CompilerParams(
            vmem_limit_bytes=(24 << 20) + 2 * count * part * width
        ),
        cost_estimate=pl.CostEstimate(
            flops=4 * feats * width * count * part,
            bytes_accessed=2 * width * count * part + 6 * feats * width,
            transcendentals=0,
        ),
        name="idle",
    )(core, *map(in_hbm, tokens), in_hbm(w_enc), bias, masks, marks)


def gradients(core, tokens, errors, features, side, w_dec, marks, start):
    count = len(tokens)
    part, width = errors[0].shape
    feats = w_dec.shape[0] // 2
    rows = block_rows(feats, 256 if part <= 512 else 128)
    steps = feats // rows

    def kernel(core_ref, *refs):
        token_refs, error_refs = refs[:count], refs[count : 2 * count]
        feat_ref, dec_ref, mark_ref, start_ref, out_ref, *square_ref = refs[2 * count :]
        weight = dec_ref[...].astype(jnp.bfloat16)
        if side:
            enc, dec = start_ref[0], start_ref[1]
        else:
            enc, dec = start_ref[...], jnp.zeros((rows, width), jnp.float32)
        for k in range(count):
            at = pl.ds(k * part, part)
            feat = feat_ref[:, at]
            dfeat = times_trans(weight, error_refs[k][...]) + mark_ref[:, at]
            dpre = jnp.where(feat > 0, dfeat, 0.0).astype(jnp.bfloat16)
            enc = enc + times(dpre, token_refs[k][...])
            dec = dec + times(feat, error_refs[k][...])
        out_ref[0] = enc
        out_ref[1] = dec
        if side:

            @pl.when(pl.program_id(0) == 0)
            def _():
                square_ref[0][...] = jnp.zeros_like(square_ref[0])

            square_ref[0][...] += fold(enc * enc) + fold(dec * dec)

    whole = pl.BlockSpec((part, width), lambda i, s: (0, 0), pipeline_mode=ONCE)
    both = pl.BlockSpec((2, rows, width), lambda i, s: (0, i, 0))
    block = pl.BlockSpec((rows, width), lambda i, s: (i, 0))
    out_specs = [both] + [pl.BlockSpec((8, 128), lambda i, s: (0, 0))] * side
    out_shape = [pltpu.HBM((2, feats, width), jnp.float32)]
    out_shape = out_shape + [jax.ShapeDtypeStruct((8, 128), jnp.float32)] * side
    outs = pl.pallas_call(
        kernel,
        grid_spec=scalars(
            (steps,),
            [whole] * (2 * count)
            + [
                pl.BlockSpec((rows, count * part), lambda i, s: (i, side)),
                pl.BlockSpec((rows, width), lambda i, s: (s[0] * steps + i, 0)),
                pl.BlockSpec((1, count * part), lambda i, s: (0, side)),
                both if side else block,
            ],
            out_specs,
        ),
        out_shape=out_shape,
        compiler_params=pltpu.CompilerParams(
            vmem_limit_bytes=(18 << 20) + 4 * count * part * width
        ),
        cost_estimate=pl.CostEstimate(
            flops=6 * feats * width * count * part,
            bytes_accessed=(2 * feats + 4 * width) * count * part + 20 * feats * width,
            transcendentals=0,
        ),
        name="gradients",
    )(
        core,
        *map(in_hbm, tokens),
        *map(in_hbm, errors),
        in_hbm(features),
        in_hbm(w_dec),
        marks,
        in_hbm(start),
    )
    return outs if side else outs[0]


def norm_of(pieces):
    def kernel(*refs):
        total = jnp.sum(paired([ref[...] for ref in refs[:-1]]), keepdims=True).reshape(1, 1)
        refs[-1][...] = jnp.broadcast_to(jnp.sqrt(total), refs[-1].shape)

    return pl.pallas_call(
        kernel,
        in_specs=[VMEM] * len(pieces),
        out_specs=VMEM,
        out_shape=jax.ShapeDtypeStruct((8, 128), jnp.float32),
        compiler_params=pltpu.CompilerParams(vmem_limit_bytes=1 << 20),
        name="norm",
    )(*pieces)


def moments(
    core, clip_norm, own, other, w_enc, enc_first, enc_second, w_dec, dec_first, dec_second
):
    feats, width = w_enc.shape
    rows = block_rows(feats // 2, 192)
    half = feats // 2 // rows
    steps = 2 * half

    def kernel(core_ref, norm_ref, own_ref, other_ref, *refs):
        enc, dec, outs = refs[:3], refs[3:6], refs[6:]
        dir_refs, (first_out, second_out, square_ref) = outs[:2], outs[2:]
        factor = clip_limit / jnp.maximum(norm_ref[:1, :1], clip_limit)
        square_ref[...] = jnp.zeros_like(square_ref)
        start = core_ref[0] * half

        def place(i):
            return lax.rem(start + i, steps)

        def body(own, other, enc_first, enc_second, dec_first, dec_second, first_ref, second_ref):
            step = pl.program_id(0)
            at = pl.ds(pl.multiple_of(place(step) * rows, rows), rows)
            sides = ((enc[0], enc_first, enc_second), (dec[0], dec_first, dec_second))
            for plane, (weight, first, second) in enumerate(sides):
                clipped = jnp.where(step < half, own[plane], other[plane]) * factor
                first_new = beta_one * first[...] + (1.0 - beta_one) * clipped
                second_new = beta_two * second[...] + (1.0 - beta_two) * clipped * clipped
                first_ref[plane] = first_new
                second_ref[plane] = second_new
                scaled = second_new * (1.0 / (1.0 - beta_two**STEP))
                spread = scaled * lax.rsqrt(scaled) + adam_eps
                direction = (
                    first_new * (1.0 / (1.0 - beta_one**STEP)) * pltpu.reciprocal(spread)
                    + weight_decay * weight[at, :]
                )
                dir_refs[plane][at, :] = direction
                square_ref[plane] += fold(direction * direction)

        block = pl.BlockSpec((rows, width), lambda i: (place(i), 0))
        both = pl.BlockSpec((2, rows, width), lambda i: (0, place(i), 0))
        early = pl.BlockSpec((2, rows, width), lambda i: (0, jnp.minimum(i, half - 1), 0))
        late = pl.BlockSpec((2, rows, width), lambda i: (0, jnp.maximum(i - half, 0), 0))
        pltpu.emit_pipeline(
            body,
            grid=(steps,),
            in_specs=[early, late] + [block] * 4,
            out_specs=[both, both],
        )(own_ref, other_ref, enc[1], enc[2], dec[1], dec[2], first_out, second_out)

    full = (2, feats, width)
    return pl.pallas_call(
        kernel,
        in_specs=[pl.BlockSpec(memory_space=pltpu.SMEM), VMEM, PLACED, PLACED]
        + [VMEM, PLACED, PLACED] * 2,
        out_specs=[VMEM, VMEM, PLACED, PLACED, VMEM],
        out_shape=[
            pltpu.VMEM((feats, width), jnp.float32),
            pltpu.VMEM((feats, width), jnp.float32),
            pltpu.HBM(full, jnp.float32),
            pltpu.HBM(full, jnp.float32),
            jax.ShapeDtypeStruct((2, 8, 128), jnp.float32),
        ],
        compiler_params=pltpu.CompilerParams(vmem_limit_bytes=16 << 20),
        cost_estimate=pl.CostEstimate(
            flops=40 * feats * width,
            bytes_accessed=40 * feats * width,
            transcendentals=4 * feats * width,
        ),
        name="moments",
    )(
        core,
        clip_norm,
        in_hbm(own),
        in_hbm(other),
        in_vmem(w_enc),
        in_hbm(enc_first),
        in_hbm(enc_second),
        in_vmem(w_dec),
        in_hbm(dec_first),
        in_hbm(dec_second),
    )


def renew(sums, small, terms, clip_norm, directions, w_enc, w_dec, total_picks):
    feats, width = w_enc.shape
    rows = block_rows(feats, 256)

    count = len(sums)

    def kernel(*refs):
        sum_refs = refs[:count]
        small_ref, term_ref, clip_ref, enc_dir, dec_dir, enc_ref, dec_ref, out_ref, row_ref = refs[count:]
        sums = paired([ref[...] for ref in sum_refs])
        def total(values):
            return jnp.sum(values, keepdims=True).reshape(1, 1)

        norms = [jnp.sqrt(total(small_ref[:, plane])) for plane in range(2)]
        steps = [jnp.sqrt(total(sums[plane])) for plane in range(2)]
        rates = [learn_rate * (norms[plane] / steps[plane]) for plane in range(2)]
        loss = term_ref[0, :1, :1] / total_picks + term_ref[1, :1, :1] * total(small_ref[:, 2])
        for i, value in enumerate((*norms, *steps, loss, clip_ref[:1, :1])):
            row_ref[i : i + 1, :] = jnp.broadcast_to(value, (1, 128))
        row_ref[6:, :] = jnp.zeros((2, 128), jnp.float32)

        def body(enc_w, dec_w, new_ref):
            at = pl.ds(pl.multiple_of(pl.program_id(0) * rows, rows), rows)
            new_ref[0] = enc_w[...] - rates[0] * enc_dir[at, :]
            raw = dec_w[...] - rates[1] * dec_dir[at, :]
            new_ref[1] = raw * lax.rsqrt(jnp.sum(raw * raw, 1, keepdims=True) + 1e-06)

        both = pl.BlockSpec((2, rows, width), lambda i: (0, i, 0))
        block = pl.BlockSpec((rows, width), lambda i: (i, 0))
        pltpu.emit_pipeline(
            body, grid=(feats // rows,), in_specs=[block, block], out_specs=[both]
        )(enc_ref, dec_ref, out_ref)

    return pl.pallas_call(
        kernel,
        in_specs=[VMEM] * (count + 5) + [PLACED] * 2,
        out_specs=[PLACED, VMEM],
        out_shape=[
            pltpu.HBM((2, feats, width), jnp.float32),
            jax.ShapeDtypeStruct((8, 128), jnp.float32),
        ],
        compiler_params=pltpu.CompilerParams(vmem_limit_bytes=16 << 20),
        cost_estimate=pl.CostEstimate(
            flops=12 * w_enc.size, bytes_accessed=8 * w_enc.size, transcendentals=0
        ),
        name="renew",
    )(*sums, small, terms, clip_norm, *map(in_vmem, directions), in_hbm(w_enc), in_hbm(w_dec))


def shards(
    resid_pre,
    token_ids,
    valid_mask,
    picked,
    norm_gains,
    norm_biases,
    qkv_w,
    out_w,
    fc_w,
    proj_w,
    layer_bias,
    wte,
    w_enc,
    enc_first,
    enc_second,
    b_enc,
    w_dec,
    dec_first,
    dec_second,
    b_dec,
):
    low = jnp.bfloat16
    count, seq_len, model_width = resid_pre.shape
    size = lax.axis_size("fsdp")
    mine = lax.axis_index("fsdp")
    pick_count = picked.shape[1]
    rest_count = seq_len - pick_count
    hidden_units = fc_w.shape[1]
    vocab_rows = wte.shape[0]
    total_picks = lax.axis_size("dp") * size * count * pick_count
    fc_b = layer_bias[4 * model_width : 4 * model_width + hidden_units]
    proj_b = layer_bias[4 * model_width + hidden_units :]

    place = lax.broadcasted_iota(jnp.int32, (1, 1, 1, seq_len), 3)
    before = lax.broadcasted_iota(jnp.int32, (seq_len, seq_len), 0) > lax.broadcasted_iota(
        jnp.int32, (seq_len, seq_len), 1
    )
    slot = lax.broadcasted_iota(jnp.int32, (1, 1, rest_count, 1), 2)

    def selectors(picks):
        chosen = picks[..., None] == place
        free = jnp.logical_not(jnp.any(chosen, 2))
        rank = jnp.sum(jnp.where(before & free[:, :, None, :], 1, 0), -1)
        return chosen, (rank[:, :, None, :] == slot) & free[:, :, None, :]

    grouped_picks = picked.reshape(size, count, pick_count)
    own_rows, own_inputs = attention(
        resid_pre,
        lax.dynamic_index_in_dim(grouped_picks, mine, 0, keepdims=False),
        norm_gains,
        norm_biases,
        qkv_w,
        out_w,
        layer_bias.reshape(1, -1),
        b_dec.reshape(1, -1),
    )
    own_count = own_inputs.shape[0]

    tokens, rest = join(gather_near(own_rows), 2)
    group_rows = size * own_count
    me = mine.reshape(1).astype(jnp.int32)
    core = (lax.axis_index("dp") & 1).reshape(1).astype(jnp.int32)
    all_pick = gather_copies(tokens)
    shares, weight_squares = encode(
        me, tokens, size, own_count, w_enc, w_dec, b_enc.reshape(1, -1)
    )
    shares, token_ids, valid_mask, grouped_picks = lax.optimization_barrier(
        (shares, token_ids, valid_mask, grouped_picks)
    )
    recon = jnp.sum(trade(shares).astype(jnp.float32), 0) + b_dec

    ids = token_ids.reshape(size, count, seq_len)
    mask = valid_mask.reshape(size, count, seq_len).astype(jnp.float32)
    chosen, others = selectors(grouped_picks)
    targets = jnp.sum(
        jnp.where(grouped_picks[..., None] + 1 == place, ids[:, :, None, :], 0), -1
    ).reshape(-1)
    targets = targets - mine * vocab_rows
    here = (targets >= 0) & (targets < vocab_rows)
    target_rows = jnp.take(wte, jnp.clip(targets, 0, vocab_rows - 1), axis=0)
    target_rows = jnp.where(here[:, None], target_rows, jnp.zeros_like(target_rows))
    order = jnp.arange(size) ^ mine
    pick_mask = jnp.sum(jnp.where(chosen, mask[:, :, None, :], 0.0), -1)[order].reshape(1, -1)
    rest_mask = jnp.sum(jnp.where(others, mask[:, :, None, :], 0.0), -1)[order].reshape(1, -1)
    masks = gather_copies(jnp.concatenate([pick_mask, rest_mask], 1))
    half = pick_mask.shape[1]
    pick_mask = jnp.concatenate([held[:, :half] for held in masks], 1)
    rest_mask = jnp.concatenate([held[:, half:] for held in masks], 1)
    sparse_coef = l1_scale / F / (jnp.sum(pick_mask) + jnp.sum(rest_mask))
    pick_marks, rest_marks = sparse_coef * pick_mask, sparse_coef * rest_mask
    bias = b_enc.reshape(-1, 1)
    recon, target_rows, pick_marks, rest_marks, rest = lax.optimization_barrier(
        (recon, target_rows, pick_marks, rest_marks, rest)
    )
    far_rest = across(rest)

    mid = own_inputs + recon
    normed, second_norm_back = jax.vjp(
        lambda values: layer_norm(values, norm_gains[1], norm_biases[1]), mid
    )
    up_val = times(normed.astype(low), fc_w) + fc_b
    act, gelu_back = jax.vjp(lambda values: jax.nn.gelu(values, approximate=True), up_val)
    hidden = mid + times(act.astype(low), proj_w) + proj_b
    final, final_norm_back = jax.vjp(
        lambda values: layer_norm(values, norm_gains[2], norm_biases[2]), hidden
    )
    finals = gather_group(final.astype(low))
    all_feat, pick_sparse = feature_rows(
        core, all_pick, group_rows, w_enc, bias, pick_mask
    )
    far_rest, all_feat = lax.optimization_barrier((far_rest, all_feat))
    finals, all_feat, far_rest = lax.optimization_barrier((finals, all_feat, far_rest))
    all_rest = spread(rest) + spread(far_rest)

    logits = times_trans(finals, wte)
    top = jnp.max(logits, 1)
    parts = jnp.exp(logits - top[:, None])
    mass = jnp.sum(parts, 1)
    at = jnp.sum(finals.astype(jnp.float32) * target_rows.astype(jnp.float32), 1)
    stats = trade(jnp.broadcast_to(jnp.stack([top, mass, at])[None], (size, 3, top.shape[0])))
    mixed = times(parts.astype(low), wte)
    stats, mixed = lax.optimization_barrier((stats, mixed))
    best = jnp.max(stats[:, 0], 0)
    total = jnp.sum(stats[:, 1] * jnp.exp(stats[:, 0] - best), 0)
    cross = jnp.sum(best + jnp.log(total) - jnp.sum(stats[:, 2], 0))
    scale = jnp.exp(top - best) / total
    dshares = (mixed * scale[:, None] - target_rows.astype(jnp.float32)) / total_picks
    dshares = dshares.astype(low).reshape(size, -1, model_width)
    cross = jnp.broadcast_to(cross, (1, 128))
    dshares, idle_marks, cross = lax.optimization_barrier((dshares, rest_marks, cross))
    bit = lax.axis_size("dp") // 2
    while bit:
        cross = cross + swap(cross, "dp", bit)
        bit //= 2
    dfinal = jnp.sum(trade(dshares).astype(jnp.float32), 0)
    idle, rest_sparse = idle_gradient(
        core, all_rest, group_rows, w_enc, bias, rest_mask, idle_marks
    )
    dfinal, idle, pick_sparse, cross = lax.optimization_barrier((dfinal, idle, pick_sparse, cross))

    dhidden = final_norm_back(dfinal)[0]
    dact = times_trans(dhidden.astype(low), proj_w)
    dup_low = gelu_back(dact)[0].astype(low)
    dnormed = times_trans(dup_low, fc_w)
    drecon = (dhidden + second_norm_back(dnormed)[0]).astype(low)

    (errors,) = join(gather_near(drecon), 1)
    errors, pick_sparse = lax.optimization_barrier((errors, pick_sparse))
    sparse = pick_sparse + rest_sparse
    sparse = sparse + swap(sparse, "dp", 1)
    small = jnp.stack([weight_squares[0], weight_squares[1], sparse])
    small = trade(jnp.broadcast_to(small[None], (size, 3, 8, 128)))
    terms = jnp.stack([cross, jnp.broadcast_to(sparse_coef, (1, 128))])
    far_errors = across(errors)
    middle = len(all_pick) // 2
    near = gradients(
        core, all_pick[:middle], spread(errors), all_feat, 0, w_dec, pick_marks, idle
    )
    near, far_errors, small, terms = lax.optimization_barrier((near, far_errors, small, terms))
    own, squares = gradients(
        core, all_pick[middle:], spread(far_errors), all_feat, 1, w_dec, pick_marks, near
    )
    squares, own = lax.optimization_barrier((squares + swap(squares, "dp", 1), own))
    other = swap(own, "dp", 1)
    clip_norm = norm_of(pieces_of(squares))
    *directions, firsts, seconds, squares = moments(
        core,
        clip_norm,
        own,
        other,
        w_enc,
        enc_first,
        enc_second,
        w_dec,
        dec_first,
        dec_second,
    )
    weights, rows = renew(
        pieces_of(squares), small, terms, clip_norm, directions, w_enc, w_dec, total_picks
    )
    return weights, firsts, seconds, rows[4, 0], rows[5, 0], rows[:2, 0], rows[2:4, 0]


def solution(mesh):
    in_specs = (
        P(("dp", "fsdp"), None, None),
        P("dp", None),
        P("dp", None),
        P("dp", None),
        P(),
        P(),
        P(),
        P(),
        P(),
        P(),
        P(),
        P("fsdp", None),
        P("fsdp", None),
        P("fsdp", None),
        P("fsdp", None),
        P("fsdp"),
        P("fsdp", None),
        P("fsdp", None),
        P("fsdp", None),
        P(),
    )
    out_specs = (
        P(None, "fsdp", None),
        P(None, "fsdp", None),
        P(None, "fsdp", None),
        P(),
        P(),
        P(),
        P(),
    )
    return jax.shard_map(shards, mesh=mesh, in_specs=in_specs, out_specs=out_specs, check_vma=False)
```

```python
import jax
import jax.numpy as jnp
from jax import lax
from jax.experimental import pallas as pl
from jax.experimental.pallas import tpu as pltpu
from jax.sharding import PartitionSpec as P

HEADS = 12
HEAD_DIM = 64
F = 24576
STEP = 10


norm_eps = 1e-05
l1_scale = 40.0
clip_limit = 0.02
learn_rate = 0.3
beta_one = 0.9
beta_two = 0.999
adam_eps = 1e-08
weight_decay = 0.01


def layer_norm(values, gain, shift):
    center = values - jnp.mean(values, -1, keepdims=True)
    spread = jnp.mean(center * center, -1, keepdims=True)
    return center * lax.rsqrt(spread + norm_eps) * gain + shift


def times(left, right):
    return jnp.dot(left, right, preferred_element_type=jnp.float32)


def times_trans(left, right):
    return lax.dot_general(
        left, right, (((1,), (1,)), ((), ())), preferred_element_type=jnp.float32
    )


def trans_times(left, right):
    return lax.dot_general(
        left, right, (((0,), (0,)), ((), ())), preferred_element_type=jnp.float32
    )


def swap(block, axis, bit):
    size = lax.axis_size(axis)
    return lax.ppermute(block, axis, [(i, i ^ bit) for i in range(size)])


def trade(blocks):
    return lax.all_to_all(blocks, "fsdp", 0, 0, tiled=True)


def gather_group(block):
    size = lax.axis_size("fsdp")
    spread = jnp.broadcast_to(block[None], (size, *block.shape))
    return trade(spread).reshape(-1, *block.shape[1:])


def gather_near(block):
    half = lax.axis_size("fsdp") // 2
    far = swap(block, "fsdp", half)
    near = [block] + [swap(block, "fsdp", k) for k in range(1, half)]
    return near + [far] + [swap(far, "fsdp", k) for k in range(1, half)]


def pieces_of(block):
    size = lax.axis_size("fsdp")
    return [block] + [swap(block, "fsdp", k) for k in range(1, size)]


def paired(pieces):
    while len(pieces) > 1:
        pieces = [a + b for a, b in zip(pieces[::2], pieces[1::2])]
    return pieces[0]


def across(block):
    return swap(block, "dp", lax.axis_size("dp") // 2)


def spread(block):
    blocks = [block]
    bit = lax.axis_size("dp") // 4
    while bit:
        blocks = blocks + [swap(held, "dp", bit) for held in blocks]
        bit //= 2
    return blocks


def gather_copies(block):
    return spread(block) + spread(across(block))


VMEM = pl.BlockSpec(memory_space=pltpu.VMEM)
PLACED = pl.BlockSpec(memory_space=pl.ANY)
ONCE = pl.Buffered(1)


def in_vmem(values):
    return pltpu.with_memory_space_constraint(values, pltpu.VMEM)


def in_hbm(values):
    return pltpu.with_memory_space_constraint(values, pltpu.HBM)


def fold(values):
    rows, width = values.shape
    total = jnp.sum(values.reshape(rows // 8, 8, width), 0)
    return sum(total[:, k : k + 128] for k in range(0, width, 128))


def block_rows(count, most):
    return max(rows for rows in range(16, most + 1, 16) if count % rows == 0)


def scalars(grid, in_specs, out_specs, scratch_shapes=()):
    return pltpu.PrefetchScalarGridSpec(
        num_scalar_prefetch=1,
        grid=grid,
        in_specs=in_specs,
        out_specs=out_specs,
        scratch_shapes=scratch_shapes,
    )


def attention(resid, picks, gains, shifts, qkv_w, out_w, layer_bias, b_dec):
    count, length, width = resid.shape
    pick_count = picks.shape[1]
    rest_count = length - pick_count
    pair = 2 * HEAD_DIM

    def kernel(
        resid_ref,
        pick_ref,
        gain_ref,
        shift_ref,
        qkv_ref,
        out_ref,
        bias_ref,
        dec_ref,
        rows_ref,
        rest_ref,
        inputs_ref,
    ):
        values = resid_ref[...].astype(jnp.float32).reshape(count * length, width)
        normed = layer_norm(values, gain_ref[:1, :], shift_ref[:1, :]).astype(jnp.bfloat16)
        packed = (times(normed, qkv_ref[...]) + bias_ref[:, : 3 * width]).astype(jnp.bfloat16)
        first = lax.broadcasted_iota(jnp.int32, (length, pair), 1) < HEAD_DIM
        row_ids = lax.broadcasted_iota(jnp.int32, (length, length), 0)
        col_ids = lax.broadcasted_iota(jnp.int32, (length, length), 1)
        causal = jnp.concatenate([row_ids >= col_ids] * 2, 0)
        contexts = []
        for s in range(count):
            at = slice(s * length, (s + 1) * length)
            pairs = []
            for lane in range(0, width, pair):
                query = packed[at, lane : lane + pair]
                key = packed[at, width + lane : width + lane + pair]
                value = packed[at, 2 * width + lane : 2 * width + lane + pair]
                zero = jnp.zeros_like(query)
                both = jnp.concatenate(
                    [jnp.where(first, query, zero), jnp.where(first, zero, query)], 0
                )
                scores = times_trans(both, key) * HEAD_DIM ** (-0.5)
                scores = jnp.where(causal, scores, -1e30)
                powers = jnp.exp(scores - jnp.max(scores, -1, keepdims=True))
                probs = (powers / jnp.sum(powers, -1, keepdims=True)).astype(jnp.bfloat16)
                mixed = times(probs, value)
                pairs.append(jnp.where(first, mixed[:length], mixed[length:]))
            contexts.append(jnp.concatenate(pairs, 1).astype(jnp.bfloat16))
        context = jnp.concatenate(contexts, 0)
        attn = times(context, out_ref[...]) + bias_ref[:, 3 * width : 4 * width]
        centered = (attn - dec_ref[...]).astype(jnp.bfloat16)
        after = (row_ids < col_ids).astype(jnp.float32)
        lanes = lax.broadcasted_iota(jnp.int32, (pick_count, length), 1)
        slots = lax.broadcasted_iota(jnp.int32, (rest_count, length), 0).astype(jnp.float32)
        for s in range(count):
            at = slice(s * length, (s + 1) * length)
            chosen = (pick_ref[s] == lanes).astype(jnp.float32)
            free = 1.0 - jnp.sum(chosen, 0, keepdims=True)
            rank = times(jnp.broadcast_to(free, (8, length)), after)[:1]
            others = jnp.where((rank == slots) & (free > 0), 1.0, 0.0).astype(jnp.bfloat16)
            chosen = chosen.astype(jnp.bfloat16)
            rows_ref[s * pick_count : (s + 1) * pick_count, :] = times(
                chosen, centered[at]
            ).astype(jnp.bfloat16)
            rest_ref[s * rest_count : (s + 1) * rest_count, :] = times(
                others, centered[at]
            ).astype(jnp.bfloat16)
            inputs_ref[s * pick_count : (s + 1) * pick_count, :] = times(chosen, resid_ref[s])

    return pl.pallas_call(
        kernel,
        in_specs=[VMEM] * 8,
        out_specs=[VMEM, VMEM, VMEM],
        out_shape=[
            jax.ShapeDtypeStruct((count * pick_count, width), jnp.bfloat16),
            jax.ShapeDtypeStruct((count * rest_count, width), jnp.bfloat16),
            jax.ShapeDtypeStruct((count * pick_count, width), jnp.float32),
        ],
        compiler_params=pltpu.CompilerParams(vmem_limit_bytes=32 << 20),
        cost_estimate=pl.CostEstimate(
            flops=8 * count * length * width * width,
            bytes_accessed=8 * width * width,
            transcendentals=count * length * width,
        ),
        name="attention",
    )(resid, picks[..., None], gains, shifts, qkv_w, out_w, layer_bias, b_dec)


def join(blocks):
    part, width = blocks[0].shape
    count = len(blocks)

    def kernel(*refs):
        for k in range(count):
            refs[count][k * part : (k + 1) * part, :] = refs[k][...]

    return pl.pallas_call(
        kernel,
        in_specs=[VMEM] * count,
        out_specs=VMEM,
        out_shape=jax.ShapeDtypeStruct((part * count, width), blocks[0].dtype),
        name="join",
    )(*blocks)


def mask_rows(mine, size, picked, valid_mask):
    count, pick_count = picked.shape
    length = valid_mask.shape[1]
    lanes = count * pick_count
    block = lanes // size

    def kernel(mine_ref, pick_ref, mask_ref, out_ref):
        def one(test):
            return jnp.where(test, 1.0, 0.0).astype(jnp.bfloat16)

        def ids(shape, dim):
            return lax.broadcasted_iota(jnp.int32, shape, dim)

        wide, square = (length, lanes), (lanes, lanes)
        chosen = one(pick_ref[...] == ids(wide, 0))
        group = one(ids(square, 0) // pick_count == ids(square, 1) // pick_count)
        free = 1.0 - times(chosen, group)
        before = one(ids((length, length), 0) > ids((length, length), 1))
        rank = times(before, free.astype(jnp.bfloat16))
        slot = lax.rem(ids(wide, 1), pick_count).astype(jnp.float32)
        others = jnp.where((rank == slot) & (free > 0), 1.0, 0.0)
        owner = one(ids((count, lanes), 0) == ids((count, lanes), 1) // pick_count)
        mask = trans_times(mask_ref[...].astype(jnp.bfloat16), owner)
        picks = jnp.sum(chosen.astype(jnp.float32) * mask, 0, keepdims=True)
        source, target = ids(square, 0), ids(square, 1)
        moved = one(
            (source // block == ((target // block) ^ mine_ref[0]))
            & (lax.rem(source, block) == lax.rem(target, block))
        )
        out_ref[:1, :] = times(picks.astype(jnp.bfloat16), moved)
        out_ref[1:, :] = jnp.sum(others * mask, 0, keepdims=True)

    return pl.pallas_call(
        kernel,
        in_specs=[pl.BlockSpec(memory_space=pltpu.SMEM), VMEM, VMEM],
        out_specs=VMEM,
        out_shape=jax.ShapeDtypeStruct((2, lanes), jnp.float32),
        compiler_params=pltpu.CompilerParams(vmem_limit_bytes=(8 << 20) + 12 * lanes * lanes),
        name="masks",
    )(mine, picked.reshape(1, -1), valid_mask)


def mark_rows(masks):
    count = len(masks)
    lanes = masks[0].shape[1]

    def kernel(*refs):
        pick_ref, rest_ref, pick_marks, rest_marks, coef_ref = refs[count:]
        total = sum(jnp.sum(ref[...], keepdims=True).reshape(1, 1) for ref in refs[:count])
        coef = l1_scale / F / total
        coef_ref[...] = jnp.broadcast_to(coef, (1, 128))
        for k in range(count):
            at = slice(k * lanes, (k + 1) * lanes)
            pick_ref[:, at] = refs[k][:1, :]
            rest_ref[:, at] = refs[k][1:, :]
            pick_marks[:, at] = refs[k][:1, :] * coef
            rest_marks[:, at] = refs[k][1:, :] * coef

    return pl.pallas_call(
        kernel,
        in_specs=[VMEM] * count,
        out_specs=[VMEM] * 5,
        out_shape=[jax.ShapeDtypeStruct((1, count * lanes), jnp.float32)] * 4
        + [jax.ShapeDtypeStruct((1, 128), jnp.float32)],
        name="marks",
    )(*masks)


def encode(mine, tokens, count, part, w_enc, w_dec, b_enc):
    width = tokens.shape[1]
    feats = w_enc.shape[0]
    rows = block_rows(feats, 512)
    steps = feats // rows

    def kernel(mine_ref, token_ref, enc_ref, dec_ref, bias_ref, share_ref, square_ref, total_ref):

        @pl.when(pl.program_id(0) == 0)
        def _():
            square_ref[...] = jnp.zeros_like(square_ref)
            total_ref[...] = jnp.zeros_like(total_ref)

        enc, dec = enc_ref[...], dec_ref[...]
        square_ref[0] += fold(enc * enc)
        square_ref[1] += fold(dec * dec)
        enc_low, dec_low = enc.astype(jnp.bfloat16), dec.astype(jnp.bfloat16)
        features = jnp.maximum(times_trans(token_ref[...], enc_low) + bias_ref[...], 0.0)
        total_ref[...] += times(features.astype(jnp.bfloat16), dec_low)

        @pl.when(pl.program_id(0) == steps - 1)
        def _():
            for k in range(count):
                share_ref[mine_ref[0] ^ k] = total_ref[k * part : (k + 1) * part, :].astype(
                    jnp.bfloat16
                )

    whole = pl.BlockSpec((count * part, width), lambda i, s: (0, 0), pipeline_mode=ONCE)
    block = pl.BlockSpec((rows, width), lambda i, s: (i, 0))
    return pl.pallas_call(
        kernel,
        grid_spec=scalars(
            (steps,),
            [whole, block, block, pl.BlockSpec((1, rows), lambda i, s: (0, i))],
            [
                pl.BlockSpec((count, part, width), lambda i, s: (0, 0, 0)),
                pl.BlockSpec((2, 8, 128), lambda i, s: (0, 0, 0)),
            ],
            [pltpu.VMEM((count * part, width), jnp.float32)],
        ),
        out_shape=[
            jax.ShapeDtypeStruct((count, part, width), jnp.bfloat16),
            jax.ShapeDtypeStruct((2, 8, 128), jnp.float32),
        ],
        compiler_params=pltpu.CompilerParams(
            vmem_limit_bytes=(24 << 20) + 12 * count * part * width
        ),
        cost_estimate=pl.CostEstimate(
            flops=4 * feats * width * count * part, bytes_accessed=8 * feats * width, transcendentals=0
        ),
        name="encode",
    )(mine, in_hbm(tokens), in_hbm(w_enc), in_hbm(w_dec), b_enc)


def feature_rows(core, tokens, part, w_enc, bias, masks):
    count = len(tokens)
    width = tokens[0].shape[1]
    feats = w_enc.shape[0] // 2
    rows = block_rows(feats, 512 if part <= 512 else 128)
    steps = feats // rows

    def kernel(core_ref, *refs):
        token_refs = refs[:count]
        enc_ref, bias_ref, mask_ref, out_ref, sum_ref = refs[count:]

        @pl.when(pl.program_id(0) == 0)
        def _():
            sum_ref[...] = jnp.zeros_like(sum_ref)

        enc = enc_ref[...].astype(jnp.bfloat16)
        for k in range(count):
            at = pl.ds(k * part, part)
            pre = times_trans(enc, token_refs[k][...]) + bias_ref[...]
            kept = jnp.maximum(pre, 0.0)
            out_ref[:, at] = kept.astype(jnp.bfloat16)
            sum_ref[...] += fold(kept * mask_ref[:, at])

    whole = pl.BlockSpec((part, width), lambda i, s: (0, 0), pipeline_mode=ONCE)
    return pl.pallas_call(
        kernel,
        grid_spec=scalars(
            (steps,),
            [whole] * count
            + [
                pl.BlockSpec((rows, width), lambda i, s: (s[0] * steps + i, 0)),
                pl.BlockSpec((rows, 1), lambda i, s: (s[0] * steps + i, 0)),
                pl.BlockSpec((1, count * part), lambda i, s: (0, 0)),
            ],
            [
                pl.BlockSpec((rows, count * part), lambda i, s: (i, 0)),
                pl.BlockSpec((8, 128), lambda i, s: (0, 0)),
            ],
        ),
        out_shape=[
            pltpu.HBM((feats, count * part), jnp.bfloat16),
            jax.ShapeDtypeStruct((8, 128), jnp.float32),
        ],
        compiler_params=pltpu.CompilerParams(
            vmem_limit_bytes=(24 << 20) + 2 * count * part * width
        ),
        cost_estimate=pl.CostEstimate(
            flops=2 * feats * width * count * part,
            bytes_accessed=2 * (feats + width) * count * part + 2 * feats * width,
            transcendentals=0,
        ),
        name="features",
    )(core, *map(in_hbm, tokens), in_hbm(w_enc), bias, masks)


def idle_gradient(core, tokens, part, w_enc, bias, masks, marks):
    count = len(tokens)
    width = tokens[0].shape[1]
    feats = w_enc.shape[0] // 2
    rows = block_rows(feats, 512 if part <= 512 else 128)
    steps = feats // rows

    def kernel(core_ref, *refs):
        token_refs = refs[:count]
        enc_ref, bias_ref, mask_ref, mark_ref, out_ref, sum_ref = refs[count:]

        @pl.when(pl.program_id(0) == 0)
        def _():
            sum_ref[...] = jnp.zeros_like(sum_ref)

        grad = jnp.zeros(out_ref.shape, jnp.float32)
        enc = enc_ref[...].astype(jnp.bfloat16)
        for k in range(count):
            at = pl.ds(k * part, part)
            pre = times_trans(enc, token_refs[k][...]) + bias_ref[...]
            sum_ref[...] += fold(jnp.maximum(pre, 0.0) * mask_ref[:, at])
            dpre = jnp.where(pre > 0, mark_ref[:, at], 0.0).astype(jnp.bfloat16)
            grad = grad + times(dpre, token_refs[k][...])
        out_ref[...] = grad

    whole = pl.BlockSpec((part, width), lambda i, s: (0, 0), pipeline_mode=ONCE)
    row = pl.BlockSpec((1, count * part), lambda i, s: (0, 0))
    return pl.pallas_call(
        kernel,
        grid_spec=scalars(
            (steps,),
            [whole] * count
            + [
                pl.BlockSpec((rows, width), lambda i, s: (s[0] * steps + i, 0)),
                pl.BlockSpec((rows, 1), lambda i, s: (s[0] * steps + i, 0)),
                row,
                row,
            ],
            [
                pl.BlockSpec((rows, width), lambda i, s: (i, 0)),
                pl.BlockSpec((8, 128), lambda i, s: (0, 0)),
            ],
        ),
        out_shape=[
            pltpu.HBM((feats, width), jnp.float32),
            jax.ShapeDtypeStruct((8, 128), jnp.float32),
        ],
        compiler_params=pltpu.CompilerParams(
            vmem_limit_bytes=(24 << 20) + 2 * count * part * width
        ),
        cost_estimate=pl.CostEstimate(
            flops=4 * feats * width * count * part,
            bytes_accessed=2 * width * count * part + 6 * feats * width,
            transcendentals=0,
        ),
        name="idle",
    )(core, *map(in_hbm, tokens), in_hbm(w_enc), bias, masks, marks)


def gradients(core, tokens, errors, features, side, w_dec, marks, start):
    count = len(tokens)
    part, width = errors[0].shape
    feats = w_dec.shape[0] // 2
    rows = block_rows(feats, 256 if part <= 512 else 128)
    steps = feats // rows

    def kernel(core_ref, *refs):
        token_refs, error_refs = refs[:count], refs[count : 2 * count]
        feat_ref, dec_ref, mark_ref, start_ref, out_ref, *square_ref = refs[2 * count :]
        weight = dec_ref[...].astype(jnp.bfloat16)
        if side:
            enc, dec = start_ref[0], start_ref[1]
        else:
            enc, dec = start_ref[...], jnp.zeros((rows, width), jnp.float32)
        for k in range(count):
            at = pl.ds(k * part, part)
            feat = feat_ref[:, at]
            dfeat = times_trans(weight, error_refs[k][...]) + mark_ref[:, at]
            dpre = jnp.where(feat > 0, dfeat, 0.0).astype(jnp.bfloat16)
            enc = enc + times(dpre, token_refs[k][...])
            dec = dec + times(feat, error_refs[k][...])
        out_ref[0] = enc
        out_ref[1] = dec
        if side:

            @pl.when(pl.program_id(0) == 0)
            def _():
                square_ref[0][...] = jnp.zeros_like(square_ref[0])

            square_ref[0][...] += fold(enc * enc) + fold(dec * dec)

    whole = pl.BlockSpec((part, width), lambda i, s: (0, 0), pipeline_mode=ONCE)
    both = pl.BlockSpec((2, rows, width), lambda i, s: (0, i, 0))
    block = pl.BlockSpec((rows, width), lambda i, s: (i, 0))
    out_specs = [both] + [pl.BlockSpec((8, 128), lambda i, s: (0, 0))] * side
    out_shape = [pltpu.HBM((2, feats, width), jnp.float32)]
    out_shape = out_shape + [jax.ShapeDtypeStruct((8, 128), jnp.float32)] * side
    outs = pl.pallas_call(
        kernel,
        grid_spec=scalars(
            (steps,),
            [whole] * (2 * count)
            + [
                pl.BlockSpec((rows, count * part), lambda i, s: (i, side)),
                pl.BlockSpec((rows, width), lambda i, s: (s[0] * steps + i, 0)),
                pl.BlockSpec((1, count * part), lambda i, s: (0, side)),
                both if side else block,
            ],
            out_specs,
        ),
        out_shape=out_shape,
        compiler_params=pltpu.CompilerParams(
            vmem_limit_bytes=(18 << 20) + 4 * count * part * width
        ),
        cost_estimate=pl.CostEstimate(
            flops=6 * feats * width * count * part,
            bytes_accessed=(2 * feats + 4 * width) * count * part + 20 * feats * width,
            transcendentals=0,
        ),
        name="gradients",
    )(
        core,
        *map(in_hbm, tokens),
        *map(in_hbm, errors),
        in_hbm(features),
        in_hbm(w_dec),
        marks,
        in_hbm(start),
    )
    return outs if side else outs[0]


def norm_of(pieces):
    def kernel(*refs):
        total = jnp.sum(paired([ref[0] for ref in refs[:-1]]), keepdims=True).reshape(1, 1)
        refs[-1][...] = jnp.broadcast_to(jnp.sqrt(total), refs[-1].shape)

    return pl.pallas_call(
        kernel,
        in_specs=[VMEM] * len(pieces),
        out_specs=VMEM,
        out_shape=jax.ShapeDtypeStruct((8, 128), jnp.float32),
        compiler_params=pltpu.CompilerParams(vmem_limit_bytes=1 << 20),
        name="norm",
    )(*pieces)


def moments(
    core, clip_norm, own, other, w_enc, enc_first, enc_second, w_dec, dec_first, dec_second
):
    feats, width = w_enc.shape
    rows = block_rows(feats // 2, 192)
    half = feats // 2 // rows
    steps = 2 * half

    def kernel(core_ref, norm_ref, own_ref, other_ref, *refs):
        enc, dec, outs = refs[:3], refs[3:6], refs[6:]
        dir_refs, (first_out, second_out, square_ref) = outs[:2], outs[2:]
        factor = clip_limit / jnp.maximum(norm_ref[:1, :1], clip_limit)
        square_ref[...] = jnp.zeros_like(square_ref)
        start = core_ref[0] * half

        def place(i):
            return lax.rem(start + i, steps)

        def body(own, other, enc_first, enc_second, dec_first, dec_second, first_ref, second_ref):
            step = pl.program_id(0)
            at = pl.ds(pl.multiple_of(place(step) * rows, rows), rows)
            sides = ((enc[0], enc_first, enc_second), (dec[0], dec_first, dec_second))
            for plane, (weight, first, second) in enumerate(sides):
                clipped = jnp.where(step < half, own[plane], other[plane]) * factor
                first_new = beta_one * first[...] + (1.0 - beta_one) * clipped
                second_new = beta_two * second[...] + (1.0 - beta_two) * clipped * clipped
                first_ref[plane] = first_new
                second_ref[plane] = second_new
                scaled = second_new * (1.0 / (1.0 - beta_two**STEP))
                spread = scaled * lax.rsqrt(scaled) + adam_eps
                direction = (
                    first_new * (1.0 / (1.0 - beta_one**STEP)) * pltpu.reciprocal(spread)
                    + weight_decay * weight[at, :]
                )
                dir_refs[plane][at, :] = direction
                square_ref[plane] += fold(direction * direction)

        block = pl.BlockSpec((rows, width), lambda i: (place(i), 0))
        both = pl.BlockSpec((2, rows, width), lambda i: (0, place(i), 0))
        early = pl.BlockSpec((2, rows, width), lambda i: (0, jnp.minimum(i, half - 1), 0))
        late = pl.BlockSpec((2, rows, width), lambda i: (0, jnp.maximum(i - half, 0), 0))
        pltpu.emit_pipeline(
            body,
            grid=(steps,),
            in_specs=[early, late] + [block] * 4,
            out_specs=[both, both],
        )(own_ref, other_ref, enc[1], enc[2], dec[1], dec[2], first_out, second_out)

    full = (2, feats, width)
    return pl.pallas_call(
        kernel,
        in_specs=[pl.BlockSpec(memory_space=pltpu.SMEM), VMEM, PLACED, PLACED]
        + [VMEM, PLACED, PLACED] * 2,
        out_specs=[VMEM, VMEM, PLACED, PLACED, VMEM],
        out_shape=[
            pltpu.VMEM((feats, width), jnp.float32),
            pltpu.VMEM((feats, width), jnp.float32),
            pltpu.HBM(full, jnp.float32),
            pltpu.HBM(full, jnp.float32),
            jax.ShapeDtypeStruct((2, 8, 128), jnp.float32),
        ],
        compiler_params=pltpu.CompilerParams(vmem_limit_bytes=16 << 20),
        cost_estimate=pl.CostEstimate(
            flops=40 * feats * width,
            bytes_accessed=40 * feats * width,
            transcendentals=4 * feats * width,
        ),
        name="moments",
    )(
        core,
        clip_norm,
        in_hbm(own),
        in_hbm(other),
        in_vmem(w_enc),
        in_hbm(enc_first),
        in_hbm(enc_second),
        in_vmem(w_dec),
        in_hbm(dec_first),
        in_hbm(dec_second),
    )


def renew(sums, small, terms, clip_norm, directions, w_enc, w_dec, total_picks):
    feats, width = w_enc.shape
    rows = block_rows(feats, 256)

    count = len(sums)

    def kernel(*refs):
        sum_refs, small_refs, refs = refs[:count], refs[count : 2 * count], refs[2 * count :]
        term_ref, clip_ref, enc_dir, dec_dir, enc_ref, dec_ref, out_ref, row_ref = refs
        sums = paired([ref[...] for ref in sum_refs])
        small = paired([ref[...] for ref in small_refs])
        def total(values):
            return jnp.sum(values, keepdims=True).reshape(1, 1)

        norms = [jnp.sqrt(0.5 * total(small[2 + plane])) for plane in range(2)]
        steps = [jnp.sqrt(total(sums[plane])) for plane in range(2)]
        rates = [learn_rate * (norms[plane] / steps[plane]) for plane in range(2)]
        loss = term_ref[0, :1, :1] / total_picks + term_ref[1, :1, :1] * total(small[1])
        for i, value in enumerate((*norms, *steps, loss, clip_ref[:1, :1])):
            row_ref[i : i + 1, :] = jnp.broadcast_to(value, (1, 128))
        row_ref[6:, :] = jnp.zeros((2, 128), jnp.float32)

        def body(enc_w, dec_w, new_ref):
            at = pl.ds(pl.multiple_of(pl.program_id(0) * rows, rows), rows)
            new_ref[0] = enc_w[...] - rates[0] * enc_dir[at, :]
            raw = dec_w[...] - rates[1] * dec_dir[at, :]
            new_ref[1] = raw * lax.rsqrt(jnp.sum(raw * raw, 1, keepdims=True) + 1e-06)

        both = pl.BlockSpec((2, rows, width), lambda i: (0, i, 0))
        block = pl.BlockSpec((rows, width), lambda i: (i, 0))
        pltpu.emit_pipeline(
            body, grid=(feats // rows,), in_specs=[block, block], out_specs=[both]
        )(enc_ref, dec_ref, out_ref)

    return pl.pallas_call(
        kernel,
        in_specs=[VMEM] * (2 * count + 4) + [PLACED] * 2,
        out_specs=[PLACED, VMEM],
        out_shape=[
            pltpu.HBM((2, feats, width), jnp.float32),
            jax.ShapeDtypeStruct((8, 128), jnp.float32),
        ],
        compiler_params=pltpu.CompilerParams(vmem_limit_bytes=16 << 20),
        cost_estimate=pl.CostEstimate(
            flops=12 * w_enc.size, bytes_accessed=8 * w_enc.size, transcendentals=0
        ),
        name="renew",
    )(*sums, *small, terms, clip_norm, *map(in_vmem, directions), in_hbm(w_enc), in_hbm(w_dec))


def shards(
    resid_pre,
    token_ids,
    valid_mask,
    picked,
    norm_gains,
    norm_biases,
    qkv_w,
    out_w,
    fc_w,
    proj_w,
    layer_bias,
    wte,
    w_enc,
    enc_first,
    enc_second,
    b_enc,
    w_dec,
    dec_first,
    dec_second,
    b_dec,
):
    low = jnp.bfloat16
    count, seq_len, model_width = resid_pre.shape
    size = lax.axis_size("fsdp")
    mine = lax.axis_index("fsdp")
    pick_count = picked.shape[1]
    rest_count = seq_len - pick_count
    hidden_units = fc_w.shape[1]
    vocab_rows = wte.shape[0]
    total_picks = lax.axis_size("dp") * size * count * pick_count
    fc_b = layer_bias[4 * model_width : 4 * model_width + hidden_units]
    proj_b = layer_bias[4 * model_width + hidden_units :]

    grouped_picks = picked.reshape(size, count, pick_count)
    own_pick, own_rest, own_inputs = attention(
        resid_pre,
        lax.dynamic_index_in_dim(grouped_picks, mine, 0, keepdims=False),
        norm_gains,
        norm_biases,
        qkv_w,
        out_w,
        layer_bias.reshape(1, -1),
        b_dec.reshape(1, -1),
    )
    own_count = own_inputs.shape[0]

    me = mine.reshape(1).astype(jnp.int32)
    core = (lax.axis_index("dp") & 1).reshape(1).astype(jnp.int32)
    own_pick, picked, valid_mask = lax.optimization_barrier((own_pick, picked, valid_mask))
    masks = gather_copies(mask_rows(me, size, picked, valid_mask))
    tokens = join(gather_near(own_pick))
    tokens, own_rest = lax.optimization_barrier((tokens, own_rest))
    rest = gather_group(own_rest)
    all_pick = gather_copies(tokens)
    shares, weight_squares = encode(
        me, tokens, size, own_count, w_enc, w_dec, b_enc.reshape(1, -1)
    )
    shares, rest, token_ids, grouped_picks, masks = lax.optimization_barrier(
        (shares, rest, token_ids, grouped_picks, masks)
    )
    recon = jnp.sum(trade(shares).astype(jnp.float32), 0) + b_dec

    place = lax.broadcasted_iota(jnp.int32, (1, 1, 1, seq_len), 3)
    ids = token_ids.reshape(size, count, 1, seq_len)
    targets = jnp.sum(jnp.where(grouped_picks[..., None] + 1 == place, ids, 0), -1).reshape(-1)
    targets = targets - mine * vocab_rows
    here = (targets >= 0) & (targets < vocab_rows)
    target_rows = jnp.take(wte, jnp.clip(targets, 0, vocab_rows - 1), axis=0)
    target_rows = jnp.where(here[:, None], target_rows, jnp.zeros_like(target_rows))
    pick_mask, rest_mask, pick_marks, rest_marks, sparse_coef = mark_rows(masks)
    bias = b_enc.reshape(-1, 1)
    recon, target_rows, pick_marks, rest_marks, rest = lax.optimization_barrier(
        (recon, target_rows, pick_marks, rest_marks, rest)
    )
    far_rest = across(rest)

    mid = own_inputs + recon
    normed, second_norm_back = jax.vjp(
        lambda values: layer_norm(values, norm_gains[1], norm_biases[1]), mid
    )
    up_val = times(normed.astype(low), fc_w) + fc_b
    act, gelu_back = jax.vjp(lambda values: jax.nn.gelu(values, approximate=True), up_val)
    hidden = mid + times(act.astype(low), proj_w) + proj_b
    final, final_norm_back = jax.vjp(
        lambda values: layer_norm(values, norm_gains[2], norm_biases[2]), hidden
    )
    finals = gather_group(final.astype(low))
    all_feat, pick_sparse = feature_rows(
        core, all_pick, size * own_count, w_enc, bias, pick_mask
    )
    far_rest, all_feat = lax.optimization_barrier((far_rest, all_feat))
    finals, all_feat, far_rest = lax.optimization_barrier((finals, all_feat, far_rest))
    all_rest = spread(rest) + spread(far_rest)

    logits = times_trans(finals, wte)
    top = jnp.max(logits, 1)
    parts = jnp.exp(logits - top[:, None])
    mass = jnp.sum(parts, 1)
    at = jnp.sum(finals.astype(jnp.float32) * target_rows.astype(jnp.float32), 1)
    stats = trade(jnp.broadcast_to(jnp.stack([top, mass, at])[None], (size, 3, top.shape[0])))
    mixed = times(parts.astype(low), wte)
    stats, mixed = lax.optimization_barrier((stats, mixed))
    best = jnp.max(stats[:, 0], 0)
    total = jnp.sum(stats[:, 1] * jnp.exp(stats[:, 0] - best), 0)
    cross = jnp.sum(best + jnp.log(total) - jnp.sum(stats[:, 2], 0))
    scale = jnp.exp(top - best) / total
    dshares = (mixed * scale[:, None] - target_rows.astype(jnp.float32)) / total_picks
    dshares = dshares.astype(low).reshape(size, -1, model_width)
    cross = jnp.broadcast_to(cross, (1, 128))
    dshares, idle_marks, cross = lax.optimization_barrier((dshares, rest_marks, cross))
    bit = lax.axis_size("dp") // 2
    while bit:
        cross = cross + swap(cross, "dp", bit)
        bit //= 2
    dfinal = jnp.sum(trade(dshares).astype(jnp.float32), 0)
    idle, rest_sparse = idle_gradient(
        core, all_rest, size * own_count, w_enc, bias, rest_mask, idle_marks
    )
    dfinal, idle, pick_sparse, cross = lax.optimization_barrier((dfinal, idle, pick_sparse, cross))

    dhidden = final_norm_back(dfinal)[0]
    dact = times_trans(dhidden.astype(low), proj_w)
    dup_low = gelu_back(dact)[0].astype(low)
    dnormed = times_trans(dup_low, fc_w)
    drecon = (dhidden + second_norm_back(dnormed)[0]).astype(low)

    errors = join(gather_near(drecon))
    far_errors = across(errors)
    middle = len(all_pick) // 2
    near = gradients(
        core, all_pick[:middle], spread(errors), all_feat, 0, w_dec, pick_marks, idle
    )
    near, far_errors = lax.optimization_barrier((near, far_errors))
    own, squares = gradients(
        core, all_pick[middle:], spread(far_errors), all_feat, 1, w_dec, pick_marks, near
    )
    terms = jnp.stack([cross, sparse_coef])
    small = jnp.stack([squares, pick_sparse + rest_sparse, weight_squares[0], weight_squares[1]])
    small, own, terms = lax.optimization_barrier((small + swap(small, "dp", 1), own, terms))
    other = swap(own, "dp", 1)
    small = pieces_of(small)
    clip_norm = norm_of(small)
    *directions, firsts, seconds, squares = moments(
        core,
        clip_norm,
        own,
        other,
        w_enc,
        enc_first,
        enc_second,
        w_dec,
        dec_first,
        dec_second,
    )
    weights, rows = renew(
        pieces_of(squares), small, terms, clip_norm, directions, w_enc, w_dec, total_picks
    )
    return weights, firsts, seconds, rows[4, 0], rows[5, 0], rows[:2, 0], rows[2:4, 0]


def solution(mesh):
    in_specs = (
        P(("dp", "fsdp"), None, None),
        P("dp", None),
        P("dp", None),
        P("dp", None),
        P(),
        P(),
        P(),
        P(),
        P(),
        P(),
        P(),
        P("fsdp", None),
        P("fsdp", None),
        P("fsdp", None),
        P("fsdp", None),
        P("fsdp"),
        P("fsdp", None),
        P("fsdp", None),
        P("fsdp", None),
        P(),
    )
    out_specs = (
        P(None, "fsdp", None),
        P(None, "fsdp", None),
        P(None, "fsdp", None),
        P(),
        P(),
        P(),
        P(),
    )
    return jax.shard_map(shards, mesh=mesh, in_specs=in_specs, out_specs=out_specs, check_vma=False)
```

```python
import jax
import jax.numpy as jnp
from jax import lax
from jax.experimental import pallas as pl
from jax.experimental.pallas import tpu as pltpu
from jax.sharding import PartitionSpec as P

HEADS = 12
HEAD_DIM = 64
F = 24576
STEP = 10


norm_eps = 1e-05
l1_scale = 40.0
clip_limit = 0.02
learn_rate = 0.3
beta_one = 0.9
beta_two = 0.999
adam_eps = 1e-08
weight_decay = 0.01


def layer_norm(values, gain, shift):
    center = values - jnp.mean(values, -1, keepdims=True)
    spread = jnp.mean(center * center, -1, keepdims=True)
    return center * lax.rsqrt(spread + norm_eps) * gain + shift


def times(left, right):
    return jnp.dot(left, right, preferred_element_type=jnp.float32)


def times_trans(left, right):
    return lax.dot_general(
        left, right, (((1,), (1,)), ((), ())), preferred_element_type=jnp.float32
    )


def trans_times(left, right):
    return lax.dot_general(
        left, right, (((0,), (0,)), ((), ())), preferred_element_type=jnp.float32
    )


def swap(block, axis, bit):
    size = lax.axis_size(axis)
    return lax.ppermute(block, axis, [(i, i ^ bit) for i in range(size)])


def trade(blocks):
    return lax.all_to_all(blocks, "fsdp", 0, 0, tiled=True)


def gather_group(block):
    size = lax.axis_size("fsdp")
    spread = jnp.broadcast_to(block[None], (size, *block.shape))
    return trade(spread).reshape(-1, *block.shape[1:])


def gather_near(block):
    half = lax.axis_size("fsdp") // 2
    far = swap(block, "fsdp", half)
    near = [block] + [swap(block, "fsdp", k) for k in range(1, half)]
    return near + [far] + [swap(far, "fsdp", k) for k in range(1, half)]


def pieces_of(block):
    size = lax.axis_size("fsdp")
    return [block] + [swap(block, "fsdp", k) for k in range(1, size)]


def paired(pieces):
    while len(pieces) > 1:
        pieces = [a + b for a, b in zip(pieces[::2], pieces[1::2])]
    return pieces[0]


def across(block):
    return swap(block, "dp", lax.axis_size("dp") // 2)


def spread(block):
    blocks = [block]
    bit = lax.axis_size("dp") // 4
    while bit:
        blocks = blocks + [swap(held, "dp", bit) for held in blocks]
        bit //= 2
    return blocks


def gather_copies(block):
    return spread(block) + spread(across(block))


VMEM = pl.BlockSpec(memory_space=pltpu.VMEM)
PLACED = pl.BlockSpec(memory_space=pl.ANY)
ONCE = pl.Buffered(1)


def in_vmem(values):
    return pltpu.with_memory_space_constraint(values, pltpu.VMEM)


def in_hbm(values):
    return pltpu.with_memory_space_constraint(values, pltpu.HBM)


def fold(values):
    rows, width = values.shape
    total = jnp.sum(values.reshape(rows // 8, 8, width), 0)
    return sum(total[:, k : k + 128] for k in range(0, width, 128))


def block_rows(count, most):
    return max(rows for rows in range(16, most + 1, 16) if count % rows == 0)


def scalars(grid, in_specs, out_specs, scratch_shapes=()):
    return pltpu.PrefetchScalarGridSpec(
        num_scalar_prefetch=1,
        grid=grid,
        in_specs=in_specs,
        out_specs=out_specs,
        scratch_shapes=scratch_shapes,
    )


def attention(resid, picks, gains, shifts, qkv_w, out_w, layer_bias, b_dec):
    count, length, width = resid.shape
    pick_count = picks.shape[1]
    rest_count = length - pick_count
    pair = 2 * HEAD_DIM

    def kernel(
        resid_ref,
        pick_ref,
        gain_ref,
        shift_ref,
        qkv_ref,
        out_ref,
        bias_ref,
        dec_ref,
        rows_ref,
        rest_ref,
        inputs_ref,
    ):
        values = resid_ref[...].astype(jnp.float32).reshape(count * length, width)
        normed = layer_norm(values, gain_ref[:1, :], shift_ref[:1, :]).astype(jnp.bfloat16)
        packed = (times(normed, qkv_ref[...]) + bias_ref[:, : 3 * width]).astype(jnp.bfloat16)
        first = lax.broadcasted_iota(jnp.int32, (length, pair), 1) < HEAD_DIM
        row_ids = lax.broadcasted_iota(jnp.int32, (length, length), 0)
        col_ids = lax.broadcasted_iota(jnp.int32, (length, length), 1)
        causal = jnp.concatenate([row_ids >= col_ids] * 2, 0)
        contexts = []
        for s in range(count):
            at = slice(s * length, (s + 1) * length)
            pairs = []
            for lane in range(0, width, pair):
                query = packed[at, lane : lane + pair]
                key = packed[at, width + lane : width + lane + pair]
                value = packed[at, 2 * width + lane : 2 * width + lane + pair]
                zero = jnp.zeros_like(query)
                both = jnp.concatenate(
                    [jnp.where(first, query, zero), jnp.where(first, zero, query)], 0
                )
                scores = times_trans(both, key) * HEAD_DIM ** (-0.5)
                scores = jnp.where(causal, scores, -1e30)
                powers = jnp.exp(scores - jnp.max(scores, -1, keepdims=True))
                probs = (powers / jnp.sum(powers, -1, keepdims=True)).astype(jnp.bfloat16)
                mixed = times(probs, value)
                pairs.append(jnp.where(first, mixed[:length], mixed[length:]))
            contexts.append(jnp.concatenate(pairs, 1).astype(jnp.bfloat16))
        context = jnp.concatenate(contexts, 0)
        attn = times(context, out_ref[...]) + bias_ref[:, 3 * width : 4 * width]
        centered = (attn - dec_ref[...]).astype(jnp.bfloat16)
        after = (row_ids < col_ids).astype(jnp.float32)
        lanes = lax.broadcasted_iota(jnp.int32, (pick_count, length), 1)
        slots = lax.broadcasted_iota(jnp.int32, (rest_count, length), 0).astype(jnp.float32)
        for s in range(count):
            at = slice(s * length, (s + 1) * length)
            chosen = (pick_ref[s] == lanes).astype(jnp.float32)
            free = 1.0 - jnp.sum(chosen, 0, keepdims=True)
            rank = times(jnp.broadcast_to(free, (8, length)), after)[:1]
            others = jnp.where((rank == slots) & (free > 0), 1.0, 0.0).astype(jnp.bfloat16)
            chosen = chosen.astype(jnp.bfloat16)
            rows_ref[s * pick_count : (s + 1) * pick_count, :] = times(
                chosen, centered[at]
            ).astype(jnp.bfloat16)
            rest_ref[s * rest_count : (s + 1) * rest_count, :] = times(
                others, centered[at]
            ).astype(jnp.bfloat16)
            inputs_ref[s * pick_count : (s + 1) * pick_count, :] = times(chosen, resid_ref[s])

    return pl.pallas_call(
        kernel,
        in_specs=[VMEM] * 8,
        out_specs=[VMEM, VMEM, VMEM],
        out_shape=[
            jax.ShapeDtypeStruct((count * pick_count, width), jnp.bfloat16),
            jax.ShapeDtypeStruct((count * rest_count, width), jnp.bfloat16),
            jax.ShapeDtypeStruct((count * pick_count, width), jnp.float32),
        ],
        compiler_params=pltpu.CompilerParams(vmem_limit_bytes=32 << 20),
        cost_estimate=pl.CostEstimate(
            flops=8 * count * length * width * width,
            bytes_accessed=8 * width * width,
            transcendentals=count * length * width,
        ),
        name="attention",
    )(resid, picks[..., None], gains, shifts, qkv_w, out_w, layer_bias, b_dec)


def join(blocks):
    part, width = blocks[0].shape
    count = len(blocks)

    def kernel(*refs):
        for k in range(count):
            refs[count][k * part : (k + 1) * part, :] = refs[k][...]

    return pl.pallas_call(
        kernel,
        in_specs=[VMEM] * count,
        out_specs=VMEM,
        out_shape=jax.ShapeDtypeStruct((part * count, width), blocks[0].dtype),
        name="join",
    )(*blocks)


def mask_rows(mine, size, picked, valid_mask):
    count, pick_count = picked.shape
    length = valid_mask.shape[1]
    lanes = count * pick_count
    block = lanes // size

    def kernel(mine_ref, pick_ref, mask_ref, out_ref):
        def one(test):
            return jnp.where(test, 1.0, 0.0).astype(jnp.bfloat16)

        def ids(shape, dim):
            return lax.broadcasted_iota(jnp.int32, shape, dim)

        wide, square = (length, lanes), (lanes, lanes)
        chosen = one(pick_ref[...] == ids(wide, 0))
        group = one(ids(square, 0) // pick_count == ids(square, 1) // pick_count)
        free = 1.0 - times(chosen, group)
        before = one(ids((length, length), 0) > ids((length, length), 1))
        rank = times(before, free.astype(jnp.bfloat16))
        slot = lax.rem(ids(wide, 1), pick_count).astype(jnp.float32)
        others = jnp.where((rank == slot) & (free > 0), 1.0, 0.0)
        owner = one(ids((count, lanes), 0) == ids((count, lanes), 1) // pick_count)
        mask = trans_times(mask_ref[...].astype(jnp.bfloat16), owner)
        picks = jnp.sum(chosen.astype(jnp.float32) * mask, 0, keepdims=True)
        source, target = ids(square, 0), ids(square, 1)
        moved = one(
            (source // block == ((target // block) ^ mine_ref[0]))
            & (lax.rem(source, block) == lax.rem(target, block))
        )
        out_ref[:1, :] = times(picks.astype(jnp.bfloat16), moved)
        out_ref[1:, :] = jnp.sum(others * mask, 0, keepdims=True)

    return pl.pallas_call(
        kernel,
        in_specs=[pl.BlockSpec(memory_space=pltpu.SMEM), VMEM, VMEM],
        out_specs=VMEM,
        out_shape=jax.ShapeDtypeStruct((2, lanes), jnp.float32),
        compiler_params=pltpu.CompilerParams(vmem_limit_bytes=(8 << 20) + 12 * lanes * lanes),
        name="masks",
    )(mine, picked.reshape(1, -1), valid_mask)


def mark_rows(masks):
    count = len(masks)
    lanes = masks[0].shape[1]

    def kernel(*refs):
        pick_ref, rest_ref, pick_marks, rest_marks, coef_ref = refs[count:]
        total = sum(jnp.sum(ref[...], keepdims=True).reshape(1, 1) for ref in refs[:count])
        coef = l1_scale / F / total
        coef_ref[...] = jnp.broadcast_to(coef, (1, 128))
        for k in range(count):
            at = slice(k * lanes, (k + 1) * lanes)
            pick_ref[:, at] = refs[k][:1, :]
            rest_ref[:, at] = refs[k][1:, :]
            pick_marks[:, at] = refs[k][:1, :] * coef
            rest_marks[:, at] = refs[k][1:, :] * coef

    return pl.pallas_call(
        kernel,
        in_specs=[VMEM] * count,
        out_specs=[VMEM] * 5,
        out_shape=[jax.ShapeDtypeStruct((1, count * lanes), jnp.float32)] * 4
        + [jax.ShapeDtypeStruct((1, 128), jnp.float32)],
        name="marks",
    )(*masks)


def encode(mine, tokens, count, part, w_enc, w_dec, b_enc):
    width = tokens.shape[1]
    feats = w_enc.shape[0]
    rows = block_rows(feats, 512)
    steps = feats // rows

    def kernel(mine_ref, token_ref, enc_ref, dec_ref, bias_ref, share_ref, square_ref, total_ref):

        @pl.when(pl.program_id(0) == 0)
        def _():
            square_ref[...] = jnp.zeros_like(square_ref)
            total_ref[...] = jnp.zeros_like(total_ref)

        enc, dec = enc_ref[...], dec_ref[...]
        square_ref[0] += fold(enc * enc)
        square_ref[1] += fold(dec * dec)
        enc_low, dec_low = enc.astype(jnp.bfloat16), dec.astype(jnp.bfloat16)
        features = jnp.maximum(times_trans(token_ref[...], enc_low) + bias_ref[...], 0.0)
        total_ref[...] += times(features.astype(jnp.bfloat16), dec_low)

        @pl.when(pl.program_id(0) == steps - 1)
        def _():
            for k in range(count):
                share_ref[mine_ref[0] ^ k] = total_ref[k * part : (k + 1) * part, :].astype(
                    jnp.bfloat16
                )

    whole = pl.BlockSpec((count * part, width), lambda i, s: (0, 0), pipeline_mode=ONCE)
    block = pl.BlockSpec((rows, width), lambda i, s: (i, 0))
    return pl.pallas_call(
        kernel,
        grid_spec=scalars(
            (steps,),
            [whole, block, block, pl.BlockSpec((1, rows), lambda i, s: (0, i))],
            [
                pl.BlockSpec((count, part, width), lambda i, s: (0, 0, 0)),
                pl.BlockSpec((2, 8, 128), lambda i, s: (0, 0, 0)),
            ],
            [pltpu.VMEM((count * part, width), jnp.float32)],
        ),
        out_shape=[
            jax.ShapeDtypeStruct((count, part, width), jnp.bfloat16),
            jax.ShapeDtypeStruct((2, 8, 128), jnp.float32),
        ],
        compiler_params=pltpu.CompilerParams(
            vmem_limit_bytes=(24 << 20) + 12 * count * part * width
        ),
        cost_estimate=pl.CostEstimate(
            flops=4 * feats * width * count * part, bytes_accessed=8 * feats * width, transcendentals=0
        ),
        name="encode",
    )(mine, in_hbm(tokens), in_hbm(w_enc), in_hbm(w_dec), b_enc)


def feature_rows(core, tokens, part, w_enc, bias, masks):
    count = len(tokens)
    width = tokens[0].shape[1]
    feats = w_enc.shape[0] // 2
    rows = block_rows(feats, 512 if part <= 512 else 128)
    steps = feats // rows

    def kernel(core_ref, *refs):
        token_refs = refs[:count]
        enc_ref, bias_ref, mask_ref, out_ref, sum_ref = refs[count:]

        @pl.when(pl.program_id(0) == 0)
        def _():
            sum_ref[...] = jnp.zeros_like(sum_ref)

        enc = enc_ref[...].astype(jnp.bfloat16)
        for k in range(count):
            at = pl.ds(k * part, part)
            pre = times_trans(enc, token_refs[k][...]) + bias_ref[...]
            kept = jnp.maximum(pre, 0.0)
            out_ref[:, at] = kept.astype(jnp.bfloat16)
            sum_ref[...] += fold(kept * mask_ref[:, at])

    whole = pl.BlockSpec((part, width), lambda i, s: (0, 0), pipeline_mode=ONCE)
    return pl.pallas_call(
        kernel,
        grid_spec=scalars(
            (steps,),
            [whole] * count
            + [
                pl.BlockSpec((rows, width), lambda i, s: (s[0] * steps + i, 0)),
                pl.BlockSpec((rows, 1), lambda i, s: (s[0] * steps + i, 0)),
                pl.BlockSpec((1, count * part), lambda i, s: (0, 0)),
            ],
            [
                pl.BlockSpec((rows, count * part), lambda i, s: (i, 0)),
                pl.BlockSpec((8, 128), lambda i, s: (0, 0)),
            ],
        ),
        out_shape=[
            pltpu.HBM((feats, count * part), jnp.bfloat16),
            jax.ShapeDtypeStruct((8, 128), jnp.float32),
        ],
        compiler_params=pltpu.CompilerParams(
            vmem_limit_bytes=(24 << 20) + 2 * count * part * width
        ),
        cost_estimate=pl.CostEstimate(
            flops=2 * feats * width * count * part,
            bytes_accessed=2 * (feats + width) * count * part + 2 * feats * width,
            transcendentals=0,
        ),
        name="features",
    )(core, *map(in_hbm, tokens), in_hbm(w_enc), bias, masks)


def idle_gradient(core, tokens, part, w_enc, bias, masks, marks):
    count = len(tokens)
    width = tokens[0].shape[1]
    feats = w_enc.shape[0] // 2
    rows = block_rows(feats, 512 if part <= 512 else 128)
    steps = feats // rows

    def kernel(core_ref, *refs):
        token_refs = refs[:count]
        enc_ref, bias_ref, mask_ref, mark_ref, out_ref, sum_ref = refs[count:]

        @pl.when(pl.program_id(0) == 0)
        def _():
            sum_ref[...] = jnp.zeros_like(sum_ref)

        grad = jnp.zeros(out_ref.shape, jnp.float32)
        enc = enc_ref[...].astype(jnp.bfloat16)
        for k in range(count):
            at = pl.ds(k * part, part)
            pre = times_trans(enc, token_refs[k][...]) + bias_ref[...]
            sum_ref[...] += fold(jnp.maximum(pre, 0.0) * mask_ref[:, at])
            dpre = jnp.where(pre > 0, mark_ref[:, at], 0.0).astype(jnp.bfloat16)
            grad = grad + times(dpre, token_refs[k][...])
        out_ref[...] = grad

    whole = pl.BlockSpec((part, width), lambda i, s: (0, 0), pipeline_mode=ONCE)
    row = pl.BlockSpec((1, count * part), lambda i, s: (0, 0))
    return pl.pallas_call(
        kernel,
        grid_spec=scalars(
            (steps,),
            [whole] * count
            + [
                pl.BlockSpec((rows, width), lambda i, s: (s[0] * steps + i, 0)),
                pl.BlockSpec((rows, 1), lambda i, s: (s[0] * steps + i, 0)),
                row,
                row,
            ],
            [
                pl.BlockSpec((rows, width), lambda i, s: (i, 0)),
                pl.BlockSpec((8, 128), lambda i, s: (0, 0)),
            ],
        ),
        out_shape=[
            pltpu.HBM((feats, width), jnp.float32),
            jax.ShapeDtypeStruct((8, 128), jnp.float32),
        ],
        compiler_params=pltpu.CompilerParams(
            vmem_limit_bytes=(24 << 20) + 2 * count * part * width
        ),
        cost_estimate=pl.CostEstimate(
            flops=4 * feats * width * count * part,
            bytes_accessed=2 * width * count * part + 6 * feats * width,
            transcendentals=0,
        ),
        name="idle",
    )(core, *map(in_hbm, tokens), in_hbm(w_enc), bias, masks, marks)


def gradients(core, tokens, errors, features, side, w_dec, marks, start):
    count = len(tokens)
    part, width = errors[0].shape
    feats = w_dec.shape[0] // 2
    rows = block_rows(feats, 256 if part <= 512 else 128)
    steps = feats // rows

    def kernel(core_ref, *refs):
        token_refs, error_refs = refs[:count], refs[count : 2 * count]
        feat_ref, dec_ref, mark_ref, start_ref, out_ref, *square_ref = refs[2 * count :]
        weight = dec_ref[...].astype(jnp.bfloat16)
        if side:
            enc, dec = start_ref[0], start_ref[1]
        else:
            enc, dec = start_ref[...], jnp.zeros((rows, width), jnp.float32)
        for k in range(count):
            at = pl.ds(k * part, part)
            feat = feat_ref[:, at]
            dfeat = times_trans(weight, error_refs[k][...]) + mark_ref[:, at]
            dpre = jnp.where(feat > 0, dfeat, 0.0).astype(jnp.bfloat16)
            enc = enc + times(dpre, token_refs[k][...])
            dec = dec + times(feat, error_refs[k][...])
        out_ref[0] = enc
        out_ref[1] = dec
        if side:

            @pl.when(pl.program_id(0) == 0)
            def _():
                square_ref[0][...] = jnp.zeros_like(square_ref[0])

            square_ref[0][...] += fold(enc * enc) + fold(dec * dec)

    whole = pl.BlockSpec((part, width), lambda i, s: (0, 0), pipeline_mode=ONCE)
    both = pl.BlockSpec((2, rows, width), lambda i, s: (0, i, 0))
    block = pl.BlockSpec((rows, width), lambda i, s: (i, 0))
    out_specs = [both] + [pl.BlockSpec((8, 128), lambda i, s: (0, 0))] * side
    out_shape = [pltpu.HBM((2, feats, width), jnp.float32)]
    out_shape = out_shape + [jax.ShapeDtypeStruct((8, 128), jnp.float32)] * side
    outs = pl.pallas_call(
        kernel,
        grid_spec=scalars(
            (steps,),
            [whole] * (2 * count)
            + [
                pl.BlockSpec((rows, count * part), lambda i, s: (i, side)),
                pl.BlockSpec((rows, width), lambda i, s: (s[0] * steps + i, 0)),
                pl.BlockSpec((1, count * part), lambda i, s: (0, side)),
                both if side else block,
            ],
            out_specs,
        ),
        out_shape=out_shape,
        compiler_params=pltpu.CompilerParams(
            vmem_limit_bytes=(18 << 20) + 4 * count * part * width
        ),
        cost_estimate=pl.CostEstimate(
            flops=6 * feats * width * count * part,
            bytes_accessed=(2 * feats + 4 * width) * count * part + 20 * feats * width,
            transcendentals=0,
        ),
        name="gradients",
    )(
        core,
        *map(in_hbm, tokens),
        *map(in_hbm, errors),
        in_hbm(features),
        in_hbm(w_dec),
        marks,
        in_hbm(start),
    )
    return outs if side else outs[0]


def norm_of(pieces):
    def kernel(*refs):
        total = jnp.sum(paired([ref[0] for ref in refs[:-1]]), keepdims=True).reshape(1, 1)
        refs[-1][...] = jnp.broadcast_to(jnp.sqrt(total), refs[-1].shape)

    return pl.pallas_call(
        kernel,
        in_specs=[VMEM] * len(pieces),
        out_specs=VMEM,
        out_shape=jax.ShapeDtypeStruct((8, 128), jnp.float32),
        compiler_params=pltpu.CompilerParams(vmem_limit_bytes=1 << 20),
        name="norm",
    )(*pieces)


def moments(
    core, clip_norm, own, other, w_enc, enc_first, enc_second, w_dec, dec_first, dec_second
):
    feats, width = w_enc.shape
    rows = block_rows(feats // 2, 192)
    half = feats // 2 // rows
    steps = 2 * half

    def kernel(core_ref, norm_ref, own_ref, other_ref, *refs):
        enc, dec, outs = refs[:3], refs[3:6], refs[6:]
        dir_refs, (first_out, second_out, square_ref) = outs[:2], outs[2:]
        factor = clip_limit / jnp.maximum(norm_ref[:1, :1], clip_limit)
        square_ref[...] = jnp.zeros_like(square_ref)
        start = core_ref[0] * half

        def place(i):
            return lax.rem(start + i, steps)

        def body(own, other, enc_first, enc_second, dec_first, dec_second, first_ref, second_ref):
            step = pl.program_id(0)
            at = pl.ds(pl.multiple_of(place(step) * rows, rows), rows)
            sides = ((enc[0], enc_first, enc_second), (dec[0], dec_first, dec_second))
            for plane, (weight, first, second) in enumerate(sides):
                clipped = jnp.where(step < half, own[plane], other[plane]) * factor
                first_new = beta_one * first[...] + (1.0 - beta_one) * clipped
                second_new = beta_two * second[...] + (1.0 - beta_two) * clipped * clipped
                first_ref[plane] = first_new
                second_ref[plane] = second_new
                scaled = second_new * (1.0 / (1.0 - beta_two**STEP))
                spread = scaled * lax.rsqrt(scaled) + adam_eps
                direction = (
                    first_new * (1.0 / (1.0 - beta_one**STEP)) * pltpu.reciprocal(spread)
                    + weight_decay * weight[at, :]
                )
                dir_refs[plane][at, :] = direction.astype(jnp.bfloat16)
                square_ref[plane] += fold(direction * direction)

        block = pl.BlockSpec((rows, width), lambda i: (place(i), 0))
        both = pl.BlockSpec((2, rows, width), lambda i: (0, place(i), 0))
        early = pl.BlockSpec((2, rows, width), lambda i: (0, jnp.minimum(i, half - 1), 0))
        late = pl.BlockSpec((2, rows, width), lambda i: (0, jnp.maximum(i - half, 0), 0))
        pltpu.emit_pipeline(
            body,
            grid=(steps,),
            in_specs=[early, late] + [block] * 4,
            out_specs=[both, both],
        )(own_ref, other_ref, enc[1], enc[2], dec[1], dec[2], first_out, second_out)

    full = (2, feats, width)
    return pl.pallas_call(
        kernel,
        in_specs=[pl.BlockSpec(memory_space=pltpu.SMEM), VMEM, PLACED, PLACED]
        + [VMEM, PLACED, PLACED] * 2,
        out_specs=[VMEM, VMEM, PLACED, PLACED, VMEM],
        out_shape=[
            pltpu.VMEM((feats, width), jnp.bfloat16),
            pltpu.VMEM((feats, width), jnp.bfloat16),
            pltpu.HBM(full, jnp.float32),
            pltpu.HBM(full, jnp.float32),
            jax.ShapeDtypeStruct((2, 8, 128), jnp.float32),
        ],
        compiler_params=pltpu.CompilerParams(vmem_limit_bytes=16 << 20),
        cost_estimate=pl.CostEstimate(
            flops=40 * feats * width,
            bytes_accessed=40 * feats * width,
            transcendentals=4 * feats * width,
        ),
        name="moments",
    )(
        core,
        clip_norm,
        in_hbm(own),
        other,
        in_vmem(w_enc),
        in_hbm(enc_first),
        in_hbm(enc_second),
        in_vmem(w_dec),
        in_hbm(dec_first),
        in_hbm(dec_second),
    )


def renew(sums, small, terms, clip_norm, directions, w_enc, w_dec, total_picks):
    feats, width = w_enc.shape
    rows = block_rows(feats, 256)

    count = len(sums)

    def kernel(*refs):
        sum_refs, small_refs, refs = refs[:count], refs[count : 2 * count], refs[2 * count :]
        term_ref, clip_ref, enc_dir, dec_dir, enc_ref, dec_ref, out_ref, row_ref = refs
        sums = paired([ref[...] for ref in sum_refs])
        small = paired([ref[...] for ref in small_refs])
        def total(values):
            return jnp.sum(values, keepdims=True).reshape(1, 1)

        norms = [jnp.sqrt(0.5 * total(small[2 + plane])) for plane in range(2)]
        steps = [jnp.sqrt(total(sums[plane])) for plane in range(2)]
        rates = [learn_rate * (norms[plane] / steps[plane]) for plane in range(2)]
        loss = term_ref[0, :1, :1] / total_picks + term_ref[1, :1, :1] * total(small[1])
        for i, value in enumerate((*norms, *steps, loss, clip_ref[:1, :1])):
            row_ref[i : i + 1, :] = jnp.broadcast_to(value, (1, 128))
        row_ref[6:, :] = jnp.zeros((2, 128), jnp.float32)

        def body(new_ref):
            at = pl.ds(pl.multiple_of(pl.program_id(0) * rows, rows), rows)
            new_ref[0] = enc_ref[at, :] - rates[0] * enc_dir[at, :].astype(jnp.float32)
            raw = dec_ref[at, :] - rates[1] * dec_dir[at, :].astype(jnp.float32)
            new_ref[1] = raw * lax.rsqrt(jnp.sum(raw * raw, 1, keepdims=True) + 1e-06)

        both = pl.BlockSpec((2, rows, width), lambda i: (0, i, 0))
        pltpu.emit_pipeline(body, grid=(feats // rows,), out_specs=[both])(out_ref)

    return pl.pallas_call(
        kernel,
        in_specs=[VMEM] * (2 * count + 6),
        out_specs=[PLACED, VMEM],
        out_shape=[
            pltpu.HBM((2, feats, width), jnp.float32),
            jax.ShapeDtypeStruct((8, 128), jnp.float32),
        ],
        compiler_params=pltpu.CompilerParams(vmem_limit_bytes=16 << 20),
        cost_estimate=pl.CostEstimate(
            flops=12 * w_enc.size, bytes_accessed=8 * w_enc.size, transcendentals=0
        ),
        name="renew",
    )(*sums, *small, terms, clip_norm, *map(in_vmem, directions), in_vmem(w_enc), in_vmem(w_dec))


def shards(
    resid_pre,
    token_ids,
    valid_mask,
    picked,
    norm_gains,
    norm_biases,
    qkv_w,
    out_w,
    fc_w,
    proj_w,
    layer_bias,
    wte,
    w_enc,
    enc_first,
    enc_second,
    b_enc,
    w_dec,
    dec_first,
    dec_second,
    b_dec,
):
    low = jnp.bfloat16
    count, seq_len, model_width = resid_pre.shape
    size = lax.axis_size("fsdp")
    mine = lax.axis_index("fsdp")
    pick_count = picked.shape[1]
    rest_count = seq_len - pick_count
    hidden_units = fc_w.shape[1]
    vocab_rows = wte.shape[0]
    total_picks = lax.axis_size("dp") * size * count * pick_count
    fc_b = layer_bias[4 * model_width : 4 * model_width + hidden_units]
    proj_b = layer_bias[4 * model_width + hidden_units :]

    grouped_picks = picked.reshape(size, count, pick_count)
    own_pick, own_rest, own_inputs = attention(
        resid_pre,
        lax.dynamic_index_in_dim(grouped_picks, mine, 0, keepdims=False),
        norm_gains,
        norm_biases,
        qkv_w,
        out_w,
        layer_bias.reshape(1, -1),
        b_dec.reshape(1, -1),
    )
    own_count = own_inputs.shape[0]

    me = mine.reshape(1).astype(jnp.int32)
    core = (lax.axis_index("dp") & 1).reshape(1).astype(jnp.int32)
    own_pick, picked, valid_mask = lax.optimization_barrier((own_pick, picked, valid_mask))
    masks = gather_copies(mask_rows(me, size, picked, valid_mask))
    tokens = join(gather_near(own_pick))
    tokens, own_rest = lax.optimization_barrier((tokens, own_rest))
    rest = gather_group(own_rest)
    all_pick = gather_copies(tokens)
    shares, weight_squares = encode(
        me, tokens, size, own_count, w_enc, w_dec, b_enc.reshape(1, -1)
    )
    shares, rest, token_ids, grouped_picks, masks = lax.optimization_barrier(
        (shares, rest, token_ids, grouped_picks, masks)
    )
    recon = jnp.sum(trade(shares).astype(jnp.float32), 0) + b_dec

    place = lax.broadcasted_iota(jnp.int32, (1, 1, 1, seq_len), 3)
    ids = token_ids.reshape(size, count, 1, seq_len)
    targets = jnp.sum(jnp.where(grouped_picks[..., None] + 1 == place, ids, 0), -1).reshape(-1)
    targets = targets - mine * vocab_rows
    here = (targets >= 0) & (targets < vocab_rows)
    target_rows = jnp.take(wte, jnp.clip(targets, 0, vocab_rows - 1), axis=0)
    target_rows = jnp.where(here[:, None], target_rows, jnp.zeros_like(target_rows))
    pick_mask, rest_mask, pick_marks, rest_marks, sparse_coef = mark_rows(masks)
    bias = b_enc.reshape(-1, 1)
    recon, target_rows, pick_marks, rest_marks, rest = lax.optimization_barrier(
        (recon, target_rows, pick_marks, rest_marks, rest)
    )
    far_rest = across(rest)

    mid = own_inputs + recon
    normed, second_norm_back = jax.vjp(
        lambda values: layer_norm(values, norm_gains[1], norm_biases[1]), mid
    )
    up_val = times(normed.astype(low), fc_w) + fc_b
    act, gelu_back = jax.vjp(lambda values: jax.nn.gelu(values, approximate=True), up_val)
    hidden = mid + times(act.astype(low), proj_w) + proj_b
    final, final_norm_back = jax.vjp(
        lambda values: layer_norm(values, norm_gains[2], norm_biases[2]), hidden
    )
    finals = gather_group(final.astype(low))
    all_feat, pick_sparse = feature_rows(
        core, all_pick, size * own_count, w_enc, bias, pick_mask
    )
    far_rest, all_feat = lax.optimization_barrier((far_rest, all_feat))
    finals, all_feat, far_rest = lax.optimization_barrier((finals, all_feat, far_rest))
    all_rest = spread(rest) + spread(far_rest)

    logits = times_trans(finals, wte)
    top = jnp.max(logits, 1)
    parts = jnp.exp(logits - top[:, None])
    mass = jnp.sum(parts, 1)
    at = jnp.sum(finals.astype(jnp.float32) * target_rows.astype(jnp.float32), 1)
    stats = trade(jnp.broadcast_to(jnp.stack([top, mass, at])[None], (size, 3, top.shape[0])))
    mixed = times(parts.astype(low), wte)
    stats, mixed = lax.optimization_barrier((stats, mixed))
    best = jnp.max(stats[:, 0], 0)
    total = jnp.sum(stats[:, 1] * jnp.exp(stats[:, 0] - best), 0)
    cross = jnp.sum(best + jnp.log(total) - jnp.sum(stats[:, 2], 0))
    scale = jnp.exp(top - best) / total
    dshares = (mixed * scale[:, None] - target_rows.astype(jnp.float32)) / total_picks
    dshares = dshares.astype(low).reshape(size, -1, model_width)
    cross = jnp.broadcast_to(cross, (1, 128))
    dshares, idle_marks, cross = lax.optimization_barrier((dshares, rest_marks, cross))
    bit = lax.axis_size("dp") // 2
    while bit:
        cross = cross + swap(cross, "dp", bit)
        bit //= 2
    dfinal = jnp.sum(trade(dshares).astype(jnp.float32), 0)
    idle, rest_sparse = idle_gradient(
        core, all_rest, size * own_count, w_enc, bias, rest_mask, idle_marks
    )
    dfinal, idle, pick_sparse, cross = lax.optimization_barrier((dfinal, idle, pick_sparse, cross))

    dhidden = final_norm_back(dfinal)[0]
    dact = times_trans(dhidden.astype(low), proj_w)
    dup_low = gelu_back(dact)[0].astype(low)
    dnormed = times_trans(dup_low, fc_w)
    drecon = (dhidden + second_norm_back(dnormed)[0]).astype(low)

    errors = join(gather_near(drecon))
    far_errors = across(errors)
    middle = len(all_pick) // 2
    near = gradients(
        core, all_pick[:middle], spread(errors), all_feat, 0, w_dec, pick_marks, idle
    )
    near, far_errors = lax.optimization_barrier((near, far_errors))
    own, squares = gradients(
        core, all_pick[middle:], spread(far_errors), all_feat, 1, w_dec, pick_marks, near
    )
    terms = jnp.stack([cross, sparse_coef])
    small = jnp.stack([squares, pick_sparse + rest_sparse, weight_squares[0], weight_squares[1]])
    small, own, terms = lax.optimization_barrier((small + swap(small, "dp", 1), own, terms))
    other = swap(own, "dp", 1)
    small = pieces_of(small)
    clip_norm = norm_of(small)
    *directions, firsts, seconds, squares = moments(
        core,
        clip_norm,
        own,
        other,
        w_enc,
        enc_first,
        enc_second,
        w_dec,
        dec_first,
        dec_second,
    )
    weights, rows = renew(
        pieces_of(squares), small, terms, clip_norm, directions, w_enc, w_dec, total_picks
    )
    return weights, firsts, seconds, rows[4, 0], rows[5, 0], rows[:2, 0], rows[2:4, 0]


def solution(mesh):
    in_specs = (
        P(("dp", "fsdp"), None, None),
        P("dp", None),
        P("dp", None),
        P("dp", None),
        P(),
        P(),
        P(),
        P(),
        P(),
        P(),
        P(),
        P("fsdp", None),
        P("fsdp", None),
        P("fsdp", None),
        P("fsdp", None),
        P("fsdp"),
        P("fsdp", None),
        P("fsdp", None),
        P("fsdp", None),
        P(),
    )
    out_specs = (
        P(None, "fsdp", None),
        P(None, "fsdp", None),
        P(None, "fsdp", None),
        P(),
        P(),
        P(),
        P(),
    )
    return jax.shard_map(shards, mesh=mesh, in_specs=in_specs, out_specs=out_specs, check_vma=False)
```

```python
import jax
import jax.numpy as jnp
from jax import lax
from jax.experimental import pallas as pl
from jax.experimental.pallas import tpu as pltpu
from jax.sharding import PartitionSpec as P

HEADS = 12
HEAD_DIM = 64
F = 24576
STEP = 10


norm_eps = 1e-05
l1_scale = 40.0
clip_limit = 0.02
learn_rate = 0.3
beta_one = 0.9
beta_two = 0.999
adam_eps = 1e-08
weight_decay = 0.01


def layer_norm(values, gain, shift):
    center = values - jnp.mean(values, -1, keepdims=True)
    spread = jnp.mean(center * center, -1, keepdims=True)
    return center * lax.rsqrt(spread + norm_eps) * gain + shift


def times(left, right):
    return jnp.dot(left, right, preferred_element_type=jnp.float32)


def times_trans(left, right):
    return lax.dot_general(
        left, right, (((1,), (1,)), ((), ())), preferred_element_type=jnp.float32
    )


def trans_times(left, right):
    return lax.dot_general(
        left, right, (((0,), (0,)), ((), ())), preferred_element_type=jnp.float32
    )


def swap(block, axis, bit):
    size = lax.axis_size(axis)
    return lax.ppermute(block, axis, [(i, i ^ bit) for i in range(size)])


def trade(blocks):
    return lax.all_to_all(blocks, "fsdp", 0, 0, tiled=True)


def gather_group(block):
    size = lax.axis_size("fsdp")
    spread = jnp.broadcast_to(block[None], (size, *block.shape))
    return trade(spread).reshape(-1, *block.shape[1:])


def gather_near(block):
    half = lax.axis_size("fsdp") // 2
    far = swap(block, "fsdp", half)
    near = [block] + [swap(block, "fsdp", k) for k in range(1, half)]
    return near + [far] + [swap(far, "fsdp", k) for k in range(1, half)]


def pieces_of(block):
    size = lax.axis_size("fsdp")
    return [block] + [swap(block, "fsdp", k) for k in range(1, size)]


def paired(pieces):
    while len(pieces) > 1:
        pieces = [a + b for a, b in zip(pieces[::2], pieces[1::2])]
    return pieces[0]


def across(block):
    return swap(block, "dp", lax.axis_size("dp") // 2)


def spread(block):
    blocks = [block]
    bit = lax.axis_size("dp") // 4
    while bit:
        blocks = blocks + [swap(held, "dp", bit) for held in blocks]
        bit //= 2
    return blocks


def gather_copies(block):
    return spread(block) + spread(across(block))


VMEM = pl.BlockSpec(memory_space=pltpu.VMEM)
PLACED = pl.BlockSpec(memory_space=pl.ANY)
ONCE = pl.Buffered(1)


def in_vmem(values):
    return pltpu.with_memory_space_constraint(values, pltpu.VMEM)


def in_hbm(values):
    return pltpu.with_memory_space_constraint(values, pltpu.HBM)


def fold(values):
    rows, width = values.shape
    total = jnp.sum(values.reshape(rows // 8, 8, width), 0)
    return sum(total[:, k : k + 128] for k in range(0, width, 128))


def block_rows(count, most):
    return max(rows for rows in range(16, most + 1, 16) if count % rows == 0)


def scalars(grid, in_specs, out_specs, scratch_shapes=()):
    return pltpu.PrefetchScalarGridSpec(
        num_scalar_prefetch=1,
        grid=grid,
        in_specs=in_specs,
        out_specs=out_specs,
        scratch_shapes=scratch_shapes,
    )


def attention(resid, picks, gains, shifts, qkv_w, out_w, layer_bias, b_dec):
    count, length, width = resid.shape
    pick_count = picks.shape[1]
    rest_count = length - pick_count
    pair = 2 * HEAD_DIM

    def kernel(
        resid_ref,
        pick_ref,
        gain_ref,
        shift_ref,
        qkv_ref,
        out_ref,
        bias_ref,
        dec_ref,
        rows_ref,
        rest_ref,
        inputs_ref,
    ):
        values = resid_ref[...].astype(jnp.float32).reshape(count * length, width)
        normed = layer_norm(values, gain_ref[:1, :], shift_ref[:1, :]).astype(jnp.bfloat16)
        packed = (times(normed, qkv_ref[...]) + bias_ref[:, : 3 * width]).astype(jnp.bfloat16)
        first = lax.broadcasted_iota(jnp.int32, (length, pair), 1) < HEAD_DIM
        row_ids = lax.broadcasted_iota(jnp.int32, (length, length), 0)
        col_ids = lax.broadcasted_iota(jnp.int32, (length, length), 1)
        causal = jnp.concatenate([row_ids >= col_ids] * 2, 0)
        contexts = []
        for s in range(count):
            at = slice(s * length, (s + 1) * length)
            pairs = []
            for lane in range(0, width, pair):
                query = packed[at, lane : lane + pair]
                key = packed[at, width + lane : width + lane + pair]
                value = packed[at, 2 * width + lane : 2 * width + lane + pair]
                zero = jnp.zeros_like(query)
                both = jnp.concatenate(
                    [jnp.where(first, query, zero), jnp.where(first, zero, query)], 0
                )
                scores = times_trans(both, key) * HEAD_DIM ** (-0.5)
                scores = jnp.where(causal, scores, -1e30)
                powers = jnp.exp(scores - jnp.max(scores, -1, keepdims=True))
                probs = (powers / jnp.sum(powers, -1, keepdims=True)).astype(jnp.bfloat16)
                mixed = times(probs, value)
                pairs.append(jnp.where(first, mixed[:length], mixed[length:]))
            contexts.append(jnp.concatenate(pairs, 1).astype(jnp.bfloat16))
        context = jnp.concatenate(contexts, 0)
        attn = times(context, out_ref[...]) + bias_ref[:, 3 * width : 4 * width]
        centered = (attn - dec_ref[...]).astype(jnp.bfloat16)
        after = (row_ids < col_ids).astype(jnp.float32)
        lanes = lax.broadcasted_iota(jnp.int32, (pick_count, length), 1)
        slots = lax.broadcasted_iota(jnp.int32, (rest_count, length), 0).astype(jnp.float32)
        for s in range(count):
            at = slice(s * length, (s + 1) * length)
            chosen = (pick_ref[s] == lanes).astype(jnp.float32)
            free = 1.0 - jnp.sum(chosen, 0, keepdims=True)
            rank = times(jnp.broadcast_to(free, (8, length)), after)[:1]
            others = jnp.where((rank == slots) & (free > 0), 1.0, 0.0).astype(jnp.bfloat16)
            chosen = chosen.astype(jnp.bfloat16)
            rows_ref[s * pick_count : (s + 1) * pick_count, :] = times(
                chosen, centered[at]
            ).astype(jnp.bfloat16)
            rest_ref[s * rest_count : (s + 1) * rest_count, :] = times(
                others, centered[at]
            ).astype(jnp.bfloat16)
            inputs_ref[s * pick_count : (s + 1) * pick_count, :] = times(chosen, resid_ref[s])

    return pl.pallas_call(
        kernel,
        in_specs=[VMEM] * 8,
        out_specs=[VMEM, VMEM, VMEM],
        out_shape=[
            jax.ShapeDtypeStruct((count * pick_count, width), jnp.bfloat16),
            jax.ShapeDtypeStruct((count * rest_count, width), jnp.bfloat16),
            jax.ShapeDtypeStruct((count * pick_count, width), jnp.float32),
        ],
        compiler_params=pltpu.CompilerParams(vmem_limit_bytes=32 << 20),
        cost_estimate=pl.CostEstimate(
            flops=8 * count * length * width * width,
            bytes_accessed=8 * width * width,
            transcendentals=count * length * width,
        ),
        name="attention",
    )(resid, picks[..., None], gains, shifts, qkv_w, out_w, layer_bias, b_dec)


def join(blocks):
    part, width = blocks[0].shape
    count = len(blocks)

    def kernel(*refs):
        for k in range(count):
            refs[count][k * part : (k + 1) * part, :] = refs[k][...]

    return pl.pallas_call(
        kernel,
        in_specs=[VMEM] * count,
        out_specs=VMEM,
        out_shape=jax.ShapeDtypeStruct((part * count, width), blocks[0].dtype),
        name="join",
    )(*blocks)


def mask_rows(mine, size, picked, valid_mask):
    count, pick_count = picked.shape
    length = valid_mask.shape[1]
    lanes = count * pick_count
    block = lanes // size

    def kernel(mine_ref, pick_ref, mask_ref, out_ref):
        def one(test):
            return jnp.where(test, 1.0, 0.0).astype(jnp.bfloat16)

        def ids(shape, dim):
            return lax.broadcasted_iota(jnp.int32, shape, dim)

        wide, square = (length, lanes), (lanes, lanes)
        chosen = one(pick_ref[...] == ids(wide, 0))
        group = one(ids(square, 0) // pick_count == ids(square, 1) // pick_count)
        free = 1.0 - times(chosen, group)
        before = one(ids((length, length), 0) > ids((length, length), 1))
        rank = times(before, free.astype(jnp.bfloat16))
        slot = lax.rem(ids(wide, 1), pick_count).astype(jnp.float32)
        others = jnp.where((rank == slot) & (free > 0), 1.0, 0.0)
        owner = one(ids((count, lanes), 0) == ids((count, lanes), 1) // pick_count)
        mask = trans_times(mask_ref[...].astype(jnp.bfloat16), owner)
        picks = jnp.sum(chosen.astype(jnp.float32) * mask, 0, keepdims=True)
        source, target = ids(square, 0), ids(square, 1)
        moved = one(
            (source // block == ((target // block) ^ mine_ref[0]))
            & (lax.rem(source, block) == lax.rem(target, block))
        )
        out_ref[:1, :] = times(picks.astype(jnp.bfloat16), moved)
        out_ref[1:, :] = jnp.sum(others * mask, 0, keepdims=True)

    return pl.pallas_call(
        kernel,
        in_specs=[pl.BlockSpec(memory_space=pltpu.SMEM), VMEM, VMEM],
        out_specs=VMEM,
        out_shape=jax.ShapeDtypeStruct((2, lanes), jnp.float32),
        compiler_params=pltpu.CompilerParams(vmem_limit_bytes=(8 << 20) + 12 * lanes * lanes),
        name="masks",
    )(mine, picked.reshape(1, -1), valid_mask)


def mark_rows(masks):
    count = len(masks)
    lanes = masks[0].shape[1]

    def kernel(*refs):
        pick_ref, rest_ref, pick_marks, rest_marks, coef_ref = refs[count:]
        total = sum(jnp.sum(ref[...], keepdims=True).reshape(1, 1) for ref in refs[:count])
        coef = l1_scale / F / total
        coef_ref[...] = jnp.broadcast_to(coef, (1, 128))
        for k in range(count):
            at = slice(k * lanes, (k + 1) * lanes)
            pick_ref[:, at] = refs[k][:1, :]
            rest_ref[:, at] = refs[k][1:, :]
            pick_marks[:, at] = refs[k][:1, :] * coef
            rest_marks[:, at] = refs[k][1:, :] * coef

    return pl.pallas_call(
        kernel,
        in_specs=[VMEM] * count,
        out_specs=[VMEM] * 5,
        out_shape=[jax.ShapeDtypeStruct((1, count * lanes), jnp.float32)] * 4
        + [jax.ShapeDtypeStruct((1, 128), jnp.float32)],
        name="marks",
    )(*masks)


def encode(mine, tokens, count, part, w_enc, w_dec, b_enc):
    width = tokens.shape[1]
    feats = w_enc.shape[0]
    rows = block_rows(feats, 1024)
    steps = feats // rows

    def kernel(mine_ref, token_ref, enc_ref, dec_ref, bias_ref, share_ref, square_ref, total_ref):

        @pl.when(pl.program_id(0) == 0)
        def _():
            square_ref[...] = jnp.zeros_like(square_ref)
            total_ref[...] = jnp.zeros_like(total_ref)

        enc, dec = enc_ref[...], dec_ref[...]
        square_ref[0] += fold(enc * enc)
        square_ref[1] += fold(dec * dec)
        enc_low, dec_low = enc.astype(jnp.bfloat16), dec.astype(jnp.bfloat16)
        features = jnp.maximum(times_trans(token_ref[...], enc_low) + bias_ref[...], 0.0)
        total_ref[...] += times(features.astype(jnp.bfloat16), dec_low)

        @pl.when(pl.program_id(0) == steps - 1)
        def _():
            for k in range(count):
                share_ref[mine_ref[0] ^ k] = total_ref[k * part : (k + 1) * part, :].astype(
                    jnp.bfloat16
                )

    whole = pl.BlockSpec((count * part, width), lambda i, s: (0, 0), pipeline_mode=ONCE)
    block = pl.BlockSpec((rows, width), lambda i, s: (i, 0))
    return pl.pallas_call(
        kernel,
        grid_spec=scalars(
            (steps,),
            [whole, block, block, pl.BlockSpec((1, rows), lambda i, s: (0, i))],
            [
                pl.BlockSpec((count, part, width), lambda i, s: (0, 0, 0)),
                pl.BlockSpec((2, 8, 128), lambda i, s: (0, 0, 0)),
            ],
            [pltpu.VMEM((count * part, width), jnp.float32)],
        ),
        out_shape=[
            jax.ShapeDtypeStruct((count, part, width), jnp.bfloat16),
            jax.ShapeDtypeStruct((2, 8, 128), jnp.float32),
        ],
        compiler_params=pltpu.CompilerParams(
            vmem_limit_bytes=(36 << 20) + 12 * count * part * width
        ),
        cost_estimate=pl.CostEstimate(
            flops=4 * feats * width * count * part, bytes_accessed=8 * feats * width, transcendentals=0
        ),
        name="encode",
    )(mine, in_hbm(tokens), in_hbm(w_enc), in_hbm(w_dec), b_enc)


def feature_rows(core, tokens, part, w_enc, bias, masks):
    count = len(tokens)
    width = tokens[0].shape[1]
    feats = w_enc.shape[0] // 2
    rows = block_rows(feats, 512 if part <= 512 else 128)
    steps = feats // rows

    def kernel(core_ref, *refs):
        token_refs = refs[:count]
        enc_ref, bias_ref, mask_ref, out_ref, sum_ref = refs[count:]

        @pl.when(pl.program_id(0) == 0)
        def _():
            sum_ref[...] = jnp.zeros_like(sum_ref)

        enc = enc_ref[...].astype(jnp.bfloat16)
        for k in range(count):
            at = pl.ds(k * part, part)
            pre = times_trans(enc, token_refs[k][...]) + bias_ref[...]
            kept = jnp.maximum(pre, 0.0)
            out_ref[:, at] = kept.astype(jnp.bfloat16)
            sum_ref[...] += fold(kept * mask_ref[:, at])

    whole = pl.BlockSpec((part, width), lambda i, s: (0, 0), pipeline_mode=ONCE)
    return pl.pallas_call(
        kernel,
        grid_spec=scalars(
            (steps,),
            [whole] * count
            + [
                pl.BlockSpec((rows, width), lambda i, s: (s[0] * steps + i, 0)),
                pl.BlockSpec((rows, 1), lambda i, s: (s[0] * steps + i, 0)),
                pl.BlockSpec((1, count * part), lambda i, s: (0, 0)),
            ],
            [
                pl.BlockSpec((rows, count * part), lambda i, s: (i, 0)),
                pl.BlockSpec((8, 128), lambda i, s: (0, 0)),
            ],
        ),
        out_shape=[
            pltpu.HBM((feats, count * part), jnp.bfloat16),
            jax.ShapeDtypeStruct((8, 128), jnp.float32),
        ],
        compiler_params=pltpu.CompilerParams(
            vmem_limit_bytes=(24 << 20) + 2 * count * part * width
        ),
        cost_estimate=pl.CostEstimate(
            flops=2 * feats * width * count * part,
            bytes_accessed=2 * (feats + width) * count * part + 2 * feats * width,
            transcendentals=0,
        ),
        name="features",
    )(core, *map(in_hbm, tokens), in_hbm(w_enc), bias, masks)


def idle_gradient(core, tokens, part, w_enc, bias, masks, marks):
    count = len(tokens)
    width = tokens[0].shape[1]
    feats = w_enc.shape[0] // 2
    rows = block_rows(feats, 512 if part <= 512 else 128)
    steps = feats // rows

    def kernel(core_ref, *refs):
        token_refs = refs[:count]
        enc_ref, bias_ref, mask_ref, mark_ref, out_ref, sum_ref = refs[count:]

        @pl.when(pl.program_id(0) == 0)
        def _():
            sum_ref[...] = jnp.zeros_like(sum_ref)

        grad = jnp.zeros(out_ref.shape, jnp.float32)
        enc = enc_ref[...].astype(jnp.bfloat16)
        for k in range(count):
            at = pl.ds(k * part, part)
            pre = times_trans(enc, token_refs[k][...]) + bias_ref[...]
            sum_ref[...] += fold(jnp.maximum(pre, 0.0) * mask_ref[:, at])
            dpre = jnp.where(pre > 0, mark_ref[:, at], 0.0).astype(jnp.bfloat16)
            grad = grad + times(dpre, token_refs[k][...])
        out_ref[...] = grad

    whole = pl.BlockSpec((part, width), lambda i, s: (0, 0), pipeline_mode=ONCE)
    row = pl.BlockSpec((1, count * part), lambda i, s: (0, 0))
    return pl.pallas_call(
        kernel,
        grid_spec=scalars(
            (steps,),
            [whole] * count
            + [
                pl.BlockSpec((rows, width), lambda i, s: (s[0] * steps + i, 0)),
                pl.BlockSpec((rows, 1), lambda i, s: (s[0] * steps + i, 0)),
                row,
                row,
            ],
            [
                pl.BlockSpec((rows, width), lambda i, s: (i, 0)),
                pl.BlockSpec((8, 128), lambda i, s: (0, 0)),
            ],
        ),
        out_shape=[
            pltpu.HBM((feats, width), jnp.float32),
            jax.ShapeDtypeStruct((8, 128), jnp.float32),
        ],
        compiler_params=pltpu.CompilerParams(
            vmem_limit_bytes=(24 << 20) + 2 * count * part * width
        ),
        cost_estimate=pl.CostEstimate(
            flops=4 * feats * width * count * part,
            bytes_accessed=2 * width * count * part + 6 * feats * width,
            transcendentals=0,
        ),
        name="idle",
    )(core, *map(in_hbm, tokens), in_hbm(w_enc), bias, masks, marks)


def gradients(core, tokens, errors, features, side, w_dec, marks, start):
    count = len(tokens)
    part, width = errors[0].shape
    feats = w_dec.shape[0] // 2
    rows = block_rows(feats, 256 if part <= 512 else 128)
    steps = feats // rows

    def kernel(core_ref, *refs):
        token_refs, error_refs = refs[:count], refs[count : 2 * count]
        feat_ref, dec_ref, mark_ref, start_ref, out_ref, *square_ref = refs[2 * count :]
        weight = dec_ref[...].astype(jnp.bfloat16)
        if side:
            enc, dec = start_ref[0], start_ref[1]
        else:
            enc, dec = start_ref[...], jnp.zeros((rows, width), jnp.float32)
        for k in range(count):
            at = pl.ds(k * part, part)
            feat = feat_ref[:, at]
            dfeat = times_trans(weight, error_refs[k][...]) + mark_ref[:, at]
            dpre = jnp.where(feat > 0, dfeat, 0.0).astype(jnp.bfloat16)
            enc = enc + times(dpre, token_refs[k][...])
            dec = dec + times(feat, error_refs[k][...])
        out_ref[0] = enc
        out_ref[1] = dec
        if side:

            @pl.when(pl.program_id(0) == 0)
            def _():
                square_ref[0][...] = jnp.zeros_like(square_ref[0])

            square_ref[0][...] += fold(enc * enc) + fold(dec * dec)

    whole = pl.BlockSpec((part, width), lambda i, s: (0, 0), pipeline_mode=ONCE)
    both = pl.BlockSpec((2, rows, width), lambda i, s: (0, i, 0))
    block = pl.BlockSpec((rows, width), lambda i, s: (i, 0))
    out_specs = [both] + [pl.BlockSpec((8, 128), lambda i, s: (0, 0))] * side
    out_shape = [pltpu.HBM((2, feats, width), jnp.float32)]
    out_shape = out_shape + [jax.ShapeDtypeStruct((8, 128), jnp.float32)] * side
    outs = pl.pallas_call(
        kernel,
        grid_spec=scalars(
            (steps,),
            [whole] * (2 * count)
            + [
                pl.BlockSpec((rows, count * part), lambda i, s: (i, side)),
                pl.BlockSpec((rows, width), lambda i, s: (s[0] * steps + i, 0)),
                pl.BlockSpec((1, count * part), lambda i, s: (0, side)),
                both if side else block,
            ],
            out_specs,
        ),
        out_shape=out_shape,
        compiler_params=pltpu.CompilerParams(
            vmem_limit_bytes=(18 << 20) + 4 * count * part * width
        ),
        cost_estimate=pl.CostEstimate(
            flops=6 * feats * width * count * part,
            bytes_accessed=(2 * feats + 4 * width) * count * part + 20 * feats * width,
            transcendentals=0,
        ),
        name="gradients",
    )(
        core,
        *map(in_hbm, tokens),
        *map(in_hbm, errors),
        in_hbm(features),
        in_hbm(w_dec),
        marks,
        in_hbm(start),
    )
    return outs if side else outs[0]


def norm_of(pieces):
    def kernel(*refs):
        total = jnp.sum(paired([ref[0] for ref in refs[:-1]]), keepdims=True).reshape(1, 1)
        refs[-1][...] = jnp.broadcast_to(jnp.sqrt(total), refs[-1].shape)

    return pl.pallas_call(
        kernel,
        in_specs=[VMEM] * len(pieces),
        out_specs=VMEM,
        out_shape=jax.ShapeDtypeStruct((8, 128), jnp.float32),
        compiler_params=pltpu.CompilerParams(vmem_limit_bytes=1 << 20),
        name="norm",
    )(*pieces)


def moments(
    size, core, clip_norm, own, other, w_enc, enc_first, enc_second, w_dec, dec_first, dec_second
):
    feats, width = w_enc.shape
    rows = block_rows(feats // 2, 256)
    half = feats // 2 // rows
    steps = 2 * half

    def kernel(core_ref, norm_ref, own_ref, other_ref, *refs):
        enc, dec, outs = refs[:3], refs[3:6], refs[6:]
        dir_refs, (first_out, second_out, square_ref) = outs[:2], outs[2:]
        factor = clip_limit / jnp.maximum(norm_ref[:1, :1], clip_limit)
        square_ref[...] = jnp.zeros_like(square_ref)
        start = core_ref[0] * half

        def place(i):
            return lax.rem(start + i, steps)

        def body(own, enc_first, enc_second, dec_first, dec_second, first_ref, second_ref):
            step = pl.program_id(0)
            at = pl.ds(pl.multiple_of(place(step) * rows, rows), rows)
            back = pl.ds(pl.multiple_of(jnp.maximum(step - half, 0) * rows, rows), rows)
            sides = ((enc[0], enc_first, enc_second), (dec[0], dec_first, dec_second))
            for plane, (weight, first, second) in enumerate(sides):
                clipped = jnp.where(step < half, own[plane], other_ref[plane, back, :]) * factor
                first_new = beta_one * first[...] + (1.0 - beta_one) * clipped
                second_new = beta_two * second[...] + (1.0 - beta_two) * clipped * clipped
                first_ref[plane] = first_new
                second_ref[plane] = second_new
                scaled = second_new * (1.0 / (1.0 - beta_two**STEP))
                spread = scaled * lax.rsqrt(scaled) + adam_eps
                direction = (
                    first_new * (1.0 / (1.0 - beta_one**STEP)) * pltpu.reciprocal(spread)
                    + weight_decay * weight[at, :]
                )
                dir_refs[plane][at, :] = direction.astype(jnp.bfloat16)
                square_ref[:, plane] += jnp.broadcast_to(
                    fold(direction * direction)[None], (size, 8, 128)
                )

        block = pl.BlockSpec((rows, width), lambda i: (place(i), 0))
        both = pl.BlockSpec((2, rows, width), lambda i: (0, place(i), 0))
        early = pl.BlockSpec((2, rows, width), lambda i: (0, jnp.minimum(i, half - 1), 0))
        pltpu.emit_pipeline(
            body,
            grid=(steps,),
            in_specs=[early] + [block] * 4,
            out_specs=[both, both],
        )(own_ref, enc[1], enc[2], dec[1], dec[2], first_out, second_out)

    full = (2, feats, width)
    return pl.pallas_call(
        kernel,
        in_specs=[pl.BlockSpec(memory_space=pltpu.SMEM), VMEM, PLACED, VMEM]
        + [VMEM, PLACED, PLACED] * 2,
        out_specs=[VMEM, VMEM, PLACED, PLACED, VMEM],
        out_shape=[
            pltpu.VMEM((feats, width), jnp.bfloat16),
            pltpu.VMEM((feats, width), jnp.bfloat16),
            pltpu.HBM(full, jnp.float32),
            pltpu.HBM(full, jnp.float32),
            jax.ShapeDtypeStruct((size, 2, 8, 128), jnp.float32),
        ],
        compiler_params=pltpu.CompilerParams(vmem_limit_bytes=18 << 20),
        cost_estimate=pl.CostEstimate(
            flops=40 * feats * width,
            bytes_accessed=40 * feats * width,
            transcendentals=4 * feats * width,
        ),
        name="moments",
    )(
        core,
        clip_norm,
        in_hbm(own),
        in_vmem(other),
        in_vmem(w_enc),
        in_hbm(enc_first),
        in_hbm(enc_second),
        in_vmem(w_dec),
        in_hbm(dec_first),
        in_hbm(dec_second),
    )


def renew(sums, small, terms, clip_norm, directions, w_enc, w_dec, total_picks):
    feats, width = w_enc.shape
    rows = block_rows(feats, 512)

    count = len(small)

    def kernel(*refs):
        sum_refs, small_refs, refs = refs[:1], refs[1 : count + 1], refs[count + 1 :]
        term_ref, clip_ref, enc_dir, dec_dir, enc_ref, dec_ref, out_ref, row_ref = refs
        sums = paired([sum_refs[0][k] for k in range(count)])
        small = paired([ref[...] for ref in small_refs])
        def total(values):
            return jnp.sum(values, keepdims=True).reshape(1, 1)

        norms = [jnp.sqrt(0.5 * total(small[2 + plane])) for plane in range(2)]
        steps = [jnp.sqrt(total(sums[plane])) for plane in range(2)]
        rates = [learn_rate * (norms[plane] / steps[plane]) for plane in range(2)]
        loss = term_ref[0, :1, :1] / total_picks + term_ref[1, :1, :1] * total(small[1])
        for i, value in enumerate((*norms, *steps, loss, clip_ref[:1, :1])):
            row_ref[i : i + 1, :] = jnp.broadcast_to(value, (1, 128))
        row_ref[6:, :] = jnp.zeros((2, 128), jnp.float32)

        def body(new_ref):
            at = pl.ds(pl.multiple_of(pl.program_id(0) * rows, rows), rows)
            new_ref[0] = enc_ref[at, :] - rates[0] * enc_dir[at, :].astype(jnp.float32)
            raw = dec_ref[at, :] - rates[1] * dec_dir[at, :].astype(jnp.float32)
            new_ref[1] = raw * lax.rsqrt(jnp.sum(raw * raw, 1, keepdims=True) + 1e-06)

        both = pl.BlockSpec((2, rows, width), lambda i: (0, i, 0))
        pltpu.emit_pipeline(body, grid=(feats // rows,), out_specs=[both])(out_ref)

    return pl.pallas_call(
        kernel,
        in_specs=[VMEM] * (count + 7),
        out_specs=[PLACED, VMEM],
        out_shape=[
            pltpu.HBM((2, feats, width), jnp.float32),
            jax.ShapeDtypeStruct((8, 128), jnp.float32),
        ],
        compiler_params=pltpu.CompilerParams(vmem_limit_bytes=16 << 20),
        cost_estimate=pl.CostEstimate(
            flops=12 * w_enc.size, bytes_accessed=8 * w_enc.size, transcendentals=0
        ),
        name="renew",
    )(sums, *small, terms, clip_norm, *map(in_vmem, directions), in_vmem(w_enc), in_vmem(w_dec))


def shards(
    resid_pre,
    token_ids,
    valid_mask,
    picked,
    norm_gains,
    norm_biases,
    qkv_w,
    out_w,
    fc_w,
    proj_w,
    layer_bias,
    wte,
    w_enc,
    enc_first,
    enc_second,
    b_enc,
    w_dec,
    dec_first,
    dec_second,
    b_dec,
):
    low = jnp.bfloat16
    count, seq_len, model_width = resid_pre.shape
    size = lax.axis_size("fsdp")
    mine = lax.axis_index("fsdp")
    pick_count = picked.shape[1]
    rest_count = seq_len - pick_count
    hidden_units = fc_w.shape[1]
    vocab_rows = wte.shape[0]
    total_picks = lax.axis_size("dp") * size * count * pick_count
    fc_b = layer_bias[4 * model_width : 4 * model_width + hidden_units]
    proj_b = layer_bias[4 * model_width + hidden_units :]

    grouped_picks = picked.reshape(size, count, pick_count)
    own_pick, own_rest, own_inputs = attention(
        resid_pre,
        lax.dynamic_index_in_dim(grouped_picks, mine, 0, keepdims=False),
        norm_gains,
        norm_biases,
        qkv_w,
        out_w,
        layer_bias.reshape(1, -1),
        b_dec.reshape(1, -1),
    )
    own_count = own_inputs.shape[0]

    me = mine.reshape(1).astype(jnp.int32)
    core = (lax.axis_index("dp") & 1).reshape(1).astype(jnp.int32)
    own_pick, picked, valid_mask = lax.optimization_barrier((own_pick, picked, valid_mask))
    masks = mask_rows(me, size, picked, valid_mask)
    tokens = join(gather_near(own_pick))
    tokens, own_rest = lax.optimization_barrier((tokens, own_rest))
    rest = gather_group(own_rest)
    all_pick = gather_copies(tokens)
    shares, weight_squares = encode(
        me, tokens, size, own_count, w_enc, w_dec, b_enc.reshape(1, -1)
    )
    shares, rest, token_ids, grouped_picks, masks = lax.optimization_barrier(
        (shares, rest, token_ids, grouped_picks, masks)
    )
    masks = gather_copies(masks)
    recon = jnp.sum(trade(shares).astype(jnp.float32), 0) + b_dec

    place = lax.broadcasted_iota(jnp.int32, (1, 1, 1, seq_len), 3)
    ids = token_ids.reshape(size, count, 1, seq_len)
    targets = jnp.sum(jnp.where(grouped_picks[..., None] + 1 == place, ids, 0), -1).reshape(-1)
    targets = targets - mine * vocab_rows
    here = (targets >= 0) & (targets < vocab_rows)
    target_rows = jnp.take(wte, jnp.clip(targets, 0, vocab_rows - 1), axis=0)
    target_rows = jnp.where(here[:, None], target_rows, jnp.zeros_like(target_rows))
    pick_mask, rest_mask, pick_marks, rest_marks, sparse_coef = mark_rows(masks)
    bias = b_enc.reshape(-1, 1)
    recon, target_rows, pick_marks, rest_marks, rest = lax.optimization_barrier(
        (recon, target_rows, pick_marks, rest_marks, rest)
    )
    far_rest = across(rest)

    mid = own_inputs + recon
    normed, second_norm_back = jax.vjp(
        lambda values: layer_norm(values, norm_gains[1], norm_biases[1]), mid
    )
    up_val = times(normed.astype(low), fc_w) + fc_b
    act, gelu_back = jax.vjp(lambda values: jax.nn.gelu(values, approximate=True), up_val)
    hidden = mid + times(act.astype(low), proj_w) + proj_b
    final, final_norm_back = jax.vjp(
        lambda values: layer_norm(values, norm_gains[2], norm_biases[2]), hidden
    )
    finals = gather_group(final.astype(low))
    all_feat, pick_sparse = feature_rows(
        core, all_pick, size * own_count, w_enc, bias, pick_mask
    )
    far_rest, all_feat = lax.optimization_barrier((far_rest, all_feat))
    finals, all_feat, far_rest = lax.optimization_barrier((finals, all_feat, far_rest))
    all_rest = spread(rest) + spread(far_rest)

    logits = times_trans(finals, wte)
    top = jnp.max(logits, 1)
    parts = jnp.exp(logits - top[:, None])
    mass = jnp.sum(parts, 1)
    at = jnp.sum(finals.astype(jnp.float32) * target_rows.astype(jnp.float32), 1)
    stats = trade(jnp.broadcast_to(jnp.stack([top, mass, at])[None], (size, 3, top.shape[0])))
    mixed = times(parts.astype(low), wte)
    stats, mixed = lax.optimization_barrier((stats, mixed))
    best = jnp.max(stats[:, 0], 0)
    total = jnp.sum(stats[:, 1] * jnp.exp(stats[:, 0] - best), 0)
    cross = jnp.sum(best + jnp.log(total) - jnp.sum(stats[:, 2], 0))
    scale = jnp.exp(top - best) / total
    dshares = (mixed * scale[:, None] - target_rows.astype(jnp.float32)) / total_picks
    dshares = dshares.astype(low).reshape(size, -1, model_width)
    cross = jnp.broadcast_to(cross, (1, 128))
    dshares, idle_marks, cross = lax.optimization_barrier((dshares, rest_marks, cross))
    bit = lax.axis_size("dp") // 2
    while bit:
        cross = cross + swap(cross, "dp", bit)
        bit //= 2
    dfinal = jnp.sum(trade(dshares).astype(jnp.float32), 0)
    idle, rest_sparse = idle_gradient(
        core, all_rest, size * own_count, w_enc, bias, rest_mask, idle_marks
    )
    dfinal, idle, pick_sparse, cross = lax.optimization_barrier((dfinal, idle, pick_sparse, cross))

    dhidden = final_norm_back(dfinal)[0]
    dact = times_trans(dhidden.astype(low), proj_w)
    dup_low = gelu_back(dact)[0].astype(low)
    dnormed = times_trans(dup_low, fc_w)
    drecon = (dhidden + second_norm_back(dnormed)[0]).astype(low)

    errors = join(gather_near(drecon))
    far_errors = across(errors)
    middle = len(all_pick) // 2
    near = gradients(
        core, all_pick[:middle], spread(errors), all_feat, 0, w_dec, pick_marks, idle
    )
    near, far_errors = lax.optimization_barrier((near, far_errors))
    own, squares = gradients(
        core, all_pick[middle:], spread(far_errors), all_feat, 1, w_dec, pick_marks, near
    )
    terms = jnp.stack([cross, sparse_coef])
    small = jnp.stack([squares, pick_sparse + rest_sparse, weight_squares[0], weight_squares[1]])
    small, own, terms = lax.optimization_barrier((small + swap(small, "dp", 1), own, terms))
    other = swap(own, "dp", 1)
    small = pieces_of(small)
    clip_norm = norm_of(small)
    *directions, firsts, seconds, squares = moments(
        size,
        core,
        clip_norm,
        own,
        other,
        w_enc,
        enc_first,
        enc_second,
        w_dec,
        dec_first,
        dec_second,
    )
    weights, rows = renew(
        trade(squares), small, terms, clip_norm, directions, w_enc, w_dec, total_picks
    )
    return weights, firsts, seconds, rows[4, 0], rows[5, 0], rows[:2, 0], rows[2:4, 0]


def solution(mesh):
    in_specs = (
        P(("dp", "fsdp"), None, None),
        P("dp", None),
        P("dp", None),
        P("dp", None),
        P(),
        P(),
        P(),
        P(),
        P(),
        P(),
        P(),
        P("fsdp", None),
        P("fsdp", None),
        P("fsdp", None),
        P("fsdp", None),
        P("fsdp"),
        P("fsdp", None),
        P("fsdp", None),
        P("fsdp", None),
        P(),
    )
    out_specs = (
        P(None, "fsdp", None),
        P(None, "fsdp", None),
        P(None, "fsdp", None),
        P(),
        P(),
        P(),
        P(),
    )
    return jax.shard_map(shards, mesh=mesh, in_specs=in_specs, out_specs=out_specs, check_vma=False)
```

```python
import jax
import jax.numpy as jnp
from jax import lax
from jax.experimental import pallas as pl
from jax.experimental.pallas import tpu as pltpu
from jax.sharding import PartitionSpec as P

HEADS = 12
HEAD_DIM = 64
F = 24576
STEP = 10


norm_eps = 1e-05
l1_scale = 40.0
clip_limit = 0.02
learn_rate = 0.3
beta_one = 0.9
beta_two = 0.999
adam_eps = 1e-08
weight_decay = 0.01


def layer_norm(values, gain, shift):
    center = values - jnp.mean(values, -1, keepdims=True)
    spread = jnp.mean(center * center, -1, keepdims=True)
    return center * lax.rsqrt(spread + norm_eps) * gain + shift


def times(left, right):
    return jnp.dot(left, right, preferred_element_type=jnp.float32)


def times_trans(left, right):
    return lax.dot_general(
        left, right, (((1,), (1,)), ((), ())), preferred_element_type=jnp.float32
    )


def trans_times(left, right):
    return lax.dot_general(
        left, right, (((0,), (0,)), ((), ())), preferred_element_type=jnp.float32
    )


def swap(block, axis, bit):
    size = lax.axis_size(axis)
    return lax.ppermute(block, axis, [(i, i ^ bit) for i in range(size)])


def trade(blocks):
    return lax.all_to_all(blocks, "fsdp", 0, 0, tiled=True)


def gather_group(block):
    size = lax.axis_size("fsdp")
    spread = jnp.broadcast_to(block[None], (size, *block.shape))
    return trade(spread).reshape(-1, *block.shape[1:])


def gather_halves(own, far):
    size = lax.axis_size("fsdp")
    half = size // 2
    both = jnp.concatenate([own, far], 0)
    groups = [list(range(half)), list(range(half, size))]
    blocks = lax.all_to_all(
        jnp.broadcast_to(both[None], (half, *both.shape)),
        "fsdp",
        0,
        0,
        axis_index_groups=groups,
        tiled=True,
    )
    return blocks.reshape(-1, both.shape[1])


def gather_near(block):
    half = lax.axis_size("fsdp") // 2
    far = swap(block, "fsdp", half)
    near = [block] + [swap(block, "fsdp", k) for k in range(1, half)]
    return near + [far] + [swap(far, "fsdp", k) for k in range(1, half)]


def pieces_of(block):
    size = lax.axis_size("fsdp")
    return [block] + [swap(block, "fsdp", k) for k in range(1, size)]


def paired(pieces):
    while len(pieces) > 1:
        pieces = [a + b for a, b in zip(pieces[::2], pieces[1::2])]
    return pieces[0]


def across(block):
    return swap(block, "dp", lax.axis_size("dp") // 2)


def spread(block):
    blocks = [block]
    bit = lax.axis_size("dp") // 4
    while bit:
        blocks = blocks + [swap(held, "dp", bit) for held in blocks]
        bit //= 2
    return blocks


def gather_copies(block):
    return spread(block) + spread(across(block))


VMEM = pl.BlockSpec(memory_space=pltpu.VMEM)
PLACED = pl.BlockSpec(memory_space=pl.ANY)
ONCE = pl.Buffered(1)


def in_vmem(values):
    return pltpu.with_memory_space_constraint(values, pltpu.VMEM)


def in_hbm(values):
    return pltpu.with_memory_space_constraint(values, pltpu.HBM)


def fold(values):
    rows, width = values.shape
    total = jnp.sum(values.reshape(rows // 8, 8, width), 0)
    return sum(total[:, k : k + 128] for k in range(0, width, 128))


def block_rows(count, most):
    return max(rows for rows in range(16, most + 1, 16) if count % rows == 0)


def scalars(grid, in_specs, out_specs, scratch_shapes=()):
    return pltpu.PrefetchScalarGridSpec(
        num_scalar_prefetch=1,
        grid=grid,
        in_specs=in_specs,
        out_specs=out_specs,
        scratch_shapes=scratch_shapes,
    )


def attention(resid, picks, gains, shifts, qkv_w, out_w, layer_bias, b_dec):
    count, length, width = resid.shape
    pick_count = picks.shape[1]
    rest_count = length - pick_count
    pair = 2 * HEAD_DIM

    def kernel(
        resid_ref,
        pick_ref,
        gain_ref,
        shift_ref,
        qkv_ref,
        out_ref,
        bias_ref,
        dec_ref,
        rows_ref,
        rest_ref,
        inputs_ref,
    ):
        values = resid_ref[...].astype(jnp.float32).reshape(count * length, width)
        normed = layer_norm(values, gain_ref[:1, :], shift_ref[:1, :]).astype(jnp.bfloat16)
        packed = (times(normed, qkv_ref[...]) + bias_ref[:, : 3 * width]).astype(jnp.bfloat16)
        first = lax.broadcasted_iota(jnp.int32, (length, pair), 1) < HEAD_DIM
        row_ids = lax.broadcasted_iota(jnp.int32, (length, length), 0)
        col_ids = lax.broadcasted_iota(jnp.int32, (length, length), 1)
        causal = jnp.concatenate([row_ids >= col_ids] * 2, 0)
        contexts = []
        for s in range(count):
            at = slice(s * length, (s + 1) * length)
            pairs = []
            for lane in range(0, width, pair):
                query = packed[at, lane : lane + pair]
                key = packed[at, width + lane : width + lane + pair]
                value = packed[at, 2 * width + lane : 2 * width + lane + pair]
                zero = jnp.zeros_like(query)
                both = jnp.concatenate(
                    [jnp.where(first, query, zero), jnp.where(first, zero, query)], 0
                )
                scores = times_trans(both, key) * HEAD_DIM ** (-0.5)
                scores = jnp.where(causal, scores, -1e30)
                powers = jnp.exp(scores - jnp.max(scores, -1, keepdims=True))
                probs = (powers / jnp.sum(powers, -1, keepdims=True)).astype(jnp.bfloat16)
                mixed = times(probs, value)
                pairs.append(jnp.where(first, mixed[:length], mixed[length:]))
            contexts.append(jnp.concatenate(pairs, 1).astype(jnp.bfloat16))
        context = jnp.concatenate(contexts, 0)
        attn = times(context, out_ref[...]) + bias_ref[:, 3 * width : 4 * width]
        centered = (attn - dec_ref[...]).astype(jnp.bfloat16)
        after = (row_ids < col_ids).astype(jnp.float32)
        lanes = lax.broadcasted_iota(jnp.int32, (pick_count, length), 1)
        slots = lax.broadcasted_iota(jnp.int32, (rest_count, length), 0).astype(jnp.float32)
        for s in range(count):
            at = slice(s * length, (s + 1) * length)
            chosen = (pick_ref[s] == lanes).astype(jnp.float32)
            free = 1.0 - jnp.sum(chosen, 0, keepdims=True)
            rank = times(jnp.broadcast_to(free, (8, length)), after)[:1]
            others = jnp.where((rank == slots) & (free > 0), 1.0, 0.0).astype(jnp.bfloat16)
            chosen = chosen.astype(jnp.bfloat16)
            rows_ref[s * pick_count : (s + 1) * pick_count, :] = times(
                chosen, centered[at]
            ).astype(jnp.bfloat16)
            rest_ref[s * rest_count : (s + 1) * rest_count, :] = times(
                others, centered[at]
            ).astype(jnp.bfloat16)
            inputs_ref[s * pick_count : (s + 1) * pick_count, :] = times(chosen, resid_ref[s])

    return pl.pallas_call(
        kernel,
        in_specs=[VMEM] * 8,
        out_specs=[VMEM, VMEM, VMEM],
        out_shape=[
            jax.ShapeDtypeStruct((count * pick_count, width), jnp.bfloat16),
            jax.ShapeDtypeStruct((count * rest_count, width), jnp.bfloat16),
            jax.ShapeDtypeStruct((count * pick_count, width), jnp.float32),
        ],
        compiler_params=pltpu.CompilerParams(vmem_limit_bytes=32 << 20),
        cost_estimate=pl.CostEstimate(
            flops=8 * count * length * width * width,
            bytes_accessed=8 * width * width,
            transcendentals=count * length * width,
        ),
        name="attention",
    )(resid, picks[..., None], gains, shifts, qkv_w, out_w, layer_bias, b_dec)


def join(blocks):
    part, width = blocks[0].shape
    count = len(blocks)

    def kernel(*refs):
        for k in range(count):
            refs[count][k * part : (k + 1) * part, :] = refs[k][...]

    return pl.pallas_call(
        kernel,
        in_specs=[VMEM] * count,
        out_specs=VMEM,
        out_shape=jax.ShapeDtypeStruct((part * count, width), blocks[0].dtype),
        name="join",
    )(*blocks)


def mask_rows(mine, size, picked, valid_mask):
    count, pick_count = picked.shape
    length = valid_mask.shape[1]
    lanes = count * pick_count
    block = lanes // size

    def kernel(mine_ref, pick_ref, mask_ref, out_ref):
        def one(test):
            return jnp.where(test, 1.0, 0.0).astype(jnp.bfloat16)

        def ids(shape, dim):
            return lax.broadcasted_iota(jnp.int32, shape, dim)

        wide, square = (length, lanes), (lanes, lanes)
        chosen = one(pick_ref[...] == ids(wide, 0))
        group = one(ids(square, 0) // pick_count == ids(square, 1) // pick_count)
        free = 1.0 - times(chosen, group)
        before = one(ids((length, length), 0) > ids((length, length), 1))
        rank = times(before, free.astype(jnp.bfloat16))
        slot = lax.rem(ids(wide, 1), pick_count).astype(jnp.float32)
        others = jnp.where((rank == slot) & (free > 0), 1.0, 0.0)
        owner = one(ids((count, lanes), 0) == ids((count, lanes), 1) // pick_count)
        mask = trans_times(mask_ref[...].astype(jnp.bfloat16), owner)
        picks = jnp.sum(chosen.astype(jnp.float32) * mask, 0, keepdims=True)
        source, target = ids(square, 0), ids(square, 1)
        moved = one(
            (source // block == ((target // block) ^ mine_ref[0]))
            & (lax.rem(source, block) == lax.rem(target, block))
        )
        out_ref[:1, :] = times(picks.astype(jnp.bfloat16), moved)
        rests = jnp.sum(others * mask, 0, keepdims=True)
        half = size // 2
        place = target // block
        mate = place // 2 + ((mine_ref[0] // half) ^ lax.rem(place, 2)) * half
        moved = one((source // block == mate) & (lax.rem(source, block) == lax.rem(target, block)))
        out_ref[1:, :] = times(rests.astype(jnp.bfloat16), moved)

    return pl.pallas_call(
        kernel,
        in_specs=[pl.BlockSpec(memory_space=pltpu.SMEM), VMEM, VMEM],
        out_specs=VMEM,
        out_shape=jax.ShapeDtypeStruct((2, lanes), jnp.float32),
        compiler_params=pltpu.CompilerParams(vmem_limit_bytes=(8 << 20) + 12 * lanes * lanes),
        name="masks",
    )(mine, picked.reshape(1, -1), valid_mask)


def mark_rows(masks):
    count = len(masks)
    lanes = masks[0].shape[1]

    def kernel(*refs):
        pick_ref, rest_ref, pick_marks, rest_marks, coef_ref = refs[count:]
        total = sum(jnp.sum(ref[...], keepdims=True).reshape(1, 1) for ref in refs[:count])
        coef = l1_scale / F / total
        coef_ref[...] = jnp.broadcast_to(coef, (1, 128))
        for k in range(count):
            at = slice(k * lanes, (k + 1) * lanes)
            pick_ref[:, at] = refs[k][:1, :]
            rest_ref[:, at] = refs[k][1:, :]
            pick_marks[:, at] = refs[k][:1, :] * coef
            rest_marks[:, at] = refs[k][1:, :] * coef

    return pl.pallas_call(
        kernel,
        in_specs=[VMEM] * count,
        out_specs=[VMEM] * 5,
        out_shape=[jax.ShapeDtypeStruct((1, count * lanes), jnp.float32)] * 4
        + [jax.ShapeDtypeStruct((1, 128), jnp.float32)],
        name="marks",
    )(*masks)


def encode(mine, tokens, count, part, w_enc, w_dec, b_enc):
    width = tokens.shape[1]
    feats = w_enc.shape[0]
    rows = block_rows(feats, 1024)
    steps = feats // rows

    def kernel(mine_ref, token_ref, enc_ref, dec_ref, bias_ref, share_ref, square_ref, total_ref):

        @pl.when(pl.program_id(0) == 0)
        def _():
            square_ref[...] = jnp.zeros_like(square_ref)
            total_ref[...] = jnp.zeros_like(total_ref)

        enc, dec = enc_ref[...], dec_ref[...]
        square_ref[0] += fold(enc * enc)
        square_ref[1] += fold(dec * dec)
        enc_low, dec_low = enc.astype(jnp.bfloat16), dec.astype(jnp.bfloat16)
        features = jnp.maximum(times_trans(token_ref[...], enc_low) + bias_ref[...], 0.0)
        total_ref[...] += times(features.astype(jnp.bfloat16), dec_low)

        @pl.when(pl.program_id(0) == steps - 1)
        def _():
            for k in range(count):
                share_ref[mine_ref[0] ^ k] = total_ref[k * part : (k + 1) * part, :].astype(
                    jnp.bfloat16
                )

    whole = pl.BlockSpec((count * part, width), lambda i, s: (0, 0), pipeline_mode=ONCE)
    block = pl.BlockSpec((rows, width), lambda i, s: (i, 0))
    return pl.pallas_call(
        kernel,
        grid_spec=scalars(
            (steps,),
            [whole, block, block, pl.BlockSpec((1, rows), lambda i, s: (0, i))],
            [
                pl.BlockSpec((count, part, width), lambda i, s: (0, 0, 0)),
                pl.BlockSpec((2, 8, 128), lambda i, s: (0, 0, 0)),
            ],
            [pltpu.VMEM((count * part, width), jnp.float32)],
        ),
        out_shape=[
            jax.ShapeDtypeStruct((count, part, width), jnp.bfloat16),
            jax.ShapeDtypeStruct((2, 8, 128), jnp.float32),
        ],
        compiler_params=pltpu.CompilerParams(
            vmem_limit_bytes=(36 << 20) + 12 * count * part * width
        ),
        cost_estimate=pl.CostEstimate(
            flops=4 * feats * width * count * part, bytes_accessed=8 * feats * width, transcendentals=0
        ),
        name="encode",
    )(mine, in_hbm(tokens), in_hbm(w_enc), in_hbm(w_dec), b_enc)


def feature_rows(core, tokens, part, w_enc, bias, masks):
    count = len(tokens)
    width = tokens[0].shape[1]
    feats = w_enc.shape[0] // 2
    rows = block_rows(feats, 512 if part <= 512 else 128)
    steps = feats // rows

    def kernel(core_ref, *refs):
        token_refs = refs[:count]
        enc_ref, bias_ref, mask_ref, out_ref, sum_ref = refs[count:]

        @pl.when(pl.program_id(0) == 0)
        def _():
            sum_ref[...] = jnp.zeros_like(sum_ref)

        enc = enc_ref[...].astype(jnp.bfloat16)
        for k in range(count):
            at = pl.ds(k * part, part)
            pre = times_trans(enc, token_refs[k][...]) + bias_ref[...]
            kept = jnp.maximum(pre, 0.0)
            out_ref[:, at] = kept.astype(jnp.bfloat16)
            sum_ref[...] += fold(kept * mask_ref[:, at])

    whole = pl.BlockSpec((part, width), lambda i, s: (0, 0), pipeline_mode=ONCE)
    return pl.pallas_call(
        kernel,
        grid_spec=scalars(
            (steps,),
            [whole] * count
            + [
                pl.BlockSpec((rows, width), lambda i, s: (s[0] * steps + i, 0)),
                pl.BlockSpec((rows, 1), lambda i, s: (s[0] * steps + i, 0)),
                pl.BlockSpec((1, count * part), lambda i, s: (0, 0)),
            ],
            [
                pl.BlockSpec((rows, count * part), lambda i, s: (i, 0)),
                pl.BlockSpec((8, 128), lambda i, s: (0, 0)),
            ],
        ),
        out_shape=[
            pltpu.HBM((feats, count * part), jnp.bfloat16),
            jax.ShapeDtypeStruct((8, 128), jnp.float32),
        ],
        compiler_params=pltpu.CompilerParams(
            vmem_limit_bytes=(24 << 20) + 2 * count * part * width
        ),
        cost_estimate=pl.CostEstimate(
            flops=2 * feats * width * count * part,
            bytes_accessed=2 * (feats + width) * count * part + 2 * feats * width,
            transcendentals=0,
        ),
        name="features",
    )(core, *map(in_hbm, tokens), in_hbm(w_enc), bias, masks)


def idle_gradient(core, tokens, part, w_enc, bias, masks, marks):
    count = len(tokens)
    width = tokens[0].shape[1]
    feats = w_enc.shape[0] // 2
    rows = block_rows(feats, 512 if part <= 512 else 128)
    steps = feats // rows

    def kernel(core_ref, *refs):
        token_refs = refs[:count]
        enc_ref, bias_ref, mask_ref, mark_ref, out_ref, sum_ref = refs[count:]

        @pl.when(pl.program_id(0) == 0)
        def _():
            sum_ref[...] = jnp.zeros_like(sum_ref)

        grad = jnp.zeros(out_ref.shape, jnp.float32)
        enc = enc_ref[...].astype(jnp.bfloat16)
        for k in range(count):
            at = pl.ds(k * part, part)
            pre = times_trans(enc, token_refs[k][...]) + bias_ref[...]
            sum_ref[...] += fold(jnp.maximum(pre, 0.0) * mask_ref[:, at])
            dpre = jnp.where(pre > 0, mark_ref[:, at], 0.0).astype(jnp.bfloat16)
            grad = grad + times(dpre, token_refs[k][...])
        out_ref[...] = grad

    whole = pl.BlockSpec((part, width), lambda i, s: (0, 0), pipeline_mode=ONCE)
    row = pl.BlockSpec((1, count * part), lambda i, s: (0, 0))
    return pl.pallas_call(
        kernel,
        grid_spec=scalars(
            (steps,),
            [whole] * count
            + [
                pl.BlockSpec((rows, width), lambda i, s: (s[0] * steps + i, 0)),
                pl.BlockSpec((rows, 1), lambda i, s: (s[0] * steps + i, 0)),
                row,
                row,
            ],
            [
                pl.BlockSpec((rows, width), lambda i, s: (i, 0)),
                pl.BlockSpec((8, 128), lambda i, s: (0, 0)),
            ],
        ),
        out_shape=[
            pltpu.HBM((feats, width), jnp.float32),
            jax.ShapeDtypeStruct((8, 128), jnp.float32),
        ],
        compiler_params=pltpu.CompilerParams(
            vmem_limit_bytes=(24 << 20) + 2 * count * part * width
        ),
        cost_estimate=pl.CostEstimate(
            flops=4 * feats * width * count * part,
            bytes_accessed=2 * width * count * part + 6 * feats * width,
            transcendentals=0,
        ),
        name="idle",
    )(core, *map(in_hbm, tokens), in_hbm(w_enc), bias, masks, marks)


def gradients(core, tokens, errors, features, side, w_dec, marks, start):
    count = len(tokens)
    part, width = errors[0].shape
    feats = w_dec.shape[0] // 2
    rows = block_rows(feats, 256 if part <= 512 else 128)
    steps = feats // rows

    def kernel(core_ref, *refs):
        token_refs, error_refs = refs[:count], refs[count : 2 * count]
        feat_ref, dec_ref, mark_ref, start_ref, out_ref, *square_ref = refs[2 * count :]
        weight = dec_ref[...].astype(jnp.bfloat16)
        if side:
            enc, dec = start_ref[0], start_ref[1]
        else:
            enc, dec = start_ref[...], jnp.zeros((rows, width), jnp.float32)
        for k in range(count):
            at = pl.ds(k * part, part)
            feat = feat_ref[:, at]
            dfeat = times_trans(weight, error_refs[k][...]) + mark_ref[:, at]
            dpre = jnp.where(feat > 0, dfeat, 0.0).astype(jnp.bfloat16)
            enc = enc + times(dpre, token_refs[k][...])
            dec = dec + times(feat, error_refs[k][...])
        out_ref[0] = enc
        out_ref[1] = dec
        if side:

            @pl.when(pl.program_id(0) == 0)
            def _():
                square_ref[0][...] = jnp.zeros_like(square_ref[0])

            square_ref[0][...] += fold(enc * enc) + fold(dec * dec)

    whole = pl.BlockSpec((part, width), lambda i, s: (0, 0), pipeline_mode=ONCE)
    both = pl.BlockSpec((2, rows, width), lambda i, s: (0, i, 0))
    block = pl.BlockSpec((rows, width), lambda i, s: (i, 0))
    out_specs = [both] + [pl.BlockSpec((8, 128), lambda i, s: (0, 0))] * side
    out_shape = [pltpu.HBM((2, feats, width), jnp.float32)]
    out_shape = out_shape + [jax.ShapeDtypeStruct((8, 128), jnp.float32)] * side
    outs = pl.pallas_call(
        kernel,
        grid_spec=scalars(
            (steps,),
            [whole] * (2 * count)
            + [
                pl.BlockSpec((rows, count * part), lambda i, s: (i, side)),
                pl.BlockSpec((rows, width), lambda i, s: (s[0] * steps + i, 0)),
                pl.BlockSpec((1, count * part), lambda i, s: (0, side)),
                both if side else block,
            ],
            out_specs,
        ),
        out_shape=out_shape,
        compiler_params=pltpu.CompilerParams(
            vmem_limit_bytes=(18 << 20) + 4 * count * part * width
        ),
        cost_estimate=pl.CostEstimate(
            flops=6 * feats * width * count * part,
            bytes_accessed=(2 * feats + 4 * width) * count * part + 20 * feats * width,
            transcendentals=0,
        ),
        name="gradients",
    )(
        core,
        *map(in_hbm, tokens),
        *map(in_hbm, errors),
        in_hbm(features),
        in_hbm(w_dec),
        marks,
        in_hbm(start),
    )
    return outs if side else outs[0]


def norm_of(pieces):
    def kernel(*refs):
        total = jnp.sum(paired([ref[0] for ref in refs[:-1]]), keepdims=True).reshape(1, 1)
        refs[-1][...] = jnp.broadcast_to(jnp.sqrt(total), refs[-1].shape)

    return pl.pallas_call(
        kernel,
        in_specs=[VMEM] * len(pieces),
        out_specs=VMEM,
        out_shape=jax.ShapeDtypeStruct((8, 128), jnp.float32),
        compiler_params=pltpu.CompilerParams(vmem_limit_bytes=1 << 20),
        name="norm",
    )(*pieces)


def moments(
    size, core, clip_norm, own, other, w_enc, enc_first, enc_second, w_dec, dec_first, dec_second
):
    feats, width = w_enc.shape
    rows = block_rows(feats // 2, 256)
    half = feats // 2 // rows
    steps = 2 * half

    def kernel(core_ref, norm_ref, own_ref, other_ref, *refs):
        enc, dec, outs = refs[:3], refs[3:6], refs[6:]
        dir_refs, (first_out, second_out, square_ref) = outs[:2], outs[2:]
        factor = clip_limit / jnp.maximum(norm_ref[:1, :1], clip_limit)
        square_ref[...] = jnp.zeros_like(square_ref)
        start = core_ref[0] * half

        def place(i):
            return lax.rem(start + i, steps)

        def body(own, enc_first, enc_second, dec_first, dec_second, first_ref, second_ref):
            step = pl.program_id(0)
            at = pl.ds(pl.multiple_of(place(step) * rows, rows), rows)
            back = pl.ds(pl.multiple_of(jnp.maximum(step - half, 0) * rows, rows), rows)
            sides = ((enc[0], enc_first, enc_second), (dec[0], dec_first, dec_second))
            for plane, (weight, first, second) in enumerate(sides):
                clipped = jnp.where(step < half, own[plane], other_ref[plane, back, :]) * factor
                first_new = beta_one * first[...] + (1.0 - beta_one) * clipped
                second_new = beta_two * second[...] + (1.0 - beta_two) * clipped * clipped
                first_ref[plane] = first_new
                second_ref[plane] = second_new
                scaled = second_new * (1.0 / (1.0 - beta_two**STEP))
                spread = scaled * lax.rsqrt(scaled) + adam_eps
                direction = (
                    first_new * (1.0 / (1.0 - beta_one**STEP)) * pltpu.reciprocal(spread)
                    + weight_decay * weight[at, :]
                )
                dir_refs[plane][at, :] = direction.astype(jnp.bfloat16)
                square_ref[:, plane] += jnp.broadcast_to(
                    fold(direction * direction)[None], (size, 8, 128)
                )

        block = pl.BlockSpec((rows, width), lambda i: (place(i), 0))
        both = pl.BlockSpec((2, rows, width), lambda i: (0, place(i), 0))
        early = pl.BlockSpec((2, rows, width), lambda i: (0, jnp.minimum(i, half - 1), 0))
        pltpu.emit_pipeline(
            body,
            grid=(steps,),
            in_specs=[early] + [block] * 4,
            out_specs=[both, both],
        )(own_ref, enc[1], enc[2], dec[1], dec[2], first_out, second_out)

    full = (2, feats, width)
    return pl.pallas_call(
        kernel,
        in_specs=[pl.BlockSpec(memory_space=pltpu.SMEM), VMEM, PLACED, VMEM]
        + [VMEM, PLACED, PLACED] * 2,
        out_specs=[VMEM, VMEM, PLACED, PLACED, VMEM],
        out_shape=[
            pltpu.VMEM((feats, width), jnp.bfloat16),
            pltpu.VMEM((feats, width), jnp.bfloat16),
            pltpu.HBM(full, jnp.float32),
            pltpu.HBM(full, jnp.float32),
            jax.ShapeDtypeStruct((size, 2, 8, 128), jnp.float32),
        ],
        compiler_params=pltpu.CompilerParams(vmem_limit_bytes=18 << 20),
        cost_estimate=pl.CostEstimate(
            flops=40 * feats * width,
            bytes_accessed=40 * feats * width,
            transcendentals=4 * feats * width,
        ),
        name="moments",
    )(
        core,
        clip_norm,
        in_hbm(own),
        in_vmem(other),
        in_vmem(w_enc),
        in_hbm(enc_first),
        in_hbm(enc_second),
        in_vmem(w_dec),
        in_hbm(dec_first),
        in_hbm(dec_second),
    )


def renew(sums, small, terms, clip_norm, directions, w_enc, w_dec, total_picks):
    feats, width = w_enc.shape
    rows = block_rows(feats, 512)

    count = len(small)

    def kernel(*refs):
        sum_refs, small_refs, refs = refs[:1], refs[1 : count + 1], refs[count + 1 :]
        term_ref, clip_ref, enc_dir, dec_dir, enc_ref, dec_ref, out_ref, row_ref = refs
        sums = paired([sum_refs[0][k] for k in range(count)])
        small = paired([ref[...] for ref in small_refs])
        def total(values):
            return jnp.sum(values, keepdims=True).reshape(1, 1)

        norms = [jnp.sqrt(0.5 * total(small[2 + plane])) for plane in range(2)]
        steps = [jnp.sqrt(total(sums[plane])) for plane in range(2)]
        rates = [learn_rate * (norms[plane] / steps[plane]) for plane in range(2)]
        loss = term_ref[0, :1, :1] / total_picks + term_ref[1, :1, :1] * total(small[1])
        for i, value in enumerate((*norms, *steps, loss, clip_ref[:1, :1])):
            row_ref[i : i + 1, :] = jnp.broadcast_to(value, (1, 128))
        row_ref[6:, :] = jnp.zeros((2, 128), jnp.float32)

        def body(new_ref):
            at = pl.ds(pl.multiple_of(pl.program_id(0) * rows, rows), rows)
            new_ref[0] = enc_ref[at, :] - rates[0] * enc_dir[at, :].astype(jnp.float32)
            raw = dec_ref[at, :] - rates[1] * dec_dir[at, :].astype(jnp.float32)
            new_ref[1] = raw * lax.rsqrt(jnp.sum(raw * raw, 1, keepdims=True) + 1e-06)

        both = pl.BlockSpec((2, rows, width), lambda i: (0, i, 0))
        pltpu.emit_pipeline(body, grid=(feats // rows,), out_specs=[both])(out_ref)

    return pl.pallas_call(
        kernel,
        in_specs=[VMEM] * (count + 7),
        out_specs=[PLACED, VMEM],
        out_shape=[
            pltpu.HBM((2, feats, width), jnp.float32),
            jax.ShapeDtypeStruct((8, 128), jnp.float32),
        ],
        compiler_params=pltpu.CompilerParams(vmem_limit_bytes=16 << 20),
        cost_estimate=pl.CostEstimate(
            flops=12 * w_enc.size, bytes_accessed=8 * w_enc.size, transcendentals=0
        ),
        name="renew",
    )(sums, *small, terms, clip_norm, *map(in_vmem, directions), in_vmem(w_enc), in_vmem(w_dec))


def shards(
    resid_pre,
    token_ids,
    valid_mask,
    picked,
    norm_gains,
    norm_biases,
    qkv_w,
    out_w,
    fc_w,
    proj_w,
    layer_bias,
    wte,
    w_enc,
    enc_first,
    enc_second,
    b_enc,
    w_dec,
    dec_first,
    dec_second,
    b_dec,
):
    low = jnp.bfloat16
    count, seq_len, model_width = resid_pre.shape
    size = lax.axis_size("fsdp")
    mine = lax.axis_index("fsdp")
    pick_count = picked.shape[1]
    rest_count = seq_len - pick_count
    hidden_units = fc_w.shape[1]
    vocab_rows = wte.shape[0]
    total_picks = lax.axis_size("dp") * size * count * pick_count
    fc_b = layer_bias[4 * model_width : 4 * model_width + hidden_units]
    proj_b = layer_bias[4 * model_width + hidden_units :]

    grouped_picks = picked.reshape(size, count, pick_count)
    own_pick, own_rest, own_inputs = attention(
        resid_pre,
        lax.dynamic_index_in_dim(grouped_picks, mine, 0, keepdims=False),
        norm_gains,
        norm_biases,
        qkv_w,
        out_w,
        layer_bias.reshape(1, -1),
        b_dec.reshape(1, -1),
    )
    own_count = own_inputs.shape[0]

    me = mine.reshape(1).astype(jnp.int32)
    core = (lax.axis_index("dp") & 1).reshape(1).astype(jnp.int32)
    own_pick, picked, valid_mask = lax.optimization_barrier((own_pick, picked, valid_mask))
    masks = mask_rows(me, size, picked, valid_mask)
    tokens = join(gather_near(own_pick))
    far_rest = swap(own_rest, "fsdp", size // 2)
    tokens, own_rest, far_rest = lax.optimization_barrier((tokens, own_rest, far_rest))
    rest = gather_halves(own_rest, far_rest)
    all_pick = gather_copies(tokens)
    shares, weight_squares = encode(
        me, tokens, size, own_count, w_enc, w_dec, b_enc.reshape(1, -1)
    )
    shares, rest, token_ids, grouped_picks, masks = lax.optimization_barrier(
        (shares, rest, token_ids, grouped_picks, masks)
    )
    masks = gather_copies(masks)
    recon = jnp.sum(trade(shares).astype(jnp.float32), 0) + b_dec

    place = lax.broadcasted_iota(jnp.int32, (1, 1, 1, seq_len), 3)
    ids = token_ids.reshape(size, count, 1, seq_len)
    targets = jnp.sum(jnp.where(grouped_picks[..., None] + 1 == place, ids, 0), -1).reshape(-1)
    targets = targets - mine * vocab_rows
    here = (targets >= 0) & (targets < vocab_rows)
    target_rows = jnp.take(wte, jnp.clip(targets, 0, vocab_rows - 1), axis=0)
    target_rows = jnp.where(here[:, None], target_rows, jnp.zeros_like(target_rows))
    pick_mask, rest_mask, pick_marks, rest_marks, sparse_coef = mark_rows(masks)
    bias = b_enc.reshape(-1, 1)
    recon, target_rows, pick_marks, rest_marks, rest = lax.optimization_barrier(
        (recon, target_rows, pick_marks, rest_marks, rest)
    )
    far_rest = across(rest)

    mid = own_inputs + recon
    normed, second_norm_back = jax.vjp(
        lambda values: layer_norm(values, norm_gains[1], norm_biases[1]), mid
    )
    up_val = times(normed.astype(low), fc_w) + fc_b
    act, gelu_back = jax.vjp(lambda values: jax.nn.gelu(values, approximate=True), up_val)
    hidden = mid + times(act.astype(low), proj_w) + proj_b
    final, final_norm_back = jax.vjp(
        lambda values: layer_norm(values, norm_gains[2], norm_biases[2]), hidden
    )
    finals = gather_group(final.astype(low))
    all_feat, pick_sparse = feature_rows(
        core, all_pick, size * own_count, w_enc, bias, pick_mask
    )
    far_rest, all_feat = lax.optimization_barrier((far_rest, all_feat))
    finals, all_feat, far_rest = lax.optimization_barrier((finals, all_feat, far_rest))
    all_rest = spread(rest) + spread(far_rest)

    logits = times_trans(finals, wte)
    top = jnp.max(logits, 1)
    parts = jnp.exp(logits - top[:, None])
    mass = jnp.sum(parts, 1)
    at = jnp.sum(finals.astype(jnp.float32) * target_rows.astype(jnp.float32), 1)
    stats = trade(jnp.broadcast_to(jnp.stack([top, mass, at])[None], (size, 3, top.shape[0])))
    mixed = times(parts.astype(low), wte)
    stats, mixed = lax.optimization_barrier((stats, mixed))
    best = jnp.max(stats[:, 0], 0)
    total = jnp.sum(stats[:, 1] * jnp.exp(stats[:, 0] - best), 0)
    cross = jnp.sum(best + jnp.log(total) - jnp.sum(stats[:, 2], 0))
    scale = jnp.exp(top - best) / total
    dshares = (mixed * scale[:, None] - target_rows.astype(jnp.float32)) / total_picks
    dshares = dshares.astype(low).reshape(size, -1, model_width)
    cross = jnp.broadcast_to(cross, (1, 128))
    dshares, idle_marks, cross = lax.optimization_barrier((dshares, rest_marks, cross))
    bit = lax.axis_size("dp") // 2
    while bit:
        cross = cross + swap(cross, "dp", bit)
        bit //= 2
    dfinal = jnp.sum(trade(dshares).astype(jnp.float32), 0)
    idle, rest_sparse = idle_gradient(
        core, all_rest, size * own_count, w_enc, bias, rest_mask, idle_marks
    )
    dfinal, idle, pick_sparse, cross = lax.optimization_barrier((dfinal, idle, pick_sparse, cross))

    dhidden = final_norm_back(dfinal)[0]
    dact = times_trans(dhidden.astype(low), proj_w)
    dup_low = gelu_back(dact)[0].astype(low)
    dnormed = times_trans(dup_low, fc_w)
    drecon = (dhidden + second_norm_back(dnormed)[0]).astype(low)

    errors = join(gather_near(drecon))
    far_errors = across(errors)
    middle = len(all_pick) // 2
    near = gradients(
        core, all_pick[:middle], spread(errors), all_feat, 0, w_dec, pick_marks, idle
    )
    near, far_errors = lax.optimization_barrier((near, far_errors))
    own, squares = gradients(
        core, all_pick[middle:], spread(far_errors), all_feat, 1, w_dec, pick_marks, near
    )
    terms = jnp.stack([cross, sparse_coef])
    small = jnp.stack([squares, pick_sparse + rest_sparse, weight_squares[0], weight_squares[1]])
    small, own, terms = lax.optimization_barrier((small + swap(small, "dp", 1), own, terms))
    other = swap(own, "dp", 1)
    small = pieces_of(small)
    clip_norm = norm_of(small)
    *directions, firsts, seconds, squares = moments(
        size,
        core,
        clip_norm,
        own,
        other,
        w_enc,
        enc_first,
        enc_second,
        w_dec,
        dec_first,
        dec_second,
    )
    weights, rows = renew(
        trade(squares), small, terms, clip_norm, directions, w_enc, w_dec, total_picks
    )
    return weights, firsts, seconds, rows[4, 0], rows[5, 0], rows[:2, 0], rows[2:4, 0]


def solution(mesh):
    in_specs = (
        P(("dp", "fsdp"), None, None),
        P("dp", None),
        P("dp", None),
        P("dp", None),
        P(),
        P(),
        P(),
        P(),
        P(),
        P(),
        P(),
        P("fsdp", None),
        P("fsdp", None),
        P("fsdp", None),
        P("fsdp", None),
        P("fsdp"),
        P("fsdp", None),
        P("fsdp", None),
        P("fsdp", None),
        P(),
    )
    out_specs = (
        P(None, "fsdp", None),
        P(None, "fsdp", None),
        P(None, "fsdp", None),
        P(),
        P(),
        P(),
        P(),
    )
    return jax.shard_map(shards, mesh=mesh, in_specs=in_specs, out_specs=out_specs, check_vma=False)
```

```python
import jax
import jax.numpy as jnp
from jax import lax
from jax.experimental import pallas as pl
from jax.experimental.pallas import tpu as pltpu
from jax.sharding import PartitionSpec as P

HEADS = 12
HEAD_DIM = 64
F = 24576
STEP = 10


norm_eps = 1e-05
l1_scale = 40.0
clip_limit = 0.02
learn_rate = 0.3
beta_one = 0.9
beta_two = 0.999
adam_eps = 1e-08
weight_decay = 0.01


def layer_norm(values, gain, shift):
    center = values - jnp.mean(values, -1, keepdims=True)
    spread = jnp.mean(center * center, -1, keepdims=True)
    return center * lax.rsqrt(spread + norm_eps) * gain + shift


def times(left, right):
    return jnp.dot(left, right, preferred_element_type=jnp.float32)


def times_trans(left, right):
    return lax.dot_general(
        left, right, (((1,), (1,)), ((), ())), preferred_element_type=jnp.float32
    )


def trans_times(left, right):
    return lax.dot_general(
        left, right, (((0,), (0,)), ((), ())), preferred_element_type=jnp.float32
    )


def swap(block, axis, bit):
    size = lax.axis_size(axis)
    return lax.ppermute(block, axis, [(i, i ^ bit) for i in range(size)])


def trade(blocks):
    return lax.all_to_all(blocks, "fsdp", 0, 0, tiled=True)


def gather_group(block):
    size = lax.axis_size("fsdp")
    spread = jnp.broadcast_to(block[None], (size, *block.shape))
    return trade(spread).reshape(-1, *block.shape[1:])


def gather_halves(own, far):
    size = lax.axis_size("fsdp")
    half = size // 2
    both = jnp.concatenate([own, far], 0)
    groups = [list(range(half)), list(range(half, size))]
    blocks = lax.all_to_all(
        jnp.broadcast_to(both[None], (half, *both.shape)),
        "fsdp",
        0,
        0,
        axis_index_groups=groups,
        tiled=True,
    )
    return blocks.reshape(-1, both.shape[1])


def gather_near(block):
    half = lax.axis_size("fsdp") // 2
    far = swap(block, "fsdp", half)
    near = [block] + [swap(block, "fsdp", k) for k in range(1, half)]
    return near + [far] + [swap(far, "fsdp", k) for k in range(1, half)]


def pieces_of(block):
    size = lax.axis_size("fsdp")
    return [block] + [swap(block, "fsdp", k) for k in range(1, size)]


def paired(pieces):
    while len(pieces) > 1:
        pieces = [a + b for a, b in zip(pieces[::2], pieces[1::2])]
    return pieces[0]


def across(block):
    return swap(block, "dp", lax.axis_size("dp") // 2)


def spread(block):
    blocks = [block]
    bit = lax.axis_size("dp") // 4
    while bit:
        blocks = blocks + [swap(held, "dp", bit) for held in blocks]
        bit //= 2
    return blocks


def gather_copies(block):
    return spread(block) + spread(across(block))


VMEM = pl.BlockSpec(memory_space=pltpu.VMEM)
PLACED = pl.BlockSpec(memory_space=pl.ANY)
ONCE = pl.Buffered(1)


def in_vmem(values):
    return pltpu.with_memory_space_constraint(values, pltpu.VMEM)


def in_hbm(values):
    return pltpu.with_memory_space_constraint(values, pltpu.HBM)


def fold(values):
    rows, width = values.shape
    total = jnp.sum(values.reshape(rows // 8, 8, width), 0)
    return sum(total[:, k : k + 128] for k in range(0, width, 128))


def block_rows(count, most):
    return max(rows for rows in range(16, most + 1, 16) if count % rows == 0)


def scalars(grid, in_specs, out_specs, scratch_shapes=()):
    return pltpu.PrefetchScalarGridSpec(
        num_scalar_prefetch=1,
        grid=grid,
        in_specs=in_specs,
        out_specs=out_specs,
        scratch_shapes=scratch_shapes,
    )


def attention(resid, picks, gains, shifts, qkv_w, out_w, layer_bias, b_dec):
    count, length, width = resid.shape
    pick_count = picks.shape[1]
    rest_count = length - pick_count
    pair = 2 * HEAD_DIM

    def kernel(
        resid_ref,
        pick_ref,
        gain_ref,
        shift_ref,
        qkv_ref,
        out_ref,
        bias_ref,
        dec_ref,
        rows_ref,
        rest_ref,
        inputs_ref,
    ):
        values = resid_ref[...].astype(jnp.float32).reshape(count * length, width)
        normed = layer_norm(values, gain_ref[:1, :], shift_ref[:1, :]).astype(jnp.bfloat16)
        packed = (times(normed, qkv_ref[...]) + bias_ref[:, : 3 * width]).astype(jnp.bfloat16)
        first = lax.broadcasted_iota(jnp.int32, (length, pair), 1) < HEAD_DIM
        row_ids = lax.broadcasted_iota(jnp.int32, (length, length), 0)
        col_ids = lax.broadcasted_iota(jnp.int32, (length, length), 1)
        causal = jnp.concatenate([row_ids >= col_ids] * 2, 0)
        contexts = []
        for s in range(count):
            at = slice(s * length, (s + 1) * length)
            pairs = []
            for lane in range(0, width, pair):
                query = packed[at, lane : lane + pair]
                key = packed[at, width + lane : width + lane + pair]
                value = packed[at, 2 * width + lane : 2 * width + lane + pair]
                zero = jnp.zeros_like(query)
                both = jnp.concatenate(
                    [jnp.where(first, query, zero), jnp.where(first, zero, query)], 0
                )
                scores = times_trans(both, key) * HEAD_DIM ** (-0.5)
                scores = jnp.where(causal, scores, -1e30)
                powers = jnp.exp(scores - jnp.max(scores, -1, keepdims=True))
                probs = (powers / jnp.sum(powers, -1, keepdims=True)).astype(jnp.bfloat16)
                mixed = times(probs, value)
                pairs.append(jnp.where(first, mixed[:length], mixed[length:]))
            contexts.append(jnp.concatenate(pairs, 1).astype(jnp.bfloat16))
        context = jnp.concatenate(contexts, 0)
        attn = times(context, out_ref[...]) + bias_ref[:, 3 * width : 4 * width]
        centered = (attn - dec_ref[...]).astype(jnp.bfloat16)
        after = (row_ids < col_ids).astype(jnp.float32)
        lanes = lax.broadcasted_iota(jnp.int32, (pick_count, length), 1)
        slots = lax.broadcasted_iota(jnp.int32, (rest_count, length), 0).astype(jnp.float32)
        for s in range(count):
            at = slice(s * length, (s + 1) * length)
            chosen = (pick_ref[s] == lanes).astype(jnp.float32)
            free = 1.0 - jnp.sum(chosen, 0, keepdims=True)
            rank = times(jnp.broadcast_to(free, (8, length)), after)[:1]
            others = jnp.where((rank == slots) & (free > 0), 1.0, 0.0).astype(jnp.bfloat16)
            chosen = chosen.astype(jnp.bfloat16)
            rows_ref[s * pick_count : (s + 1) * pick_count, :] = times(
                chosen, centered[at]
            ).astype(jnp.bfloat16)
            rest_ref[s * rest_count : (s + 1) * rest_count, :] = times(
                others, centered[at]
            ).astype(jnp.bfloat16)
            inputs_ref[s * pick_count : (s + 1) * pick_count, :] = times(chosen, resid_ref[s])

    return pl.pallas_call(
        kernel,
        in_specs=[VMEM] * 8,
        out_specs=[VMEM, VMEM, VMEM],
        out_shape=[
            jax.ShapeDtypeStruct((count * pick_count, width), jnp.bfloat16),
            jax.ShapeDtypeStruct((count * rest_count, width), jnp.bfloat16),
            jax.ShapeDtypeStruct((count * pick_count, width), jnp.float32),
        ],
        compiler_params=pltpu.CompilerParams(vmem_limit_bytes=32 << 20),
        cost_estimate=pl.CostEstimate(
            flops=8 * count * length * width * width,
            bytes_accessed=8 * width * width,
            transcendentals=count * length * width,
        ),
        name="attention",
    )(resid, picks[..., None], gains, shifts, qkv_w, out_w, layer_bias, b_dec)


def join(blocks):
    part, width = blocks[0].shape
    count = len(blocks)

    def kernel(*refs):
        for k in range(count):
            refs[count][k * part : (k + 1) * part, :] = refs[k][...]

    return pl.pallas_call(
        kernel,
        in_specs=[VMEM] * count,
        out_specs=VMEM,
        out_shape=jax.ShapeDtypeStruct((part * count, width), blocks[0].dtype),
        name="join",
    )(*blocks)


def mask_rows(mine, size, picked, valid_mask):
    count, pick_count = picked.shape
    length = valid_mask.shape[1]
    lanes = count * pick_count
    block = lanes // size

    def kernel(mine_ref, pick_ref, mask_ref, out_ref):
        def one(test):
            return jnp.where(test, 1.0, 0.0).astype(jnp.bfloat16)

        def ids(shape, dim):
            return lax.broadcasted_iota(jnp.int32, shape, dim)

        wide, square = (length, lanes), (lanes, lanes)
        chosen = one(pick_ref[...] == ids(wide, 0))
        group = one(ids(square, 0) // pick_count == ids(square, 1) // pick_count)
        free = 1.0 - times(chosen, group)
        before = one(ids((length, length), 0) > ids((length, length), 1))
        rank = times(before, free.astype(jnp.bfloat16))
        slot = lax.rem(ids(wide, 1), pick_count).astype(jnp.float32)
        others = jnp.where((rank == slot) & (free > 0), 1.0, 0.0)
        owner = one(ids((count, lanes), 0) == ids((count, lanes), 1) // pick_count)
        mask = trans_times(mask_ref[...].astype(jnp.bfloat16), owner)
        picks = jnp.sum(chosen.astype(jnp.float32) * mask, 0, keepdims=True)
        source, target = ids(square, 0), ids(square, 1)
        moved = one(
            (source // block == ((target // block) ^ mine_ref[0]))
            & (lax.rem(source, block) == lax.rem(target, block))
        )
        out_ref[:1, :] = times(picks.astype(jnp.bfloat16), moved)
        rests = jnp.sum(others * mask, 0, keepdims=True)
        half = size // 2
        place = target // block
        mate = place // 2 + ((mine_ref[0] // half) ^ lax.rem(place, 2)) * half
        moved = one((source // block == mate) & (lax.rem(source, block) == lax.rem(target, block)))
        out_ref[1:, :] = times(rests.astype(jnp.bfloat16), moved)

    return pl.pallas_call(
        kernel,
        in_specs=[pl.BlockSpec(memory_space=pltpu.SMEM), VMEM, VMEM],
        out_specs=VMEM,
        out_shape=jax.ShapeDtypeStruct((2, lanes), jnp.float32),
        compiler_params=pltpu.CompilerParams(vmem_limit_bytes=(8 << 20) + 12 * lanes * lanes),
        name="masks",
    )(mine, picked.reshape(1, -1), valid_mask)


def mark_rows(masks):
    count = len(masks)
    lanes = masks[0].shape[1]

    def kernel(*refs):
        pick_ref, rest_ref, pick_marks, rest_marks, coef_ref = refs[count:]
        total = sum(jnp.sum(ref[...], keepdims=True).reshape(1, 1) for ref in refs[:count])
        coef = l1_scale / F / total
        coef_ref[...] = jnp.broadcast_to(coef, (1, 128))
        for k in range(count):
            at = slice(k * lanes, (k + 1) * lanes)
            pick_ref[:, at] = refs[k][:1, :]
            rest_ref[:, at] = refs[k][1:, :]
            pick_marks[:, at] = refs[k][:1, :] * coef
            rest_marks[:, at] = refs[k][1:, :] * coef

    return pl.pallas_call(
        kernel,
        in_specs=[VMEM] * count,
        out_specs=[VMEM] * 5,
        out_shape=[jax.ShapeDtypeStruct((1, count * lanes), jnp.float32)] * 4
        + [jax.ShapeDtypeStruct((1, 128), jnp.float32)],
        name="marks",
    )(*masks)


def encode(mine, tokens, count, part, w_enc, w_dec, b_enc):
    width = tokens.shape[1]
    feats = w_enc.shape[0]
    rows = block_rows(feats, 1024)
    steps = feats // rows

    def kernel(mine_ref, token_ref, enc_ref, dec_ref, bias_ref, share_ref, square_ref, total_ref):

        @pl.when(pl.program_id(0) == 0)
        def _():
            square_ref[...] = jnp.zeros_like(square_ref)
            total_ref[...] = jnp.zeros_like(total_ref)

        enc, dec = enc_ref[...], dec_ref[...]
        square_ref[0] += fold(enc * enc)
        square_ref[1] += fold(dec * dec)
        enc_low, dec_low = enc.astype(jnp.bfloat16), dec.astype(jnp.bfloat16)
        features = jnp.maximum(times_trans(token_ref[...], enc_low) + bias_ref[...], 0.0)
        total_ref[...] += times(features.astype(jnp.bfloat16), dec_low)

        @pl.when(pl.program_id(0) == steps - 1)
        def _():
            for k in range(count):
                share_ref[mine_ref[0] ^ k] = total_ref[k * part : (k + 1) * part, :].astype(
                    jnp.bfloat16
                )

    whole = pl.BlockSpec((count * part, width), lambda i, s: (0, 0), pipeline_mode=ONCE)
    block = pl.BlockSpec((rows, width), lambda i, s: (i, 0))
    return pl.pallas_call(
        kernel,
        grid_spec=scalars(
            (steps,),
            [whole, block, block, pl.BlockSpec((1, rows), lambda i, s: (0, i))],
            [
                pl.BlockSpec((count, part, width), lambda i, s: (0, 0, 0)),
                pl.BlockSpec((2, 8, 128), lambda i, s: (0, 0, 0)),
            ],
            [pltpu.VMEM((count * part, width), jnp.float32)],
        ),
        out_shape=[
            jax.ShapeDtypeStruct((count, part, width), jnp.bfloat16),
            jax.ShapeDtypeStruct((2, 8, 128), jnp.float32),
        ],
        compiler_params=pltpu.CompilerParams(
            vmem_limit_bytes=(36 << 20) + 12 * count * part * width
        ),
        cost_estimate=pl.CostEstimate(
            flops=4 * feats * width * count * part, bytes_accessed=8 * feats * width, transcendentals=0
        ),
        name="encode",
    )(mine, in_hbm(tokens), in_hbm(w_enc), in_hbm(w_dec), b_enc)


def feature_rows(core, tokens, part, w_enc, bias, masks):
    count = len(tokens)
    width = tokens[0].shape[1]
    feats = w_enc.shape[0] // 2
    rows = block_rows(feats, 512 if part <= 512 else 128)
    steps = feats // rows

    def kernel(core_ref, *refs):
        token_refs = refs[:count]
        enc_ref, bias_ref, mask_ref, out_ref, sum_ref = refs[count:]

        @pl.when(pl.program_id(0) == 0)
        def _():
            sum_ref[...] = jnp.zeros_like(sum_ref)

        enc = enc_ref[...].astype(jnp.bfloat16)
        for k in range(count):
            at = pl.ds(k * part, part)
            pre = times_trans(enc, token_refs[k][...]) + bias_ref[...]
            kept = jnp.maximum(pre, 0.0)
            out_ref[:, at] = kept.astype(jnp.bfloat16)
            sum_ref[...] += fold(kept * mask_ref[:, at])

    whole = pl.BlockSpec((part, width), lambda i, s: (0, 0), pipeline_mode=ONCE)
    return pl.pallas_call(
        kernel,
        grid_spec=scalars(
            (steps,),
            [whole] * count
            + [
                pl.BlockSpec((rows, width), lambda i, s: (s[0] * steps + i, 0)),
                pl.BlockSpec((rows, 1), lambda i, s: (s[0] * steps + i, 0)),
                pl.BlockSpec((1, count * part), lambda i, s: (0, 0)),
            ],
            [
                pl.BlockSpec((rows, count * part), lambda i, s: (i, 0)),
                pl.BlockSpec((8, 128), lambda i, s: (0, 0)),
            ],
        ),
        out_shape=[
            pltpu.HBM((feats, count * part), jnp.bfloat16),
            jax.ShapeDtypeStruct((8, 128), jnp.float32),
        ],
        compiler_params=pltpu.CompilerParams(
            vmem_limit_bytes=(24 << 20) + 2 * count * part * width
        ),
        cost_estimate=pl.CostEstimate(
            flops=2 * feats * width * count * part,
            bytes_accessed=2 * (feats + width) * count * part + 2 * feats * width,
            transcendentals=0,
        ),
        name="features",
    )(core, *map(in_hbm, tokens), in_hbm(w_enc), bias, masks)


def idle_gradient(core, tokens, part, w_enc, bias, masks, marks):
    count = len(tokens)
    width = tokens[0].shape[1]
    feats = w_enc.shape[0] // 2
    rows = block_rows(feats, 512 if part <= 512 else 128)
    steps = feats // rows

    def kernel(core_ref, *refs):
        token_refs = refs[:count]
        enc_ref, bias_ref, mask_ref, mark_ref, out_ref, sum_ref = refs[count:]

        @pl.when(pl.program_id(0) == 0)
        def _():
            sum_ref[...] = jnp.zeros_like(sum_ref)

        grad = jnp.zeros(out_ref.shape, jnp.float32)
        enc = enc_ref[...].astype(jnp.bfloat16)
        for k in range(count):
            at = pl.ds(k * part, part)
            pre = times_trans(enc, token_refs[k][...]) + bias_ref[...]
            sum_ref[...] += fold(jnp.maximum(pre, 0.0) * mask_ref[:, at])
            dpre = jnp.where(pre > 0, mark_ref[:, at], 0.0).astype(jnp.bfloat16)
            grad = grad + times(dpre, token_refs[k][...])
        out_ref[...] = grad

    whole = pl.BlockSpec((part, width), lambda i, s: (0, 0), pipeline_mode=ONCE)
    row = pl.BlockSpec((1, count * part), lambda i, s: (0, 0))
    return pl.pallas_call(
        kernel,
        grid_spec=scalars(
            (steps,),
            [whole] * count
            + [
                pl.BlockSpec((rows, width), lambda i, s: (s[0] * steps + i, 0)),
                pl.BlockSpec((rows, 1), lambda i, s: (s[0] * steps + i, 0)),
                row,
                row,
            ],
            [
                pl.BlockSpec((rows, width), lambda i, s: (i, 0)),
                pl.BlockSpec((8, 128), lambda i, s: (0, 0)),
            ],
        ),
        out_shape=[
            pltpu.HBM((feats, width), jnp.float32),
            jax.ShapeDtypeStruct((8, 128), jnp.float32),
        ],
        compiler_params=pltpu.CompilerParams(
            vmem_limit_bytes=(24 << 20) + 2 * count * part * width
        ),
        cost_estimate=pl.CostEstimate(
            flops=4 * feats * width * count * part,
            bytes_accessed=2 * width * count * part + 6 * feats * width,
            transcendentals=0,
        ),
        name="idle",
    )(core, *map(in_hbm, tokens), in_hbm(w_enc), bias, masks, marks)


def gradients(core, tokens, errors, features, side, w_dec, marks, start):
    count = len(tokens)
    part, width = errors[0].shape
    feats = w_dec.shape[0] // 2
    rows = block_rows(feats, 256 if part <= 512 else 128)
    steps = feats // rows

    def kernel(core_ref, *refs):
        token_refs, error_refs = refs[:count], refs[count : 2 * count]
        feat_ref, dec_ref, mark_ref, start_ref, out_ref, *square_ref = refs[2 * count :]
        weight = dec_ref[...].astype(jnp.bfloat16)
        if side:
            enc, dec = start_ref[0], start_ref[1]
        else:
            enc, dec = start_ref[...], jnp.zeros((rows, width), jnp.float32)
        for k in range(count):
            at = pl.ds(k * part, part)
            feat = feat_ref[:, at]
            dfeat = times_trans(weight, error_refs[k][...]) + mark_ref[:, at]
            dpre = jnp.where(feat > 0, dfeat, 0.0).astype(jnp.bfloat16)
            enc = enc + times(dpre, token_refs[k][...])
            dec = dec + times(feat, error_refs[k][...])
        out_ref[0] = enc
        out_ref[1] = dec
        if side:

            @pl.when(pl.program_id(0) == 0)
            def _():
                square_ref[0][...] = jnp.zeros_like(square_ref[0])

            square_ref[0][...] += fold(enc * enc) + fold(dec * dec)

    whole = pl.BlockSpec((part, width), lambda i, s: (0, 0), pipeline_mode=ONCE)
    both = pl.BlockSpec((2, rows, width), lambda i, s: (0, i, 0))
    block = pl.BlockSpec((rows, width), lambda i, s: (i, 0))
    out_specs = [both] + [pl.BlockSpec((8, 128), lambda i, s: (0, 0))] * side
    out_shape = [pltpu.HBM((2, feats, width), jnp.float32)]
    out_shape = out_shape + [jax.ShapeDtypeStruct((8, 128), jnp.float32)] * side
    outs = pl.pallas_call(
        kernel,
        grid_spec=scalars(
            (steps,),
            [whole] * (2 * count)
            + [
                pl.BlockSpec((rows, count * part), lambda i, s: (i, side)),
                pl.BlockSpec((rows, width), lambda i, s: (s[0] * steps + i, 0)),
                pl.BlockSpec((1, count * part), lambda i, s: (0, side)),
                both if side else block,
            ],
            out_specs,
        ),
        out_shape=out_shape,
        compiler_params=pltpu.CompilerParams(
            vmem_limit_bytes=(18 << 20) + 4 * count * part * width
        ),
        cost_estimate=pl.CostEstimate(
            flops=6 * feats * width * count * part,
            bytes_accessed=(2 * feats + 4 * width) * count * part + 20 * feats * width,
            transcendentals=0,
        ),
        name="gradients",
    )(
        core,
        *map(in_hbm, tokens),
        *map(in_hbm, errors),
        in_hbm(features),
        in_hbm(w_dec),
        marks,
        in_hbm(start),
    )
    return outs if side else outs[0]


def norm_of(pieces):
    def kernel(*refs):
        total = jnp.sum(paired([ref[0] for ref in refs[:-1]]), keepdims=True).reshape(1, 1)
        refs[-1][...] = jnp.broadcast_to(jnp.sqrt(total), refs[-1].shape)

    return pl.pallas_call(
        kernel,
        in_specs=[VMEM] * len(pieces),
        out_specs=VMEM,
        out_shape=jax.ShapeDtypeStruct((8, 128), jnp.float32),
        compiler_params=pltpu.CompilerParams(vmem_limit_bytes=1 << 20),
        name="norm",
    )(*pieces)


def moments(
    size, core, clip_norm, own, other, w_enc, enc_first, enc_second, w_dec, dec_first, dec_second
):
    feats, width = w_enc.shape
    rows = block_rows(feats // 2, 256)
    half = feats // 2 // rows
    steps = 2 * half

    def kernel(core_ref, norm_ref, own_ref, other_ref, *refs):
        enc, dec, outs = refs[:3], refs[3:6], refs[6:]
        dir_refs, (first_out, second_out, square_ref) = outs[:2], outs[2:]
        factor = clip_limit / jnp.maximum(norm_ref[:1, :1], clip_limit)
        square_ref[...] = jnp.zeros_like(square_ref)
        start = core_ref[0] * half

        def place(i):
            return lax.rem(start + i, steps)

        def body(own, enc_first, enc_second, dec_first, dec_second, first_ref, second_ref):
            step = pl.program_id(0)
            at = pl.ds(pl.multiple_of(place(step) * rows, rows), rows)
            back = pl.ds(pl.multiple_of(jnp.maximum(step - half, 0) * rows, rows), rows)
            sides = ((enc[0], enc_first, enc_second), (dec[0], dec_first, dec_second))
            for plane, (weight, first, second) in enumerate(sides):
                clipped = jnp.where(step < half, own[plane], other_ref[plane, back, :]) * factor
                first_new = beta_one * first[...] + (1.0 - beta_one) * clipped
                second_new = beta_two * second[...] + (1.0 - beta_two) * clipped * clipped
                first_ref[plane] = first_new
                second_ref[plane] = second_new
                scaled = second_new * (1.0 / (1.0 - beta_two**STEP))
                spread = scaled * lax.rsqrt(scaled) + adam_eps
                direction = (
                    first_new * (1.0 / (1.0 - beta_one**STEP)) * pltpu.reciprocal(spread)
                    + weight_decay * weight[at, :]
                )
                dir_refs[plane][at, :] = direction.astype(jnp.bfloat16)
                square_ref[:, plane] += jnp.broadcast_to(
                    fold(direction * direction)[None], (size, 8, 128)
                )

        block = pl.BlockSpec((rows, width), lambda i: (place(i), 0))
        both = pl.BlockSpec((2, rows, width), lambda i: (0, place(i), 0))
        early = pl.BlockSpec((2, rows, width), lambda i: (0, jnp.minimum(i, half - 1), 0))
        pltpu.emit_pipeline(
            body,
            grid=(steps,),
            in_specs=[early] + [block] * 4,
            out_specs=[both, both],
        )(own_ref, enc[1], enc[2], dec[1], dec[2], first_out, second_out)

    full = (2, feats, width)
    return pl.pallas_call(
        kernel,
        in_specs=[pl.BlockSpec(memory_space=pltpu.SMEM), VMEM, PLACED, VMEM]
        + [VMEM, PLACED, PLACED] * 2,
        out_specs=[VMEM, VMEM, PLACED, PLACED, VMEM],
        out_shape=[
            pltpu.VMEM((feats, width), jnp.bfloat16),
            pltpu.VMEM((feats, width), jnp.bfloat16),
            pltpu.HBM(full, jnp.float32),
            pltpu.HBM(full, jnp.float32),
            jax.ShapeDtypeStruct((size, 2, 8, 128), jnp.float32),
        ],
        compiler_params=pltpu.CompilerParams(vmem_limit_bytes=18 << 20),
        cost_estimate=pl.CostEstimate(
            flops=40 * feats * width,
            bytes_accessed=40 * feats * width,
            transcendentals=4 * feats * width,
        ),
        name="moments",
    )(
        core,
        clip_norm,
        in_hbm(own),
        in_vmem(other),
        in_vmem(w_enc),
        in_hbm(enc_first),
        in_hbm(enc_second),
        in_vmem(w_dec),
        in_hbm(dec_first),
        in_hbm(dec_second),
    )


def renew(sums, small, terms, clip_norm, directions, w_enc, w_dec, total_picks):
    feats, width = w_enc.shape
    rows = block_rows(feats, 512)

    count = len(small)

    def kernel(*refs):
        sum_refs, small_refs, refs = refs[:1], refs[1 : count + 1], refs[count + 1 :]
        term_ref, clip_ref, enc_dir, dec_dir, enc_ref, dec_ref, out_ref, row_ref = refs
        sums = paired([sum_refs[0][k] for k in range(count)])
        small = paired([ref[...] for ref in small_refs])
        def total(values):
            return jnp.sum(values, keepdims=True).reshape(1, 1)

        norms = [jnp.sqrt(0.5 * total(small[2 + plane])) for plane in range(2)]
        steps = [jnp.sqrt(total(sums[plane])) for plane in range(2)]
        rates = [learn_rate * (norms[plane] / steps[plane]) for plane in range(2)]
        loss = term_ref[0, :1, :1] / total_picks + term_ref[1, :1, :1] * total(small[1])
        for i, value in enumerate((*norms, *steps, loss, clip_ref[:1, :1])):
            row_ref[i : i + 1, :] = jnp.broadcast_to(value, (1, 128))
        row_ref[6:, :] = jnp.zeros((2, 128), jnp.float32)

        def body(new_ref):
            at = pl.ds(pl.multiple_of(pl.program_id(0) * rows, rows), rows)
            new_ref[0] = enc_ref[at, :] - rates[0] * enc_dir[at, :].astype(jnp.float32)
            raw = dec_ref[at, :] - rates[1] * dec_dir[at, :].astype(jnp.float32)
            new_ref[1] = raw * lax.rsqrt(jnp.sum(raw * raw, 1, keepdims=True) + 1e-06)

        both = pl.BlockSpec((2, rows, width), lambda i: (0, i, 0))
        pltpu.emit_pipeline(body, grid=(feats // rows,), out_specs=[both])(out_ref)

    return pl.pallas_call(
        kernel,
        in_specs=[VMEM] * (count + 7),
        out_specs=[PLACED, VMEM],
        out_shape=[
            pltpu.HBM((2, feats, width), jnp.float32),
            jax.ShapeDtypeStruct((8, 128), jnp.float32),
        ],
        compiler_params=pltpu.CompilerParams(vmem_limit_bytes=16 << 20),
        cost_estimate=pl.CostEstimate(
            flops=12 * w_enc.size, bytes_accessed=8 * w_enc.size, transcendentals=0
        ),
        name="renew",
    )(sums, *small, terms, clip_norm, *map(in_vmem, directions), in_vmem(w_enc), in_vmem(w_dec))


def shards(
    resid_pre,
    token_ids,
    valid_mask,
    picked,
    norm_gains,
    norm_biases,
    qkv_w,
    out_w,
    fc_w,
    proj_w,
    layer_bias,
    wte,
    w_enc,
    enc_first,
    enc_second,
    b_enc,
    w_dec,
    dec_first,
    dec_second,
    b_dec,
):
    low = jnp.bfloat16
    count, seq_len, model_width = resid_pre.shape
    size = lax.axis_size("fsdp")
    mine = lax.axis_index("fsdp")
    pick_count = picked.shape[1]
    rest_count = seq_len - pick_count
    hidden_units = fc_w.shape[1]
    vocab_rows = wte.shape[0]
    total_picks = lax.axis_size("dp") * size * count * pick_count
    fc_b = layer_bias[4 * model_width : 4 * model_width + hidden_units]
    proj_b = layer_bias[4 * model_width + hidden_units :]

    grouped_picks = picked.reshape(size, count, pick_count)
    own_pick, own_rest, own_inputs = attention(
        resid_pre,
        lax.dynamic_index_in_dim(grouped_picks, mine, 0, keepdims=False),
        norm_gains,
        norm_biases,
        qkv_w,
        out_w,
        layer_bias.reshape(1, -1),
        b_dec.reshape(1, -1),
    )
    own_count = own_inputs.shape[0]

    me = mine.reshape(1).astype(jnp.int32)
    core = (lax.axis_index("dp") & 1).reshape(1).astype(jnp.int32)
    own_pick, picked, valid_mask = lax.optimization_barrier((own_pick, picked, valid_mask))
    masks = mask_rows(me, size, picked, valid_mask)
    tokens = join(gather_near(own_pick))
    far_rest = swap(own_rest, "fsdp", size // 2)
    tokens, own_rest, far_rest = lax.optimization_barrier((tokens, own_rest, far_rest))
    rest = gather_halves(own_rest, far_rest)
    all_pick = gather_copies(tokens)
    shares, weight_squares = encode(
        me, tokens, size, own_count, w_enc, w_dec, b_enc.reshape(1, -1)
    )
    shares, rest, token_ids, grouped_picks, masks = lax.optimization_barrier(
        (shares, rest, token_ids, grouped_picks, masks)
    )
    masks = gather_copies(masks)
    masks, rest = lax.optimization_barrier((masks, rest))
    far_rest = across(rest)
    recon = jnp.sum(trade(shares).astype(jnp.float32), 0) + b_dec

    place = lax.broadcasted_iota(jnp.int32, (1, 1, 1, seq_len), 3)
    ids = token_ids.reshape(size, count, 1, seq_len)
    targets = jnp.sum(jnp.where(grouped_picks[..., None] + 1 == place, ids, 0), -1).reshape(-1)
    targets = targets - mine * vocab_rows
    here = (targets >= 0) & (targets < vocab_rows)
    target_rows = jnp.take(wte, jnp.clip(targets, 0, vocab_rows - 1), axis=0)
    target_rows = jnp.where(here[:, None], target_rows, jnp.zeros_like(target_rows))
    pick_mask, rest_mask, pick_marks, rest_marks, sparse_coef = mark_rows(masks)
    bias = b_enc.reshape(-1, 1)
    recon, target_rows, pick_marks, rest_marks = lax.optimization_barrier(
        (recon, target_rows, pick_marks, rest_marks)
    )

    mid = own_inputs + recon
    normed, second_norm_back = jax.vjp(
        lambda values: layer_norm(values, norm_gains[1], norm_biases[1]), mid
    )
    up_val = times(normed.astype(low), fc_w) + fc_b
    act, gelu_back = jax.vjp(lambda values: jax.nn.gelu(values, approximate=True), up_val)
    hidden = mid + times(act.astype(low), proj_w) + proj_b
    final, final_norm_back = jax.vjp(
        lambda values: layer_norm(values, norm_gains[2], norm_biases[2]), hidden
    )
    finals = gather_group(final.astype(low))
    all_feat, pick_sparse = feature_rows(
        core, all_pick, size * own_count, w_enc, bias, pick_mask
    )
    far_rest, all_feat = lax.optimization_barrier((far_rest, all_feat))
    finals, all_feat, far_rest = lax.optimization_barrier((finals, all_feat, far_rest))
    all_rest = spread(rest) + spread(far_rest)

    logits = times_trans(finals, wte)
    top = jnp.max(logits, 1)
    parts = jnp.exp(logits - top[:, None])
    mass = jnp.sum(parts, 1)
    at = jnp.sum(finals.astype(jnp.float32) * target_rows.astype(jnp.float32), 1)
    stats = trade(jnp.broadcast_to(jnp.stack([top, mass, at])[None], (size, 3, top.shape[0])))
    mixed = times(parts.astype(low), wte)
    stats, mixed = lax.optimization_barrier((stats, mixed))
    best = jnp.max(stats[:, 0], 0)
    total = jnp.sum(stats[:, 1] * jnp.exp(stats[:, 0] - best), 0)
    cross = jnp.sum(best + jnp.log(total) - jnp.sum(stats[:, 2], 0))
    scale = jnp.exp(top - best) / total
    dshares = (mixed * scale[:, None] - target_rows.astype(jnp.float32)) / total_picks
    dshares = dshares.astype(low).reshape(size, -1, model_width)
    cross = jnp.broadcast_to(cross, (1, 128))
    dshares, idle_marks, cross = lax.optimization_barrier((dshares, rest_marks, cross))
    bit = lax.axis_size("dp") // 2
    while bit:
        cross = cross + swap(cross, "dp", bit)
        bit //= 2
    dfinal = jnp.sum(trade(dshares).astype(jnp.float32), 0)
    idle, rest_sparse = idle_gradient(
        core, all_rest, size * own_count, w_enc, bias, rest_mask, idle_marks
    )
    dfinal, idle, pick_sparse, cross = lax.optimization_barrier((dfinal, idle, pick_sparse, cross))

    dhidden = final_norm_back(dfinal)[0]
    dact = times_trans(dhidden.astype(low), proj_w)
    dup_low = gelu_back(dact)[0].astype(low)
    dnormed = times_trans(dup_low, fc_w)
    drecon = (dhidden + second_norm_back(dnormed)[0]).astype(low)

    errors = join(gather_near(drecon))
    far_errors = across(errors)
    middle = len(all_pick) // 2
    near = gradients(
        core, all_pick[:middle], spread(errors), all_feat, 0, w_dec, pick_marks, idle
    )
    near, far_errors = lax.optimization_barrier((near, far_errors))
    own, squares = gradients(
        core, all_pick[middle:], spread(far_errors), all_feat, 1, w_dec, pick_marks, near
    )
    terms = jnp.stack([cross, sparse_coef])
    small = jnp.stack([squares, pick_sparse + rest_sparse, weight_squares[0], weight_squares[1]])
    small, own, terms = lax.optimization_barrier((small + swap(small, "dp", 1), own, terms))
    other = swap(own, "dp", 1)
    small = pieces_of(small)
    clip_norm = norm_of(small)
    *directions, firsts, seconds, squares = moments(
        size,
        core,
        clip_norm,
        own,
        other,
        w_enc,
        enc_first,
        enc_second,
        w_dec,
        dec_first,
        dec_second,
    )
    weights, rows = renew(
        trade(squares), small, terms, clip_norm, directions, w_enc, w_dec, total_picks
    )
    return weights, firsts, seconds, rows[4, 0], rows[5, 0], rows[:2, 0], rows[2:4, 0]


def solution(mesh):
    in_specs = (
        P(("dp", "fsdp"), None, None),
        P("dp", None),
        P("dp", None),
        P("dp", None),
        P(),
        P(),
        P(),
        P(),
        P(),
        P(),
        P(),
        P("fsdp", None),
        P("fsdp", None),
        P("fsdp", None),
        P("fsdp", None),
        P("fsdp"),
        P("fsdp", None),
        P("fsdp", None),
        P("fsdp", None),
        P(),
    )
    out_specs = (
        P(None, "fsdp", None),
        P(None, "fsdp", None),
        P(None, "fsdp", None),
        P(),
        P(),
        P(),
        P(),
    )
    return jax.shard_map(shards, mesh=mesh, in_specs=in_specs, out_specs=out_specs, check_vma=False)
```
